32 devices in a mesh: dp: 8 (over z, y), mp: 4 (over x, core).
Axes of the slice: x: 2, y: 2, z: 4, core: 2. Of those that a mesh axis runs over, the one named last changes fastest.
Arguments:
- inputs: float32 [7168, 2304], P(('dp', 'mp')), may hold values from -16 to 16
- out_grad: float32 [7168, 2304], P(('dp', 'mp')), may hold values from -6 to 6
- segment_ids: int32 [8, 896], P('dp'), may hold values from 0 to 13, never falling along the last dimension, each value on 1 to 448 neighbouring positions
- pad_mask: int32 [8, 896], P('dp'), may hold values 0 or 1
- bit_sel: int32 [3], replicated, may hold values from 0 to 2
- w_qo: float32 [2, 2304, 2048], P(None, 'dp', 'mp'), may hold values from -1 to 1
- w_kv: float32 [2, 2304, 1024], P(None, 'dp', 'mp'), may hold values from -1 to 1
- w_mlp: float32 [3, 2304, 9216], P(None, 'dp', 'mp'), may hold values from -1 to 1
- norm_gains: float32 [9216], P(('dp', 'mp')), may hold values from -0.32 to 0.32
- m_qo: float32 [2, 2304, 2048], P(None, 'dp', 'mp'), may hold values from -0.3125 to 0.3125
- m_kv: float32 [2, 2304, 1024], P(None, 'dp', 'mp'), may hold values from -0.3125 to 0.3125
- m_mlp: float32 [3, 2304, 9216], P(None, 'dp', 'mp'), may hold values from -0.3125 to 0.3125
- m_gains: float32 [9216], P(('dp', 'mp')), may hold values from -0.3125 to 0.3125
- v_qo: float32 [2, 2304, 2048], P(None, 'dp', 'mp'), may hold values from 0.0066 to 0.105
- v_kv: float32 [2, 2304, 1024], P(None, 'dp', 'mp'), may hold values from 0.0066 to 0.105
- v_mlp: float32 [3, 2304, 9216], P(None, 'dp', 'mp'), may hold values from 0.0066 to 0.105
- v_gains: float32 [9216], P(('dp', 'mp')), may hold values from 0.0066 to 0.105
Outputs:
- outputs: float32 [7168, 2304], P(('dp', 'mp'))
- grad_in: float32 [7168, 2304], P(('dp', 'mp'))
- grad_norm: float32 [1], replicated
- new_w_qo: float32 [2, 2304, 2048], P(None, 'dp', 'mp')
- new_w_kv: float32 [2, 2304, 1024], P(None, 'dp', 'mp')
- new_w_mlp: float32 [3, 2304, 9216], P(None, 'dp', 'mp')
- new_gains: float32 [9216], P(('dp', 'mp'))
- new_m_qo: float32 [2, 2304, 2048], P(None, 'dp', 'mp')
- new_m_kv: float32 [2, 2304, 1024], P(None, 'dp', 'mp')
- new_m_mlp: float32 [3, 2304, 9216], P(None, 'dp', 'mp')
- new_m_gains: float32 [9216], P(('dp', 'mp'))
- new_v_qo: float32 [2, 2304, 2048], P(None, 'dp', 'mp')
- new_v_kv: float32 [2, 2304, 1024], P(None, 'dp', 'mp')
- new_v_mlp: float32 [3, 2304, 9216], P(None, 'dp', 'mp')
- new_v_gains: float32 [9216], P(('dp', 'mp'))
The draws below stay inside these ranges and needn't reach their ends.
Inputs may be any that keep to these rules, and one draw needn't show every extreme that they name: `segment_ids`: ids never fall along a sequence; a document holds 1 to 448 slots, one exactly that many in each sequence.
All inputs are finite; a program needn't handle non-finite values. No bound on the sum of `pad_mask` on one device may be relied on, other than what follows from the above.
Results may differ from the reference program's by a relative error of at most 0.02.
Values may be sent and summed in bfloat16 or wider, within the bound.
A program may use at most 320 MiB of HBM per device.

```python
import math
import jax
import jax.numpy as jnp
import numpy as np
from jax import lax

D = 2304
QUERY_HEADS = 8
KEY_VALUE_HEADS = 4
HEAD_WIDTH = 256
FF = 9216
NORMS = 4
TOKEN_SLOTS = 896
SEQS = 8
TOKENS = 7168
QW = 2048
KVW = 1024
PARAMS = 77865984


def coded_master(key, shape, fan_list):
    code_key, frac_key = jax.random.split(key)
    raw_codes = 32.0 * jax.random.normal(code_key, shape, jnp.float32)
    codes = jnp.clip(jnp.floor(raw_codes + 0.5), -127.0, 127.0)
    fraction = jax.random.uniform(frac_key, shape, jnp.float32, -0.35, 0.35)
    spacing = jnp.array([1.0 / (32.0 * math.sqrt(fan_in)) for fan_in in fan_list], jnp.float32).reshape(-1, 1, 1)
    return spacing * (codes + fraction)


def draw_inputs(key, part):
    position = jnp.arange(D, dtype=jnp.float32) / (D - 1.0)
    column_scale = jnp.exp(math.log(4.0) * position)
    base = jnp.clip(jax.random.normal(key, (TOKENS, D), jnp.float32), -4.0, 4.0)
    return base * column_scale[None, :]


def draw_w_qo(key, part):
    return coded_master(key, (2, D, QW), (D, QW))


def draw_w_kv(key, part):
    return coded_master(key, (2, D, KVW), (D, D))


def draw_w_mlp(key, part):
    return coded_master(key, (3, D, FF), (D, D, FF))


def with_ends(values, key, low, high):
    longest = values.shape.index(max(values.shape))
    spots = []
    for shift in (0, 1):
        where = [jax.random.randint(jax.random.fold_in(key, axis), (), 0, length) for axis, length in enumerate(values.shape)]
        where[longest] = (where[longest] + shift) % values.shape[longest]
        spots.append(tuple(where))
    return values.at[spots[0]].set(low).at[spots[1]].set(high)


def shard_levels(key, extent, cuts, low, top_value):
    def one(axis_at, blocks):
        heights = jax.random.uniform(jax.random.fold_in(jax.random.fold_in(key, 6), axis_at), (blocks,), jnp.float32, low / len(cuts), top_value / len(cuts))
        return jnp.repeat(jnp.exp(heights), extent[axis_at] // blocks).reshape((-1,) + (1,) * (len(extent) - axis_at - 1))

    level = one(*cuts[0])
    for cut in cuts[1:]:
        level = level * one(*cut)
    return level


def split_up(count, total, reach, slope):
    loads = [(1 << 20) // math.isqrt(standing ** slope) + 1 for standing in range(2, count + 1)]
    surplus, counts = total - reach - (count - 1), [1] * (count - 1)
    while surplus > 0:
        movable = [i for i in range(count - 1) if counts[i] < reach]
        whole, left = sum([loads[i] for i in movable]), surplus
        for i in movable:
            extra = min(reach - counts[i], max(1, left * loads[i] // whole), surplus)
            counts[i] = counts[i] + extra
            surplus = surplus - extra
    return np.array([reach] + counts)


def uneven_parts(stream_key, amount, total, reach, skew):
    if amount == 2:
        one = jax.random.randint(stream_key, (), max(1, total - reach), min(reach, total - 1) + 1)
        return jnp.stack([one, total - one])
    tallies = jnp.asarray(split_up(amount, total, reach, skew), jnp.int32)
    couples = (amount - 1) // 2
    donor, receiver = tallies[1:1 + 2 * couples:2], tallies[2:2 + 2 * couples:2]
    slack = jnp.minimum(donor - 1, reach - receiver)
    passed = jax.random.randint(jax.random.fold_in(stream_key, 1), (couples,), 0, 1 << 20) % (slack + 1)
    tallies = tallies.at[1:1 + 2 * couples:2].set(donor - passed).at[2:2 + 2 * couples:2].set(receiver + passed)
    return tallies[jax.random.permutation(jax.random.fold_in(stream_key, 2), amount)]


def gaussian(stream_key, extent, scale, most, shards=(), held_as=jnp.bfloat16):
    drawn = jax.random.normal(stream_key, extent, jnp.float32) * scale
    if len(shards) > 0:
        drawn = shard_levels(stream_key, extent, shards, -0.22, 0.18) * drawn
    return jnp.clip(drawn, min=-most, max=most).astype(held_as)


def setup_inputs(seed: int = 0) -> dict:
    key_list = jax.random.split(jax.random.key(seed), 18)
    return {
        "inputs": draw_inputs(jax.random.fold_in(key_list[17], 71), 0),
        "out_grad": gaussian(key_list[1], (TOKENS, D), 1.0, 6.0, ((0, 32),), jnp.float32),
        "segment_ids": jax.vmap(lambda own: jnp.searchsorted(jnp.cumsum(uneven_parts(own, max(3, TOKEN_SLOTS // 64), TOKEN_SLOTS, TOKEN_SLOTS // 2, 2)), jnp.arange(TOKEN_SLOTS), side="right"))(jax.random.split(key_list[2], SEQS)).reshape((SEQS, TOKEN_SLOTS)).astype(jnp.int32),
        "pad_mask": with_ends((jax.random.randint(key_list[3], (SEQS, TOKEN_SLOTS), 0, 8) < 7).astype(jnp.int32), jax.random.fold_in(key_list[3], 1), 0, 1),
        "bit_sel": jax.random.randint(key_list[4], (3,), 0, 3).astype(jnp.int32),
        "w_qo": draw_w_qo(jax.random.fold_in(key_list[17], 71), 0),
        "w_kv": draw_w_kv(jax.random.fold_in(key_list[17], 71), 0),
        "w_mlp": draw_w_mlp(jax.random.fold_in(key_list[17], 71), 0),
        "norm_gains": gaussian(key_list[8], (NORMS * D,), 0.08, 0.32, ((0, 32),), jnp.float32),
        "m_qo": gaussian(key_list[9], (2, D, QW), 0.055, 0.3125, ((1, 8), (2, 4)), jnp.float32),
        "m_kv": gaussian(key_list[10], (2, D, KVW), 0.055, 0.3125, ((1, 8), (2, 4)), jnp.float32),
        "m_mlp": gaussian(key_list[11], (3, D, FF), 0.055, 0.3125, ((1, 8), (2, 4)), jnp.float32),
        "m_gains": gaussian(key_list[12], (NORMS * D,), 0.055, 0.3125, ((0, 32),), jnp.float32),
        "v_qo": jnp.clip(jnp.exp(math.log(0.105) - 2.7668907 * jax.random.uniform(key_list[13], (2, D, QW), jnp.float32) ** shard_levels(key_list[13], (2, D, QW), ((1, 8), (2, 4)), -0.2, 0.2)), 0.0066, 0.105),
        "v_kv": jnp.clip(jnp.exp(math.log(0.105) - 2.7668907 * jax.random.uniform(key_list[14], (2, D, KVW), jnp.float32) ** shard_levels(key_list[14], (2, D, KVW), ((1, 8), (2, 4)), -0.2, 0.2)), 0.0066, 0.105),
        "v_mlp": jnp.clip(jnp.exp(math.log(0.105) - 2.7668907 * jax.random.uniform(key_list[15], (3, D, FF), jnp.float32) ** shard_levels(key_list[15], (3, D, FF), ((1, 8), (2, 4)), -0.2, 0.2)), 0.0066, 0.105),
        "v_gains": jnp.clip(jnp.exp(math.log(0.105) - 2.7668907 * jax.random.uniform(key_list[16], (NORMS * D,), jnp.float32) ** shard_levels(key_list[16], (NORMS * D,), ((0, 32),), -0.2, 0.2)), 0.0066, 0.105),
    }


EPSILON = 1e-06
SOFT_CAP = 50.0
ROPE_BASE = 10000.0
MASKED_SCORE = -1e+30
FIRST_DECAY = 0.9
SECOND_DECAY = 0.95
LEARN_RATE = 0.04
WEIGHT_DECAY = 0.1
ADAM_EPSILON = 1e-08
CLIP_SCALE = 0.5
HIGHEST = lax.Precision.HIGHEST

@jax.custom_vjp
def lower_part(v):
    return lax.optimization_barrier(v.astype(jnp.bfloat16)).astype(jnp.float32)

@jax.custom_vjp
def lower_part_backward(v):
    return v

def low_keep(v):
    return (lower_part(v), None)

def low_pass(kept, grad):
    return (grad,)

def back_keep(v):
    return (v, None)

def back_low(kept, grad):
    return (lower_part(grad),)
lower_part.defvjp(low_keep, low_pass)
lower_part_backward.defvjp(back_keep, back_low)

def matrix_product(left, right):
    return jnp.dot(left, right, precision=HIGHEST, preferred_element_type=jnp.float32)

def quantize(master, fan_list, selector):
    shifts = jnp.where(selector == 0, 0, jnp.where(selector == 1, 4, 6)).astype(jnp.int32)
    spacing = jnp.left_shift(jnp.int32(1), shifts)
    step_sizes = jnp.array([1.0 / (32.0 * math.sqrt(fan_in)) for fan_in in fan_list], jnp.float32).reshape(-1, 1, 1)
    codes = jnp.clip(jnp.floor(master / step_sizes + 0.5), -128.0, 127.0).astype(jnp.int32)
    sliced = jnp.floor_divide(codes + spacing // 2, spacing)
    sliced = jnp.clip(sliced, -(128 // spacing), 128 // spacing - 1)
    return (sliced * spacing).astype(jnp.float32) * step_sizes

def rms_norm(values, norm_gain):
    return values * lax.rsqrt(lax.optimization_barrier(jnp.mean(values * values, axis=-1, keepdims=True)) + EPSILON) * (1.0 + norm_gain)

def doc_positions(segments):
    slot_index = jnp.arange(segments.shape[0], dtype=jnp.int32)
    previous = jnp.concatenate([segments[:1] - 1, segments[:-1]])
    starts = segments != previous
    doc_begin = lax.cummax(jnp.where(starts, slot_index, 0), axis=0)
    return slot_index - doc_begin

def allowed_pairs(segments, padding):
    slot_index = jnp.arange(segments.shape[0], dtype=jnp.int32)
    same_doc = segments[:, None] == segments[None, :]
    causal = slot_index[None, :] <= slot_index[:, None]
    live_key = (padding[None, :] == 1) | (slot_index[None, :] == slot_index[:, None])
    return same_doc & causal & live_key

def apply_rotation(values, token_positions):
    half_dim = HEAD_WIDTH // 2
    frequency = ROPE_BASE ** (-jnp.arange(half_dim, dtype=jnp.float32) * 2.0 / HEAD_WIDTH)
    angles = token_positions.astype(jnp.float32)[:, None] * frequency[None, :]
    angles = jnp.concatenate([angles, angles], -1)
    cosine = jnp.cos(angles)[:, None, :]
    sine = jnp.sin(angles)[:, None, :]
    first_half = values[..., :half_dim]
    second = values[..., half_dim:]
    turned = jnp.concatenate([-second, first_half], -1)
    return values * cosine + turned * sine

def layer_forward(inputs, eff_qo, eff_kv, eff_mlp, norm_gains, segment_ids, pad_mask):
    weight_qo = lower_part(eff_qo)
    key_value_weight = lower_part(eff_kv)
    weight_mlp = lower_part(eff_mlp)
    gain_rows = norm_gains.reshape(NORMS, D)
    scale = HEAD_WIDTH ** (-0.5)

    def one_sequence(carry, packed):
        seq_rows, segments, padding = packed
        token_positions = doc_positions(segments)
        allowed = allowed_pairs(segments, padding)
        normalized_rows = lower_part(rms_norm(seq_rows, gain_rows[0]))
        query_linear = lower_part_backward(matrix_product(normalized_rows, weight_qo[0]))
        key_linear = lower_part_backward(matrix_product(normalized_rows, key_value_weight[0]))
        value_matrix = lower_part(lower_part_backward(matrix_product(normalized_rows, key_value_weight[1]))).reshape(TOKEN_SLOTS, KEY_VALUE_HEADS, HEAD_WIDTH)
        query_rows = lower_part(apply_rotation(query_linear.reshape(TOKEN_SLOTS, QUERY_HEADS, HEAD_WIDTH), token_positions)).reshape(TOKEN_SLOTS, KEY_VALUE_HEADS, QUERY_HEADS // KEY_VALUE_HEADS, HEAD_WIDTH)
        key_rows = lower_part(apply_rotation(key_linear.reshape(TOKEN_SLOTS, KEY_VALUE_HEADS, HEAD_WIDTH), token_positions))
        scores = lower_part_backward(jnp.einsum('qkgd,pkd->kgqp', query_rows, key_rows, precision=HIGHEST) * scale)
        capped = SOFT_CAP * jnp.tanh(scores / SOFT_CAP)
        capped = jnp.where(allowed[None, None], capped, MASKED_SCORE)
        probs = lower_part(jax.nn.softmax(capped, axis=-1))
        mixed = jnp.einsum('kgqp,pkd->qkgd', probs, value_matrix, precision=HIGHEST).reshape(TOKEN_SLOTS, QW)
        mixed = lower_part(lower_part_backward(mixed))
        attended = lower_part_backward(matrix_product(mixed, weight_qo[1].T))
        hidden_in = seq_rows + rms_norm(attended, gain_rows[1])
        ffn_in = lower_part(rms_norm(hidden_in, gain_rows[2]))
        gate = lower_part_backward(matrix_product(ffn_in, weight_mlp[0]))
        up_proj = lower_part_backward(matrix_product(ffn_in, weight_mlp[1]))
        activated = lower_part(jax.nn.gelu(gate, approximate=True) * up_proj)
        branch = lower_part_backward(matrix_product(activated, weight_mlp[2].T))
        return (carry, hidden_in + rms_norm(branch, gain_rows[3]))
    _, results = lax.scan(jax.checkpoint(one_sequence), jnp.zeros((), jnp.float32), (inputs.reshape(SEQS, TOKEN_SLOTS, D), segment_ids, pad_mask))
    return results.reshape(TOKENS, D)

def adam_update(master, first_moment, second_moment, gradient, factor):
    clipped = gradient * factor
    new_first = FIRST_DECAY * first_moment + (1.0 - FIRST_DECAY) * clipped
    new_second = SECOND_DECAY * second_moment + (1.0 - SECOND_DECAY) * clipped * clipped
    new_master = master - LEARN_RATE * (new_first / (jnp.sqrt(new_second) + ADAM_EPSILON) + WEIGHT_DECAY * master)
    return (new_master, new_first, new_second)

def reference(inputs, out_grad, segment_ids, pad_mask, bit_sel, w_qo, w_kv, w_mlp, norm_gains, m_qo, m_kv, m_mlp, m_gains, v_qo, v_kv, v_mlp, v_gains):
    eff_qo = quantize(w_qo, (D, QW), bit_sel[0])
    eff_kv = quantize(w_kv, (D, D), bit_sel[1])
    eff_mlp = quantize(w_mlp, (D, D, FF), bit_sel[2])

    def forward(layer_in, arg_qo, arg_kv, arg_mlp, arg_gains):
        return layer_forward(layer_in, arg_qo, arg_kv, arg_mlp, arg_gains, segment_ids, pad_mask)
    outputs, pullback = jax.vjp(forward, inputs, eff_qo, eff_kv, eff_mlp, norm_gains)
    cotangent = out_grad * pad_mask.reshape(TOKENS, 1).astype(jnp.float32)
    grad_in, grad_qo, grad_kv, grad_mlp, grad_gains = pullback(cotangent)
    squares_total = jnp.sum(grad_qo * grad_qo) + jnp.sum(grad_kv * grad_kv) + jnp.sum(grad_mlp * grad_mlp) + jnp.sum(grad_gains * grad_gains)
    grad_norm = jnp.sqrt(squares_total)
    factor = jnp.minimum(1.0, CLIP_SCALE * math.sqrt(PARAMS) / grad_norm)
    new_w_qo, new_m_qo, new_v_qo = adam_update(w_qo, m_qo, v_qo, grad_qo, factor)
    new_w_kv, new_m_kv, new_v_kv = adam_update(w_kv, m_kv, v_kv, grad_kv, factor)
    new_w_mlp, new_m_mlp, new_v_mlp = adam_update(w_mlp, m_mlp, v_mlp, grad_mlp, factor)
    new_gains, new_m_gains, new_v_gains = adam_update(norm_gains, m_gains, v_gains, grad_gains, factor)
    return (outputs, grad_in, grad_norm.reshape(1), new_w_qo, new_w_kv, new_w_mlp, new_gains, new_m_qo, new_m_kv, new_m_mlp, new_m_gains, new_v_qo, new_v_kv, new_v_mlp, new_v_gains)
```

```python
import functools
import math

import jax
import jax.numpy as jnp
from jax import lax
from jax.experimental import pallas as pl
from jax.experimental.pallas import tpu as pltpu
from jax.sharding import PartitionSpec as P

D = 2304
HEAD_WIDTH = 256
FF = 9216
NORMS = 4
QW = 2048
PARAMS = 77865984

EPSILON = 1e-06
SOFT_CAP = 50.0
ROPE_BASE = 10000.0
MASKED_SCORE = -1e30
FIRST_DECAY = 0.9
SECOND_DECAY = 0.95
LEARN_RATE = 0.04
WEIGHT_DECAY = 0.1
ADAM_EPSILON = 1e-08
CLIP_SCALE = 0.5

BF = jnp.bfloat16
F32 = jnp.float32


def quantize(master, fan_in, selector):
    return quantize_by(master, jnp.float32(1.0 / (32.0 * math.sqrt(fan_in))), selector)


def quantize_by(master, step, selector):
    spacing = jnp.where(selector == 0, 1.0, jnp.where(selector == 1, 16.0, 64.0)).astype(F32)
    half = jnp.floor(spacing * 0.5)
    inverse = 1.0 / spacing
    codes = jnp.clip(jnp.floor(master / step + 0.5), -128.0, 127.0)
    top = 128.0 * inverse
    sliced = jnp.clip(jnp.floor((codes + half) * inverse), -top, top - 1.0)
    return ((sliced * spacing) * step).astype(BF)


def inv_root(values):
    return lax.rsqrt(jnp.mean(values * values, axis=-1, keepdims=True) + EPSILON)


def rms_norm(values, norm_gain):
    return values * inv_root(values) * (1.0 + norm_gain)


def rms_back(values, norm_gain, grad):
    root = inv_root(values)
    scaled = grad * (1.0 + norm_gain)
    dot = jnp.mean(values * scaled, axis=-1, keepdims=True)
    grad_values = root * scaled - values * (root * root * root * dot)
    grad_gain = jnp.sum(values * root * grad, axis=0)
    return grad_values, grad_gain


def doc_positions(segments):
    slot_index = jnp.arange(segments.shape[0], dtype=jnp.int32)
    previous = jnp.concatenate([segments[:1] - 1, segments[:-1]])
    starts = segments != previous
    doc_begin = lax.cummax(jnp.where(starts, slot_index, 0), axis=0)
    return slot_index - doc_begin


def rotate(values, cosine, sine):
    half_dim = HEAD_WIDTH // 2
    turned = jnp.concatenate([-values[..., half_dim:], values[..., :half_dim]], -1)
    return values * cosine + turned * sine


def rotate_back(grads, cosine, sine):
    half_dim = HEAD_WIDTH // 2
    scaled = grads * sine
    turned = jnp.concatenate([scaled[..., half_dim:], -scaled[..., :half_dim]], -1)
    return grads * cosine + turned


def mm(left, right):
    return lax.dot_general(left, right, (((1,), (0,)), ((), ())), preferred_element_type=F32)


def mm_rows(left, right):
    return lax.dot_general(left, right, (((0,), (0,)), ((), ())), preferred_element_type=F32)


def mm_cols(left, right):
    return lax.dot_general(left, right, (((1,), (1,)), ((), ())), preferred_element_type=F32)


def adam_update(master, first_moment, second_moment, gradient, factor):
    clipped = gradient * factor
    new_first = FIRST_DECAY * first_moment + (1.0 - FIRST_DECAY) * clipped
    new_second = SECOND_DECAY * second_moment + (1.0 - SECOND_DECAY) * clipped * clipped
    new_master = master - LEARN_RATE * (
        new_first / (jnp.sqrt(new_second) + ADAM_EPSILON) + WEIGHT_DECAY * master
    )
    return (new_master, new_first, new_second)


MESH = pl.DeviceIdType.MESH
ANY = pl.BlockSpec(memory_space=pl.ANY)
VMEM = pl.BlockSpec(memory_space=pltpu.VMEM)
ROWS = 32


class Net:
    def __init__(self, n_dp, n_mp, send_sems, recv_sems, local_sems=None):
        self.n_dp, self.n_mp = n_dp, n_mp
        self.send_sems, self.recv_sems, self.local_sems = send_sems, recv_sems, local_sems
        self.used, self.used_local, self.open = 0, 0, []
        self.i, self.m = lax.axis_index("dp"), lax.axis_index("mp")
        self.y, self.j = self.i % 2, self.i // 2
        self.zl = self.j % 2
        self.c, self.x = self.m % 2, self.m // 2
        self.core_n = (self.i, self.m + 1 - 2 * self.c)
        self.x_n = (self.i, (self.m + 2) % 4)
        self.y_n = (self.i + 1 - 2 * self.y, self.m)
        self.z_n = (self.i + 2 - 4 * self.zl, self.m)

    def z_at(self, d):
        nj = self.n_dp // 2
        return (((self.j + d) % nj) * 2 + self.y, self.m)

    def place(self):
        return (1 - self.y) * self.j + self.y * (self.n_dp - 1 - self.j)

    def ring(self, at):
        n, nj = self.n_dp, self.n_dp // 2
        at = at % n
        late = at // nj
        return (1 - late) * 2 * at + late * (2 * (n - 1 - at) + 1)

    def meet(self, devices):
        barrier = pltpu.get_barrier_semaphore()
        for device in devices:
            pl.semaphore_signal(barrier, inc=1, device_id=device, device_id_type=MESH)
        pl.semaphore_wait(barrier, len(devices))

    def send(self, src, dst, device):
        at = self.used
        self.used += 1
        copy = pltpu.make_async_remote_copy(
            src_ref=src, dst_ref=dst, send_sem=self.send_sems.at[at], recv_sem=self.recv_sems.at[at],
            device_id=device, device_id_type=MESH,
        )
        copy.start()
        self.open.append(copy.wait_send)
        return copy

    def move(self, src, dst):
        at = self.used_local
        self.used_local += 1
        copy = pltpu.make_async_copy(src, dst, self.local_sems.at[at])
        copy.start()
        return copy

    def keep(self, src, dst):
        self.open.append(self.move(src, dst).wait)

    def close(self):
        for wait in self.open:
            wait()


def upper(count):
    return count // 16 * 8


def dma(n):
    return pltpu.SemaphoreType.DMA((n,))


def call(kernel, outs, out_specs, in_specs, scratch, cid, mb, flops=0):
    return pl.pallas_call(
        kernel,
        out_shape=outs,
        in_specs=in_specs,
        out_specs=out_specs,
        scratch_shapes=scratch,
        compiler_params=pltpu.CompilerParams(
            collective_id=cid, has_side_effects=True, vmem_limit_bytes=mb << 20
        ),
    )


def by_rows(total, body, carry=0):
    return lax.fori_loop(
        0, total // ROWS, lambda t, state: body(pl.ds(pl.multiple_of(t * ROWS, ROWS), ROWS), state), carry
    )


def everyone(n_dp, n_mp, i, m):
    flat = i * n_mp + m
    total = n_dp * n_mp
    return [(((flat + t) % total) // n_mp, (flat + t) % n_mp) for t in range(1, total)]


def spread_kernel(n_dp, n_mp, own, full, ss, rs, ls):
    net = Net(n_dp, n_mp, ss, rs, ls)
    others = everyone(n_dp, n_mp, net.i, net.m)
    net.meet(others)
    flat = net.i * n_mp + net.m
    copies = [net.send(own, full.at[flat], device) for device in others]
    net.keep(own, full.at[flat])
    for copy in copies:
        copy.wait_recv()
    net.close()


def spread(n_dp, n_mp, own):
    total = n_dp * n_mp
    return call(
        functools.partial(spread_kernel, n_dp, n_mp),
        jax.ShapeDtypeStruct((total,) + own.shape, own.dtype), VMEM, [VMEM],
        [dma(total), dma(total), dma(1)], 1, 16,
    )(own)


def gather_seq_steps(net, own, seq):
    far = net.send(own, seq.at[1], net.x_n)
    near = net.send(own, seq.at[2], net.core_n)
    net.keep(own, seq.at[0])

    def finish():
        far.wait_recv()
        both = net.send(seq.at[1], seq.at[3], net.core_n)
        near.wait_recv()
        both.wait_recv()

    return finish


def head_kernel(n_dp, n_mp, q, kv, o, tok, wq, wkv, wo, seq, ss, rs, ls):
    net = Net(n_dp, n_mp, ss, rs, ls)
    p = net.place()
    right = (net.ring(p + 1), net.m)
    left = (net.ring(p + n_dp - 1), net.m)
    net.meet([right, left, net.x_n, net.core_n])
    wrows = o.shape[0]
    hr = upper(wrows)
    top, low = pl.ds(0, hr), pl.ds(hr, wrows - hr)
    a = net.send(q, wq.at[net.i], right)
    b = net.send(kv, wkv.at[net.i], left)
    finish = gather_seq_steps(net, tok, seq)
    net.keep(q, wq.at[net.i])
    net.keep(kv, wkv.at[net.i])
    net.keep(o, wo.at[net.i])
    for hop in range(1, n_dp):
        from_right, from_left = net.ring(p + n_dp - hop), net.ring(p + hop)
        a.wait_recv()
        if hop < n_dp - 1:
            a = net.send(wq.at[from_right], wq.at[from_right], right)
        else:
            oa = net.send(o.at[top], wo.at[net.i, top], right)
        b.wait_recv()
        if hop < n_dp - 1:
            b = net.send(wkv.at[from_left], wkv.at[from_left], left)
        else:
            ob = net.send(o.at[low], wo.at[net.i, low], left)
        if hop == n_dp // 2:
            finish()
    for hop in range(1, n_dp):
        from_right, from_left = net.ring(p + n_dp - hop), net.ring(p + hop)
        oa.wait_recv()
        if hop < n_dp - 1:
            oa = net.send(wo.at[from_right, top], wo.at[from_right, top], right)
        ob.wait_recv()
        if hop < n_dp - 1:
            ob = net.send(wo.at[from_left, low], wo.at[from_left, low], left)
    net.close()


def head(n_dp, n_mp, q, kv, o, tok):
    full = lambda a: jax.ShapeDtypeStruct((n_dp,) + a.shape, BF)
    count = 4 * n_dp + 8
    return call(
        functools.partial(head_kernel, n_dp, n_mp),
        [full(q), full(kv), full(o), jax.ShapeDtypeStruct((4,) + tok.shape, BF)],
        [ANY] * 4, [ANY] * 4, [dma(count), dma(count), dma(8)], 2, 16,
    )(q, kv, o, tok)


def gather_pair_steps(net, own, group):
    far = net.send(own, group.at[2], net.x_n)
    zed = net.send(own, group.at[1], net.z_n)
    near = net.send(own, group.at[4], net.core_n)
    net.keep(own, group.at[0])

    def finish():
        zed.wait_recv()
        both = net.send(group.at[1], group.at[3], net.x_n)
        near_z = net.send(group.at[1], group.at[5], net.core_n)
        far.wait_recv()
        near_x = net.send(group.at[2], group.at[6], net.core_n)
        both.wait_recv()
        near_both = net.send(group.at[3], group.at[7], net.core_n)
        for copy in (near, near_z, near_x, near_both):
            copy.wait_recv()

    return finish


def weights_start(net, low, full, ks):
    nj = net.n_dp // 2
    width = full.shape[-1]
    half = lambda which: pl.ds(pl.multiple_of(which * width, width), width)
    flight = {}
    for k in ks:
        own = low.at[k, :, half(net.zl)]
        net.keep(own, full.at[k, net.i])
        flight[k, 0] = net.send(own, full.at[k, net.i], net.y_n)
        for d in sorted(range(1, nj), key=lambda d: -abs(d - nj // 2) * 0 - (d == nj // 2)):
            flight[k, d] = net.send(
                low.at[k, :, half(((net.j + d) % nj) % 2)], full.at[k, net.i], net.z_at(d)
            )
    return flight


def weights_relay(net, full, flight, k):
    nj = net.n_dp // 2
    relays = [flight[k, 0]]
    for d in range(1, nj):
        flight[k, d].wait_recv()
        at = ((net.j + nj - d) % nj) * 2 + net.y
        relays.append(net.send(full.at[k, at], full.at[k, at], net.y_n))
    return relays


def pair_partners(net, with_y):
    nj = net.n_dp // 2
    zs = [net.z_at(d) for d in range(1, nj)] if with_y else [net.z_n]
    return [net.core_n, net.x_n] + zs + ([net.y_n] if with_y else [])


def mid_kernel(
    n_dp, n_mp, near, far, inputs, gains, low, att, hid, group, full,
    r1, s2, r2, own, ss, rs, ls,
):
    net = Net(n_dp, n_mp, ss, rs, ls)
    net.meet(pair_partners(net, True))
    rows = inputs.shape[0]
    c1 = net.send(far.at[1], r1.at[1], net.core_n)
    c0 = net.send(far.at[0], r1.at[0], net.core_n)
    flight = weights_start(net, low, full, (0, 1))
    c1.wait_recv()

    def first(at, state):
        s2[at] = (near[1, at] + r1[1, at].astype(F32)).astype(BF)
        return state

    by_rows(rows, first)
    x = net.send(s2, r2, net.x_n)
    c0.wait_recv()
    x.wait_recv()
    g1, g2 = 1.0 + gains[1:2], 1.0 + gains[2:3]

    def second(at, state):
        total = near[0, at] + r1[0, at].astype(F32) + r2[at].astype(F32)
        att[at] = total
        hidden = inputs[at] + total * inv_root(total) * g1
        hid[at] = hidden
        own[at] = (hidden * inv_root(hidden) * g2).astype(BF)
        return state

    by_rows(rows, second)
    finish = gather_pair_steps(net, own, group)
    relays = weights_relay(net, full, flight, 0)
    finish()
    flight2 = weights_start(net, low, full, (2,))
    relays += weights_relay(net, full, flight, 1)
    relays += weights_relay(net, full, flight2, 2)
    for copy in relays:
        copy.wait_recv()
    net.close()


def mid(n_dp, n_mp, near, far, inputs, gains, low):
    rows = inputs.shape[0]
    nj = n_dp // 2
    count = 16 + 6 * nj
    block = (rows, D)
    width = low.shape[2] // 2
    return call(
        functools.partial(mid_kernel, n_dp, n_mp),
        [
            jax.ShapeDtypeStruct(block, F32), jax.ShapeDtypeStruct(block, F32),
            jax.ShapeDtypeStruct((8,) + block, BF),
            jax.ShapeDtypeStruct((3, n_dp, low.shape[1], width), BF),
        ],
        [VMEM, VMEM, ANY, ANY], [VMEM, ANY, VMEM, VMEM, ANY],
        [
            pltpu.VMEM((2,) + block, BF), pltpu.VMEM(block, BF), pltpu.VMEM(block, BF),
            pltpu.VMEM(block, BF), dma(count), dma(count), dma(8),
        ],
        3, 48,
    )(near, far, inputs, gains, low)


def reduce_pair_steps(net, near, far, r1, s2, r2, s3, r3, rows):
    cores = {k: net.send(far.at[k], r1.at[k], net.core_n) for k in (3, 2, 1, 0)}
    xs = {}
    for k in (3, 2):
        cores[k].wait_recv()

        def add(at, state, k=k):
            s2[k - 2, at] = (near[k, at] + r1[k, at].astype(F32)).astype(BF)
            return state

        by_rows(rows, add)
        xs[k] = net.send(s2.at[k - 2], r2.at[k - 2], net.x_n)
    cores[1].wait_recv()
    cores[0].wait_recv()
    xs[3].wait_recv()

    def zed(at, state):
        s3[at] = (near[1, at] + r1[1, at].astype(F32) + r2[1, at].astype(F32)).astype(BF)
        return state

    by_rows(rows, zed)
    z = net.send(s3, r3, net.z_n)
    xs[2].wait_recv()
    return z


def pair_scratch(rows):
    block = (rows, D)
    return [
        pltpu.VMEM((4,) + block, BF), pltpu.VMEM((2,) + block, BF), pltpu.VMEM((2,) + block, BF),
        pltpu.VMEM(block, BF), pltpu.VMEM(block, BF), pltpu.VMEM(block, BF),
    ]


def rms_back_rows(values, gain, grad):
    root = inv_root(values)
    scaled = grad * gain
    dot = jnp.mean(values * scaled, axis=-1, keepdims=True)
    return root * scaled - values * (root * root * root * dot), jnp.sum(values * root * grad, axis=0, keepdims=True)


def turn_kernel(
    n_dp, n_mp, near, far, hid, gains, out_grad, live, outputs, dgain, group,
    r1, s2, r2, s3, r3, own, ss, rs, ls,
):
    net = Net(n_dp, n_mp, ss, rs, ls)
    net.meet(pair_partners(net, False))
    rows = hid.shape[0]
    z = reduce_pair_steps(net, near, far, r1, s2, r2, s3, r3, rows)
    z.wait_recv()
    g3 = 1.0 + gains[3:4]

    def last(at, state):
        total = near[0, at] + r1[0, at].astype(F32) + r2[0, at].astype(F32) + r3[at].astype(F32)
        outputs[at] = hid[at] + total * inv_root(total) * g3
        grad, dg = rms_back_rows(total, g3, out_grad[at] * live[at])
        own[at] = grad.astype(BF)
        return state + dg

    dgain[...] = by_rows(rows, last, jnp.zeros((1, D), F32))
    gather_pair_steps(net, own, group)()
    net.close()


def turn(n_dp, n_mp, near, far, hid, gains, out_grad, live):
    rows = hid.shape[0]
    block = (rows, D)
    return call(
        functools.partial(turn_kernel, n_dp, n_mp),
        [jax.ShapeDtypeStruct(block, F32), jax.ShapeDtypeStruct((1, D), F32), jax.ShapeDtypeStruct((8,) + block, BF)],
        [VMEM, VMEM, ANY], [VMEM, ANY, VMEM, VMEM, VMEM, VMEM],
        pair_scratch(rows) + [dma(24), dma(24), dma(2)], 4, 56,
    )(near, far, hid, gains, out_grad, live)


def back_kernel(
    n_dp, n_mp, near, far, hid, att, gains, out_grad, live, grads,
    ghid, dg1, dg2, seq, sums, squares,
    r1, s2, r2, s3, r3, own, yr, zs, zr, total, ss, rs, ls,
):
    net = Net(n_dp, n_mp, ss, rs, ls)
    nj = n_dp // 2
    net.meet(pair_partners(net, True))
    rows = hid.shape[0]
    wrows, width = yr.shape[2], yr.shape[3]
    ks = (2, 0, 1)
    turns = list(range(1, nj)) + [0]
    moves, ys = {}, {}

    def y_start(k):
        for d in turns:
            at = (net.j + d) % nj
            ys[k, d] = net.send(grads.at[k, at, 1 - net.y], yr.at[k, d], net.y_n)
            moves[k, d] = net.move(grads.at[k, at, net.y], zs.at[k, d])

    z_flight = {}

    def z_step(k, d):
        ys[k, d].wait_recv()
        moves[k, d].wait()

        def add(at, state):
            zs[k, d, at] = (zs[k, d, at].astype(F32) + yr[k, d, at].astype(F32)).astype(BF)
            return state

        lax.fori_loop(
            0, wrows // 8,
            lambda t, state: add(pl.ds(pl.multiple_of(t * 8, 8), 8), state), 0,
        ) if wrows % 16 else lax.fori_loop(
            0, wrows // 16,
            lambda t, state: add(pl.ds(pl.multiple_of(t * 16, 16), 16), state), 0,
        )
        if d:
            z_flight[k, d] = net.send(zs.at[k, d], zr.at[k, d - 1], net.z_at(d))

    z = None
    cores = None
    y_start(2)
    z = reduce_pair_steps(net, near, far, r1, s2, r2, s3, r3, rows)
    y_start(0)
    y_start(1)
    z.wait_recv()
    g1, g2 = 1.0 + gains[1:2], 1.0 + gains[2:3]

    def last(at, state):
        grad = near[0, at] + r1[0, at].astype(F32) + r2[0, at].astype(F32) + r3[at].astype(F32)
        part, d2 = rms_back_rows(hid[at], g2, grad)
        grad_hidden = out_grad[at] * live[at] + part
        ghid[at] = grad_hidden
        grad_att, d1 = rms_back_rows(att[at], g1, grad_hidden)
        own[at] = grad_att.astype(BF)
        return state[0] + d1, state[1] + d2

    zero = jnp.zeros((1, D), F32)
    done1, done2 = by_rows(rows, last, (zero, zero))
    dg1[...] = done1
    dg2[...] = done2
    finish = gather_seq_steps(net, own, seq)
    for d in turns:
        z_step(2, d)
    finish()
    for k in (0, 1):
        for d in turns:
            z_step(k, d)

    square = jnp.zeros((8, width), F32)
    writes = []
    step = 16 if wrows % 16 == 0 else 8
    for turn_at, k in enumerate(ks):
        for d in range(1, nj):
            z_flight[k, d].wait_recv()
        slot = turn_at % 2
        if len(writes) >= 2:
            for w in writes[len(writes) - 2]:
                w.wait()

        def collect(t, state, k=k, slot=slot):
            at = pl.ds(pl.multiple_of(t * step, step), step)
            halves = [zs[k, 0, at].astype(F32), jnp.zeros((step, width), F32)]
            for d in range(1, nj):
                halves[d % 2] = halves[d % 2] + zr[k, d - 1, at].astype(F32)
            for parity in range(2):
                total[slot, parity, at] = halves[parity]
                sq = halves[parity] * halves[parity]
                for r in range(step // 8):
                    state = state + sq[r * 8 : r * 8 + 8]
            return state

        square = lax.fori_loop(0, wrows // step, collect, square)
        pair = []
        for parity in range(2):
            half = (net.zl + parity) % 2
            pair.append(
                net.move(total.at[slot, parity], sums.at[k, :, pl.ds(pl.multiple_of(half * width, width), width)])
            )
        writes.append(pair)
    for pair in writes[len(writes) - 2 :]:
        for w in pair:
            w.wait()
    squares[...] = square
    net.close()


def back(n_dp, n_mp, near, far, hid, att, gains, out_grad, live, grads):
    rows = hid.shape[0]
    block = (rows, D)
    nj = n_dp // 2
    _, _, _, wrows, width = grads.shape
    count = 24 + 6 * nj
    return call(
        functools.partial(back_kernel, n_dp, n_mp),
        [
            jax.ShapeDtypeStruct(block, F32), jax.ShapeDtypeStruct((1, D), F32), jax.ShapeDtypeStruct((1, D), F32),
            jax.ShapeDtypeStruct((4,) + block, BF), jax.ShapeDtypeStruct((3, wrows, 2 * width), F32),
            jax.ShapeDtypeStruct((8, width), F32),
        ],
        [VMEM, VMEM, VMEM, ANY, ANY, VMEM], [VMEM, ANY, VMEM, VMEM, VMEM, VMEM, VMEM, ANY],
        pair_scratch(rows)
        + [
            pltpu.VMEM((3, nj, wrows, width), BF), pltpu.VMEM((3, nj, wrows, width), BF),
            pltpu.VMEM((3, nj - 1, wrows, width), BF),
            pltpu.VMEM((2, 2, wrows, width), F32), dma(count), dma(count), dma(8 + 3 * nj),
        ],
        5, 60,
    )(near, far, hid, att, gains, out_grad, live, grads)


def tail_kernel(
    n_dp, n_mp, near, far, inputs, gains, ghid, gq, gkv, go, gin, dg0, sq_, skv, so,
    r1, s2, r2, tq, tkv, to, rq, rkv, roa, rob, bq, bkv, boa, bob, ss, rs, ls,
):
    net = Net(n_dp, n_mp, ss, rs, ls)
    p = net.place()
    right = (net.ring(p + 1), net.m)
    left = (net.ring(p + n_dp - 1), net.m)
    net.meet([right, left, net.x_n, net.core_n])
    rows = inputs.shape[0]
    wrows = go.shape[1]
    hr = upper(wrows)
    top, low = pl.ds(0, hr), pl.ds(hr, wrows - hr)

    def ready(offset):
        return net.ring(p + 2 * n_dp + offset)

    oa = net.send(go.at[ready(-1), top], roa.at[0], right)
    ob = net.send(go.at[ready(1), low], rob.at[0], left)
    a = net.send(gq.at[ready(-1)], rq.at[0], right)
    b = net.send(gkv.at[ready(1)], rkv.at[0], left)
    loads = [net.move(go, to), net.move(gq, tq), net.move(gkv, tkv)]
    c1 = net.send(far.at[1], r1.at[1], net.core_n)
    c0 = net.send(far.at[0], r1.at[0], net.core_n)
    c1.wait_recv()

    def first(at, state):
        s2[at] = (near[1, at] + r1[1, at].astype(F32)).astype(BF)
        return state

    by_rows(rows, first)
    x = net.send(s2, r2, net.x_n)
    for load in loads:
        load.wait()

    def hop_add(dst, got, term, count, dtype):
        step = 16 if count % 16 == 0 else (8 if count % 8 == 0 else count)

        def add(t, state):
            at = pl.ds(pl.multiple_of(t * step, step), step)
            dst[at] = (got[at].astype(F32) + term[at].astype(F32)).astype(dtype)
            return state

        lax.fori_loop(0, count // step, add, 0)

    def finish_rows():
        c0.wait_recv()
        x.wait_recv()
        g0 = 1.0 + gains[0:1]

        def second(at, state):
            grad = near[0, at] + r1[0, at].astype(F32) + r2[at].astype(F32)
            part, d0 = rms_back_rows(inputs[at], g0, grad)
            gin[at] = ghid[at] + part
            return state + d0

        dg0[...] = by_rows(rows, second, jnp.zeros((1, D), F32))

    for hop in range(1, n_dp):
        end = hop == n_dp - 1
        at_right, at_left = ready(-1 - hop), ready(1 + hop)
        oa.wait_recv()
        hop_add(so.at[top] if end else boa.at[hop - 1], roa.at[hop - 1], to.at[at_right, top], hr, F32 if end else BF)
        if not end:
            oa = net.send(boa.at[hop - 1], roa.at[hop], right)
        ob.wait_recv()
        hop_add(so.at[low] if end else bob.at[hop - 1], rob.at[hop - 1], to.at[at_left, low], wrows - hr, F32 if end else BF)
        if not end:
            ob = net.send(bob.at[hop - 1], rob.at[hop], left)
        a.wait_recv()
        hop_add(sq_ if end else bq.at[hop - 1], rq.at[hop - 1], tq.at[at_right], wrows, F32 if end else BF)
        if not end:
            a = net.send(bq.at[hop - 1], rq.at[hop], right)
        b.wait_recv()
        hop_add(skv if end else bkv.at[hop - 1], rkv.at[hop - 1], tkv.at[at_left], wrows, F32 if end else BF)
        if not end:
            b = net.send(bkv.at[hop - 1], rkv.at[hop], left)
        if hop == (n_dp * 5) // 8:
            finish_rows()
    net.close()


def tail(n_dp, n_mp, near, far, inputs, gains, ghid, gq, gkv, go):
    rows = inputs.shape[0]
    block = (rows, D)
    _, wrows, width = gq.shape
    full, half, rest = (wrows, width), (upper(wrows), width), (wrows - upper(wrows), width)
    hops = n_dp - 1
    count = 4 * n_dp + 8
    many = lambda n, shape: pltpu.VMEM((n,) + shape, BF)
    return call(
        functools.partial(tail_kernel, n_dp, n_mp),
        [
            jax.ShapeDtypeStruct(block, F32), jax.ShapeDtypeStruct((1, D), F32),
            jax.ShapeDtypeStruct(full, F32), jax.ShapeDtypeStruct(full, F32), jax.ShapeDtypeStruct(full, F32),
        ],
        [VMEM] * 5, [VMEM, ANY, VMEM, VMEM, VMEM, ANY, ANY, ANY],
        [
            many(2, block), pltpu.VMEM(block, BF), pltpu.VMEM(block, BF),
            many(n_dp, full), many(n_dp, full), many(n_dp, full),
            many(hops, full), many(hops, full), many(hops, half), many(hops, rest),
            many(hops, full), many(hops, full), many(hops, half), many(hops, rest),
            dma(count), dma(count), dma(8),
        ],
        6, 60,
    )(near, far, inputs, gains, ghid, gq, gkv, go)


def finish_kernel(n_dp, n_mp, terms, square, total_gain, total_square, got, sgot, mine, ss, rs, ls):
    net = Net(n_dp, n_mp, ss, rs, ls)
    others = everyone(n_dp, n_mp, net.i, net.m)
    net.meet(others)
    flat = net.i * n_mp + net.m
    copies = [
        net.send(terms.at[dp * n_mp + mp], got.at[flat], (dp, mp)) for dp, mp in others
    ]
    net.keep(terms.at[flat], got.at[flat])
    net.open.pop()()
    for copy in copies:
        copy.wait_recv()
    total = lax.fori_loop(0, n_dp * n_mp, lambda t, s: s + got[t], jnp.zeros(got.shape[1:], F32))
    total_gain[...] = total
    mine[...] = square[...] + jnp.sum(total * total) * (1.0 / (mine.shape[0] * mine.shape[1]))
    copies = [net.send(mine, sgot.at[flat], device) for device in others]
    net.keep(mine, sgot.at[flat])
    net.open.pop()()
    for copy in copies:
        copy.wait_recv()
    total_square[...] = lax.fori_loop(0, n_dp * n_mp, lambda t, s: s + sgot[t], jnp.zeros(mine.shape, F32))
    net.close()


def finish_all(n_dp, n_mp, terms, square):
    total = n_dp * n_mp
    shape = terms.shape[1:]
    return call(
        functools.partial(finish_kernel, n_dp, n_mp),
        [jax.ShapeDtypeStruct(shape, F32), jax.ShapeDtypeStruct(square.shape, F32)],
        [VMEM, VMEM], [VMEM, VMEM],
        [
            pltpu.VMEM((total,) + shape, F32), pltpu.VMEM((total,) + square.shape, F32),
            pltpu.VMEM(square.shape, F32), dma(2 * total), dma(2 * total), dma(2),
        ],
        7, 16,
    )(terms, square)


def build_local(n_dp, n_mp):
    nj = n_dp // 2

    def local(
        inputs, out_grad, segment_ids, pad_mask, bit_sel, w_qo, w_kv, w_mlp, norm_gains,
        m_qo, m_kv, m_mlp, m_gains, v_qo, v_kv, v_mlp, v_gains,
    ):
        m = lax.axis_index("mp")
        rows = inputs.shape[0]
        seq_len = segment_ids.shape[1]
        wrows = w_qo.shape[1]

        gain_rows = spread(n_dp, n_mp, norm_gains.reshape(1, -1)).reshape(NORMS, D)
        low_q = quantize(w_qo[0], D, bit_sel[0])
        low_o = quantize(w_qo[1], QW, bit_sel[0])
        low_kv = jnp.concatenate([quantize(w_kv[0], D, bit_sel[1]), quantize(w_kv[1], D, bit_sel[1])], 1)
        steps = jnp.array([1.0 / (32.0 * math.sqrt(fan)) for fan in (D, D, FF)], F32).reshape(3, 1, 1)
        low_mlp = quantize_by(w_mlp, steps, bit_sel[2])
        norm_in = rms_norm(inputs, gain_rows[0]).astype(BF)
        wq, wkv, wo, seq_normed = head(n_dp, n_mp, low_q, low_kv, low_o, norm_in)
        wq = wq.reshape(D, -1)
        wkv = wkv.reshape(D, -1)
        wo = wo.reshape(D, -1)
        seq_normed = seq_normed.reshape(seq_len, D)

        order = jnp.stack([m, m ^ 2, m ^ 1, m ^ 3])

        def in_order(vector):
            return vector.reshape(n_mp, rows)[order].reshape(-1)

        segments = segment_ids[0]
        positions = in_order(doc_positions(segments))
        slots = in_order(jnp.arange(seq_len, dtype=jnp.int32))
        segs = in_order(segments)
        pads = in_order(pad_mask[0])
        allowed = (
            (segs[:, None] == segs[None, :])
            & (slots[None, :] <= slots[:, None])
            & ((pads[None, :] == 1) | (slots[None, :] == slots[:, None]))
        )
        local_heads = wq.shape[1] // HEAD_WIDTH
        kv_heads = wkv.shape[1] // 2 // HEAD_WIDTH
        kv_cols = kv_heads * HEAD_WIDTH
        group = local_heads // kv_heads
        scale = HEAD_WIDTH ** (-0.5)
        half_dim = HEAD_WIDTH // 2
        frequency = ROPE_BASE ** (-jnp.arange(half_dim, dtype=F32) * 2.0 / HEAD_WIDTH)
        angles = positions.astype(F32)[:, None] * frequency[None, :]
        angles = jnp.concatenate([angles, angles], -1)
        cosine = jnp.cos(angles)[:, None, :]
        sine = jnp.sin(angles)[:, None, :]

        query_linear = mm(seq_normed, wq).reshape(seq_len, local_heads, HEAD_WIDTH)
        kv_linear = mm(seq_normed, wkv)
        key_linear = kv_linear[:, :kv_cols].reshape(seq_len, kv_heads, HEAD_WIDTH)
        value_bf = kv_linear[:, kv_cols:].astype(BF).reshape(seq_len, kv_heads, HEAD_WIDTH)
        query_bf = rotate(query_linear, cosine, sine).astype(BF).reshape(
            seq_len, kv_heads, group, HEAD_WIDTH
        )
        key_bf = rotate(key_linear, cosine, sine).astype(BF)

        def masked_scores():
            raw = (
                jnp.einsum("qkgd,pkd->kgqp", query_bf, key_bf, preferred_element_type=F32) * scale
            )
            bent = jnp.tanh(raw / SOFT_CAP)
            return bent, jnp.where(allowed[None, None], SOFT_CAP * bent, MASKED_SCORE)

        _, capped = masked_scores()
        row_top = jnp.max(capped, axis=-1, keepdims=True)
        log_total = row_top + jnp.log(jnp.sum(jnp.exp(capped - row_top), axis=-1, keepdims=True))
        probs_bf = jnp.exp(capped - log_total).astype(BF)
        mixed_bf = (
            jnp.einsum("kgqp,pkd->qkgd", probs_bf, value_bf, preferred_element_type=F32)
            .reshape(seq_len, -1)
            .astype(BF)
        )
        half_seq = seq_len // 2

        def parts_of(near, far):
            return near.reshape(-1, rows, D), far.astype(BF).reshape(-1, rows, D)

        near, far = parts_of(mm_cols(mixed_bf[:half_seq], wo), mm_cols(mixed_bf[half_seq:], wo))
        attended, hidden_in, group_ffn, w_full = mid(n_dp, n_mp, near, far, inputs, gain_rows, low_mlp)
        w_full = w_full.reshape(3, D, -1)
        group_ffn = group_ffn.reshape(8 * rows, D)
        half_tok = 4 * rows
        gate = mm(group_ffn, w_full[0])
        up = mm(group_ffn, w_full[1])
        activated_bf = (jax.nn.gelu(gate, approximate=True) * up).astype(BF)
        near, far = parts_of(
            mm_cols(activated_bf[:half_tok], w_full[2]), mm_cols(activated_bf[half_tok:], w_full[2])
        )
        live = lax.dynamic_slice_in_dim(pad_mask[0], m * rows, rows).astype(F32)[:, None]
        outputs, grad_gain_three, group_grad = turn(
            n_dp, n_mp, near, far, hidden_in, gain_rows, out_grad, live
        )
        group_grad = group_grad.reshape(8 * rows, D)
        grad_act = mm(group_grad, w_full[2])
        grad_down = mm_rows(group_grad, activated_bf)
        _, act_pull = jax.vjp(lambda a, b: jax.nn.gelu(a, approximate=True) * b, gate, up)
        grad_gate, grad_up = act_pull(grad_act)
        grad_gate = grad_gate.astype(BF)
        grad_up = grad_up.astype(BF)
        near, far = parts_of(
            mm_cols(grad_gate[:half_tok], w_full[0]) + mm_cols(grad_up[:half_tok], w_full[1]),
            mm_cols(grad_gate[half_tok:], w_full[0]) + mm_cols(grad_up[half_tok:], w_full[1]),
        )
        grads = jnp.stack(
            [mm_rows(group_ffn, grad_gate).astype(BF), mm_rows(group_ffn, grad_up).astype(BF), grad_down.astype(BF)]
        ).reshape(3, nj, 2, wrows, -1)
        grad_hidden, grad_gain_one, grad_gain_two, seq_grad, sum_mlp, square_mlp = back(
            n_dp, n_mp, near, far, hidden_in, attended, gain_rows, out_grad, live, grads
        )
        seq_grad = seq_grad.reshape(seq_len, D)
        grad_mixed = mm(seq_grad, wo).astype(BF).reshape(seq_len, kv_heads, group, HEAD_WIDTH)
        grad_out_w = mm_rows(seq_grad, mixed_bf).astype(BF).reshape(n_dp, wrows, -1)

        bent, capped = masked_scores()
        probs = jnp.exp(capped - log_total)
        probs_bf = probs.astype(BF)
        grad_value = jnp.einsum("kgqp,qkgd->pkd", probs_bf, grad_mixed, preferred_element_type=F32)
        grad_probs = jnp.einsum("qkgd,pkd->kgqp", grad_mixed, value_bf, preferred_element_type=F32)
        inner_sum = jnp.sum(probs * grad_probs, axis=-1, keepdims=True)
        grad_raw = (probs * (grad_probs - inner_sum) * (1.0 - bent * bent)).astype(BF)
        grad_query = (
            jnp.einsum("kgqp,pkd->qkgd", grad_raw, key_bf, preferred_element_type=F32) * scale
        ).reshape(seq_len, local_heads, HEAD_WIDTH)
        grad_key = (
            jnp.einsum("kgqp,qkgd->pkd", grad_raw, query_bf, preferred_element_type=F32) * scale
        )
        grad_q = rotate_back(grad_query, cosine, sine).reshape(seq_len, -1).astype(BF)
        grad_kv = jnp.concatenate(
            [
                rotate_back(grad_key, cosine, sine).reshape(seq_len, -1).astype(BF),
                grad_value.reshape(seq_len, -1).astype(BF),
            ],
            1,
        )
        near, far = parts_of(
            mm_cols(grad_q[:half_seq], wq) + mm_cols(grad_kv[:half_seq], wkv),
            mm_cols(grad_q[half_seq:], wq) + mm_cols(grad_kv[half_seq:], wkv),
        )
        gq = mm_rows(seq_normed, grad_q).astype(BF).reshape(n_dp, wrows, -1)
        gkv = mm_rows(seq_normed, grad_kv).astype(BF).reshape(n_dp, wrows, -1)
        grad_in, grad_gain_zero, sum_q, sum_kv, sum_o = tail(
            n_dp, n_mp, near, far, inputs, gain_rows, grad_hidden, gq, gkv, grad_out_w
        )
        terms = jnp.concatenate([grad_gain_zero, grad_gain_one, grad_gain_two, grad_gain_three])
        square = jnp.sum(square_mlp)
        for part in (sum_q, sum_kv, sum_o):
            square = square + jnp.sum(part * part)
        square = jnp.broadcast_to(square * (1.0 / 1024.0), (8, 128))
        sum_gains, squares = finish_all(n_dp, n_mp, terms.reshape(n_dp * n_mp, 1, -1), square)
        grad_norm = jnp.sqrt(jnp.sum(squares)).reshape(1)
        factor = jnp.minimum(1.0, CLIP_SCALE * math.sqrt(PARAMS) / grad_norm[0])

        new_w_qo, new_m_qo, new_v_qo = adam_update(w_qo, m_qo, v_qo, jnp.stack([sum_q, sum_o]), factor)
        new_w_kv, new_m_kv, new_v_kv = adam_update(
            w_kv, m_kv, v_kv, jnp.stack([sum_kv[:, :kv_cols], sum_kv[:, kv_cols:]]), factor
        )
        new_w_mlp, new_m_mlp, new_v_mlp = adam_update(w_mlp, m_mlp, v_mlp, sum_mlp, factor)
        new_gains, new_m_gains, new_v_gains = adam_update(
            norm_gains, m_gains, v_gains, sum_gains.reshape(-1), factor
        )
        return (
            outputs, grad_in, grad_norm, new_w_qo, new_w_kv, new_w_mlp, new_gains,
            new_m_qo, new_m_kv, new_m_mlp, new_m_gains, new_v_qo, new_v_kv, new_v_mlp, new_v_gains,
        )

    return local


def solution(mesh):
    tokens = P(("dp", "mp"), None)
    weight = P(None, "dp", "mp")
    flat = P(("dp", "mp"))
    per_weight = (weight, weight, weight, flat)
    return jax.shard_map(
        build_local(mesh.shape["dp"], mesh.shape["mp"]),
        mesh=mesh,
        in_specs=(tokens, tokens, P("dp", None), P("dp", None), P()) + per_weight * 3,
        out_specs=(tokens, tokens, P()) + per_weight * 3,
        check_vma=False,
    )
```

```python
import functools
import math

import jax
import jax.numpy as jnp
from jax import lax
from jax.experimental import pallas as pl
from jax.experimental.pallas import tpu as pltpu
from jax.sharding import PartitionSpec as P

D = 2304
HEAD_WIDTH = 256
FF = 9216
NORMS = 4
QW = 2048
PARAMS = 77865984

EPSILON = 1e-06
SOFT_CAP = 50.0
ROPE_BASE = 10000.0
MASKED_SCORE = -1e30
FIRST_DECAY = 0.9
SECOND_DECAY = 0.95
LEARN_RATE = 0.04
WEIGHT_DECAY = 0.1
ADAM_EPSILON = 1e-08
CLIP_SCALE = 0.5

BF = jnp.bfloat16
F32 = jnp.float32


def quantize(master, fan_in, selector):
    return quantize_by(master, jnp.float32(1.0 / (32.0 * math.sqrt(fan_in))), selector)


def quantize_by(master, step, selector):
    spacing = jnp.where(selector == 0, 1.0, jnp.where(selector == 1, 16.0, 64.0)).astype(F32)
    half = jnp.floor(spacing * 0.5)
    inverse = 1.0 / spacing
    codes = jnp.clip(jnp.floor(master / step + 0.5), -128.0, 127.0)
    top = 128.0 * inverse
    sliced = jnp.clip(jnp.floor((codes + half) * inverse), -top, top - 1.0)
    return ((sliced * spacing) * step).astype(BF)


def inv_root(values):
    return lax.rsqrt(jnp.mean(values * values, axis=-1, keepdims=True) + EPSILON)


def rms_norm(values, norm_gain):
    return values * inv_root(values) * (1.0 + norm_gain)


def rms_back(values, norm_gain, grad):
    root = inv_root(values)
    scaled = grad * (1.0 + norm_gain)
    dot = jnp.mean(values * scaled, axis=-1, keepdims=True)
    grad_values = root * scaled - values * (root * root * root * dot)
    grad_gain = jnp.sum(values * root * grad, axis=0)
    return grad_values, grad_gain


def doc_positions(segments):
    slot_index = jnp.arange(segments.shape[0], dtype=jnp.int32)
    previous = jnp.concatenate([segments[:1] - 1, segments[:-1]])
    starts = segments != previous
    doc_begin = lax.cummax(jnp.where(starts, slot_index, 0), axis=0)
    return slot_index - doc_begin


def rotate(values, cosine, sine):
    half_dim = HEAD_WIDTH // 2
    turned = jnp.concatenate([-values[..., half_dim:], values[..., :half_dim]], -1)
    return values * cosine + turned * sine


def rotate_back(grads, cosine, sine):
    half_dim = HEAD_WIDTH // 2
    scaled = grads * sine
    turned = jnp.concatenate([scaled[..., half_dim:], -scaled[..., :half_dim]], -1)
    return grads * cosine + turned


def mm(left, right):
    return lax.dot_general(left, right, (((1,), (0,)), ((), ())), preferred_element_type=F32)


def mm_rows(left, right):
    return lax.dot_general(left, right, (((0,), (0,)), ((), ())), preferred_element_type=F32)


def mm_cols(left, right):
    return lax.dot_general(left, right, (((1,), (1,)), ((), ())), preferred_element_type=F32)


def adam_update(master, first_moment, second_moment, gradient, factor):
    clipped = gradient * factor
    new_first = FIRST_DECAY * first_moment + (1.0 - FIRST_DECAY) * clipped
    new_second = SECOND_DECAY * second_moment + (1.0 - SECOND_DECAY) * clipped * clipped
    new_master = master - LEARN_RATE * (
        new_first / (jnp.sqrt(new_second) + ADAM_EPSILON) + WEIGHT_DECAY * master
    )
    return (new_master, new_first, new_second)


MESH = pl.DeviceIdType.MESH
ANY = pl.BlockSpec(memory_space=pl.ANY)
VMEM = pl.BlockSpec(memory_space=pltpu.VMEM)
ROWS = 32


class Net:
    def __init__(self, n_dp, n_mp, send_sems, recv_sems, local_sems=None):
        self.n_dp, self.n_mp = n_dp, n_mp
        self.send_sems, self.recv_sems, self.local_sems = send_sems, recv_sems, local_sems
        self.used, self.used_local, self.open = 0, 0, []
        self.i, self.m = lax.axis_index("dp"), lax.axis_index("mp")
        self.y, self.j = self.i % 2, self.i // 2
        self.zl = self.j % 2
        self.c, self.x = self.m % 2, self.m // 2
        self.core_n = (self.i, self.m + 1 - 2 * self.c)
        self.x_n = (self.i, (self.m + 2) % 4)
        self.y_n = (self.i + 1 - 2 * self.y, self.m)
        self.z_n = (self.i + 2 - 4 * self.zl, self.m)

    def z_at(self, d):
        nj = self.n_dp // 2
        return (((self.j + d) % nj) * 2 + self.y, self.m)

    def place(self):
        return (1 - self.y) * self.j + self.y * (self.n_dp - 1 - self.j)

    def ring(self, at):
        n, nj = self.n_dp, self.n_dp // 2
        at = at % n
        late = at // nj
        return (1 - late) * 2 * at + late * (2 * (n - 1 - at) + 1)

    def meet(self, devices):
        barrier = pltpu.get_barrier_semaphore()
        for device in devices:
            pl.semaphore_signal(barrier, inc=1, device_id=device, device_id_type=MESH)
        pl.semaphore_wait(barrier, len(devices))

    def send(self, src, dst, device):
        at = self.used
        self.used += 1
        copy = pltpu.make_async_remote_copy(
            src_ref=src, dst_ref=dst, send_sem=self.send_sems.at[at], recv_sem=self.recv_sems.at[at],
            device_id=device, device_id_type=MESH,
        )
        copy.start()
        self.open.append(copy.wait_send)
        return copy

    def move(self, src, dst):
        at = self.used_local
        self.used_local += 1
        copy = pltpu.make_async_copy(src, dst, self.local_sems.at[at])
        copy.start()
        return copy

    def keep(self, src, dst):
        self.open.append(self.move(src, dst).wait)

    def close(self):
        for wait in self.open:
            wait()


def upper(count):
    return count // 16 * 8


def dma(n):
    return pltpu.SemaphoreType.DMA((n,))


def call(kernel, outs, out_specs, in_specs, scratch, cid, mb, flops=0):
    return pl.pallas_call(
        kernel,
        out_shape=outs,
        in_specs=in_specs,
        out_specs=out_specs,
        scratch_shapes=scratch,
        compiler_params=pltpu.CompilerParams(
            collective_id=cid, has_side_effects=True, vmem_limit_bytes=mb << 20
        ),
    )


def by_rows(total, body, carry=0):
    return lax.fori_loop(
        0, total // ROWS, lambda t, state: body(pl.ds(pl.multiple_of(t * ROWS, ROWS), ROWS), state), carry
    )


def everyone(n_dp, n_mp, i, m):
    flat = i * n_mp + m
    total = n_dp * n_mp
    return [(((flat + t) % total) // n_mp, (flat + t) % n_mp) for t in range(1, total)]


def spread_kernel(n_dp, n_mp, own, full, ss, rs, ls):
    net = Net(n_dp, n_mp, ss, rs, ls)
    others = everyone(n_dp, n_mp, net.i, net.m)
    net.meet(others)
    flat = net.i * n_mp + net.m
    copies = [net.send(own, full.at[flat], device) for device in others]
    net.keep(own, full.at[flat])
    for copy in copies:
        copy.wait_recv()
    net.close()


def spread(n_dp, n_mp, own):
    total = n_dp * n_mp
    return call(
        functools.partial(spread_kernel, n_dp, n_mp),
        jax.ShapeDtypeStruct((total,) + own.shape, own.dtype), VMEM, [VMEM],
        [dma(total), dma(total), dma(1)], 1, 16,
    )(own)


def gather_seq_steps(net, own, seq):
    far = net.send(own, seq.at[1], net.x_n)
    near = net.send(own, seq.at[2], net.core_n)
    net.keep(own, seq.at[0])

    def finish():
        far.wait_recv()
        both = net.send(seq.at[1], seq.at[3], net.core_n)
        near.wait_recv()
        both.wait_recv()

    return finish


def head_kernel(n_dp, n_mp, q, kv, o, tok, wq, wkv, wo, seq, ss, rs, ls):
    net = Net(n_dp, n_mp, ss, rs, ls)
    p = net.place()
    right = (net.ring(p + 1), net.m)
    left = (net.ring(p + n_dp - 1), net.m)
    net.meet([right, left, net.x_n, net.core_n])
    wrows = o.shape[0]
    hr = upper(wrows)
    top, low = pl.ds(0, hr), pl.ds(hr, wrows - hr)
    a = net.send(q, wq.at[net.i], right)
    b = net.send(kv, wkv.at[net.i], left)
    finish = gather_seq_steps(net, tok, seq)
    net.keep(q, wq.at[net.i])
    net.keep(kv, wkv.at[net.i])
    net.keep(o, wo.at[net.i])
    for hop in range(1, n_dp):
        from_right, from_left = net.ring(p + n_dp - hop), net.ring(p + hop)
        a.wait_recv()
        if hop < n_dp - 1:
            a = net.send(wq.at[from_right], wq.at[from_right], right)
        else:
            oa = net.send(o.at[top], wo.at[net.i, top], right)
        b.wait_recv()
        if hop < n_dp - 1:
            b = net.send(wkv.at[from_left], wkv.at[from_left], left)
        else:
            ob = net.send(o.at[low], wo.at[net.i, low], left)
        if hop == n_dp // 2:
            finish()
    for hop in range(1, n_dp):
        from_right, from_left = net.ring(p + n_dp - hop), net.ring(p + hop)
        oa.wait_recv()
        if hop < n_dp - 1:
            oa = net.send(wo.at[from_right, top], wo.at[from_right, top], right)
        ob.wait_recv()
        if hop < n_dp - 1:
            ob = net.send(wo.at[from_left, low], wo.at[from_left, low], left)
    net.close()


def head(n_dp, n_mp, q, kv, o, tok):
    full = lambda a: jax.ShapeDtypeStruct((n_dp,) + a.shape, BF)
    count = 4 * n_dp + 8
    return call(
        functools.partial(head_kernel, n_dp, n_mp),
        [full(q), full(kv), full(o), jax.ShapeDtypeStruct((4,) + tok.shape, BF)],
        [ANY] * 4, [ANY] * 4, [dma(count), dma(count), dma(8)], 2, 16,
    )(q, kv, o, tok)


def gather_pair_steps(net, own, group, split=False):
    far = net.send(own, group.at[2], net.x_n)
    zed = net.send(own, group.at[1], net.z_n)
    near = net.send(own, group.at[4], net.core_n)
    net.keep(own, group.at[0])

    def finish(between=lambda: None):
        head = pl.ds(0, D // 2) if split else pl.ds(0, D)
        rest = pl.ds(D // 2, D // 2)
        zed.wait_recv()
        both = net.send(group.at[1, :, head], group.at[3, :, head], net.x_n)
        far.wait_recv()
        if split:
            other = net.send(group.at[2, :, rest], group.at[3, :, rest], net.z_n)
        near_z = net.send(group.at[1], group.at[5], net.core_n)
        near_x = net.send(group.at[2], group.at[6], net.core_n)
        between()
        both.wait_recv()
        if split:
            other.wait_recv()
        near_both = net.send(group.at[3], group.at[7], net.core_n)
        for copy in (near, near_z, near_x, near_both):
            copy.wait_recv()

    return finish


def pair_partners(net, with_y):
    nj = net.n_dp // 2
    zs = [net.z_at(d) for d in range(1, nj)] if with_y else [net.z_n]
    return [net.core_n, net.x_n] + zs + ([net.y_n] if with_y else [])


def row_tiles(total, size, body):
    lax.fori_loop(
        0, total // size, lambda t, state: (body(pl.ds(pl.multiple_of(t * size, size), size)), state)[1], 0
    )


def project(seq, wq, wkv, cosine, sine, q, k, v):
    total = seq.shape[0]
    kv_cols = k.shape[1]
    half = HEAD_WIDTH // 2

    def body(at):
        tokens = seq[at]
        c, s = cosine[at], sine[at]

        def turn(lin, out, cols):
            for h in range(0, cols, HEAD_WIDTH):
                a, b = lin[:, h : h + half], lin[:, h + half : h + HEAD_WIDTH]
                out[at, h : h + half] = (a * c - b * s).astype(BF)
                out[at, h + half : h + HEAD_WIDTH] = (b * c + a * s).astype(BF)

        turn(mm(tokens, wq[...]), q, q.shape[1])
        lin = mm(tokens, wkv[...])
        turn(lin, k, kv_cols)
        v[at] = lin[:, kv_cols:].astype(BF)

    row_tiles(total, total // 2, body)


def allowed_tile(marks_col, marks_row, at):
    segs, slots = marks_col[at, 0:1], marks_col[at, 1:2]
    seg_row, slot_row, pad_row = marks_row[0:1], marks_row[1:2], marks_row[2:3]
    same_slot = slot_row == slots
    return (seg_row == segs) & (slot_row <= slots) & ((pad_row == 1) | same_slot)


def tile_probs(q, k, allowed, at, head, group):
    cols = slice(head * HEAD_WIDTH, (head + 1) * HEAD_WIDTH)
    kv = head // group
    kv_at = slice(kv * HEAD_WIDTH, (kv + 1) * HEAD_WIDTH)
    bent = jnp.tanh(mm_cols(q[at, cols], k[:, kv_at]) * (HEAD_WIDTH**-0.5 / SOFT_CAP))
    raised = jnp.where(allowed, jnp.exp(SOFT_CAP * bent), 0.0)
    return bent, raised / jnp.sum(raised, axis=-1, keepdims=True)


def attend(q, k, v, marks_col, marks_row, mixed):
    total = q.shape[0]
    heads, group = q.shape[1] // HEAD_WIDTH, q.shape[1] // k.shape[1]

    def body(at):
        allowed = allowed_tile(marks_col, marks_row, at)
        for head in range(heads):
            _, probs = tile_probs(q, k, allowed, at, head, group)
            kv = head // group
            kv_at = slice(kv * HEAD_WIDTH, (kv + 1) * HEAD_WIDTH)
            mixed[at, head * HEAD_WIDTH : (head + 1) * HEAD_WIDTH] = mm(
                probs.astype(BF), v[:, kv_at]
            ).astype(BF)

    row_tiles(total, 128, body)


def out_project(mixed, wo, part):
    blocks, rows, _ = part.shape
    wide = D // 3
    for pair in range(blocks // 2 - 1, -1, -1):
        for n in range(0, D, wide):
            got = mm_cols(mixed[pair * 2 * rows : (pair + 1) * 2 * rows], wo[n : n + wide]).astype(BF)
            part[pair * 2, :, n : n + wide] = got[:rows]
            part[pair * 2 + 1, :, n : n + wide] = got[rows:]


def chunks(wrows):
    return ((0, upper(wrows)), (upper(wrows), wrows - upper(wrows)))


def mid_kernel(
    n_dp, n_mp, seq, wq, wkv, wo, cosine, sine, marks_col, marks_row, inputs, gains, low,
    q, k, v, mixed, att, hid, group, full0, full1,
    part, r1, s2, r2, own, ss, rs, ls,
):
    net = Net(n_dp, n_mp, ss, rs, ls)
    net.meet(pair_partners(net, True))
    nj = n_dp // 2
    full = (full0, full1)
    rows = inputs.shape[0]
    wrows, width = full0.shape[1:]
    half = lambda which: pl.ds(pl.multiple_of(which * width, width), width)
    pieces = [(w, pl.ds(first, count)) for w in (0, 1) for first, count in chunks(wrows)]
    flight, relays = {}, []

    def weights_out(n):
        w, at = pieces[n]
        own_half = low.at[w, at, half(net.zl)]
        net.keep(own_half, full[w].at[net.i, at])
        relays.append(net.send(own_half, full[w].at[net.i, at], net.y_n))
        for d in range(1, nj):
            flight[n, d] = net.send(
                low.at[w, at, half(((net.j + d) % nj) % 2)], full[w].at[net.i, at], net.z_at(d)
            )

    def weights_on(n):
        w, at = pieces[n]
        for d in range(1, nj):
            flight[n, d].wait_recv()
            source = ((net.j + nj - d) % nj) * 2 + net.y
            relays.append(net.send(full[w].at[source, at], full[w].at[source, at], net.y_n))

    weights_out(0)
    weights_out(1)
    project(seq, wq, wkv, cosine, sine, q, k, v)
    attend(q, k, v, marks_col, marks_row, mixed)
    out_project(mixed, wo, part)
    c1 = net.send(part.at[3], r1.at[1], net.core_n)
    c0 = net.send(part.at[2], r1.at[0], net.core_n)
    c1.wait_recv()

    def first(at, state):
        s2[at] = (part[1, at].astype(F32) + r1[1, at].astype(F32)).astype(BF)
        return state

    by_rows(rows, first)
    x = net.send(s2, r2, net.x_n)
    c0.wait_recv()
    weights_on(0)
    weights_out(2)
    x.wait_recv()
    g1, g2 = 1.0 + gains[1:2], 1.0 + gains[2:3]

    def second(at, state):
        total = part[0, at].astype(F32) + r1[0, at].astype(F32) + r2[at].astype(F32)
        att[at] = total
        hidden = inputs[at] + total * inv_root(total) * g1
        hid[at] = hidden
        own[at] = (hidden * inv_root(hidden) * g2).astype(BF)
        return state

    by_rows(rows, second)
    finish = gather_pair_steps(net, own, group)
    weights_on(1)
    weights_out(3)
    finish(lambda: weights_on(2))
    weights_on(3)
    for copy in relays:
        copy.wait_recv()
    net.close()


def mid(n_dp, n_mp, seq, wq, wkv, wo, cosine, sine, marks_col, marks_row, inputs, gains, low):
    rows = inputs.shape[0]
    nj = n_dp // 2
    count = 16 + 8 * nj
    block = (rows, D)
    wrows, width = low.shape[1], low.shape[2] // 2
    kv_cols = wkv.shape[1] // 2
    many = lambda n: pltpu.VMEM((n,) + block, BF)
    bf = lambda *shape: jax.ShapeDtypeStruct(shape, BF)
    total = seq.shape[0]
    return call(
        functools.partial(mid_kernel, n_dp, n_mp),
        [
            bf(total, wq.shape[1]), bf(total, kv_cols), bf(total, kv_cols), bf(total, wq.shape[1]),
            jax.ShapeDtypeStruct(block, F32), jax.ShapeDtypeStruct(block, F32),
            bf(8, *block), bf(n_dp, wrows, width), bf(n_dp, wrows, width),
        ],
        [VMEM] * 6 + [ANY] * 3, [VMEM] * 10 + [ANY],
        [many(4), many(2), pltpu.VMEM(block, BF), pltpu.VMEM(block, BF), pltpu.VMEM(block, BF),
         dma(count), dma(count), dma(8)],
        3, 56,
    )(seq, wq, wkv, wo, cosine, sine, marks_col, marks_row, inputs, gains, low)


def reduce_pair_steps(net, near, far, r1, s2, r2, s3, r3, rows, loaded, split=False):
    cores = {k: net.send(far.at[k], r1.at[k], net.core_n) for k in (3, 2, 1, 0)}
    plan = [(pl.ds(0, D // 2 if split else D), (3, 2), net.x_n, 1, net.z_n)]
    if split:
        plan.append((pl.ds(D // 2, D // 2), (3, 1), net.z_n, 2, net.x_n))
    firsts = {}
    loaded.wait()
    for k in (3, 2, 1) if split else (3, 2):
        cores[k].wait_recv()
        for part, (cols, blocks, device, _, _) in enumerate(plan):
            if k not in blocks:
                continue
            at_block = blocks.index(k)

            def add(at, state, k=k, cols=cols, at_block=at_block):
                s2[at_block, at, cols] = (near[k, at, cols].astype(F32) + r1[k, at, cols].astype(F32)).astype(BF)
                return state

            by_rows(rows, add)
            firsts[part, at_block] = net.send(s2.at[at_block, :, cols], r2.at[at_block, :, cols], device)
    for k in (0,) if split else (1, 0):
        cores[k].wait_recv()
    last = []
    for part, (cols, blocks, _, second, device) in enumerate(plan):
        firsts[part, 0].wait_recv()

        def add(at, state, cols=cols, second=second):
            s3[at, cols] = (
                near[second, at, cols].astype(F32) + r1[second, at, cols].astype(F32) + r2[0, at, cols].astype(F32)
            ).astype(BF)
            return state

        by_rows(rows, add)
        last.append(net.send(s3.at[:, cols], r3.at[:, cols], device))
    for part in range(len(plan)):
        firsts[part, 1].wait_recv()
    return last


def pair_sum(near, r1, r2, r3, at):
    return near[0, at].astype(F32) + r1[0, at].astype(F32) + r2[1, at].astype(F32) + r3[at].astype(F32)


def pair_scratch(rows):
    block = (rows, D)
    return [
        pltpu.VMEM((4,) + block, BF),
        pltpu.VMEM((4,) + block, BF), pltpu.VMEM((2,) + block, BF), pltpu.VMEM((2,) + block, BF),
        pltpu.VMEM(block, BF), pltpu.VMEM(block, BF), pltpu.VMEM(block, BF),
    ]


def rms_back_rows(values, gain, grad):
    root = inv_root(values)
    scaled = grad * gain
    dot = jnp.mean(values * scaled, axis=-1, keepdims=True)
    return root * scaled - values * (root * root * root * dot), jnp.sum(values * root * grad, axis=0, keepdims=True)


def turn_kernel(
    n_dp, n_mp, part, hid, gains, out_grad, live, outputs, dgain, group,
    near, r1, s2, r2, s3, r3, own, ss, rs, ls,
):
    net = Net(n_dp, n_mp, ss, rs, ls)
    net.meet(pair_partners(net, False))
    rows = hid.shape[0]
    far = part.at[pl.ds(4, 4)]
    loaded = net.move(part.at[pl.ds(0, 4)], near)
    for copy in reduce_pair_steps(net, near, far, r1, s2, r2, s3, r3, rows, loaded, True):
        copy.wait_recv()
    g3 = 1.0 + gains[3:4]

    def last(at, state):
        total = pair_sum(near, r1, r2, r3, at)
        outputs[at] = hid[at] + total * inv_root(total) * g3
        grad, dg = rms_back_rows(total, g3, out_grad[at] * live[at])
        own[at] = grad.astype(BF)
        return state + dg

    dgain[...] = by_rows(rows, last, jnp.zeros((1, D), F32))
    gather_pair_steps(net, own, group, True)()
    net.close()


def turn(n_dp, n_mp, part, hid, gains, out_grad, live):
    rows = hid.shape[0]
    block = (rows, D)
    return call(
        functools.partial(turn_kernel, n_dp, n_mp),
        [jax.ShapeDtypeStruct(block, F32), jax.ShapeDtypeStruct((1, D), F32), jax.ShapeDtypeStruct((8,) + block, BF)],
        [VMEM, VMEM, ANY], [ANY, VMEM, VMEM, VMEM, VMEM],
        pair_scratch(rows) + [dma(32), dma(32), dma(4)], 4, 48,
    )(part, hid, gains, out_grad, live)


def in_steps(count, body, carry=0, first=0):
    step = 16 if count % 16 == 0 else 8
    return lax.fori_loop(
        0, count // step,
        lambda t, state: body(pl.ds(pl.multiple_of(first + t * step, 8), step), state, step), carry,
    )


class Scatter:
    def __init__(self, net, grads, stay, came, last):
        self.net, self.grads, self.stay, self.came, self.last = net, grads, stay, came, last
        self.nj, self.wrows, self.width = came.shape
        self.turns = list(range(1, self.nj)) + [0]
        self.ys, self.moves, self.zs = {}, {}, {}

    def along_y(self):
        net = self.net
        for d in self.turns:
            at = (net.j + d) % self.nj
            self.ys[d] = net.send(self.grads.at[at, 1 - net.y], self.came.at[d], net.y_n)
            self.moves[d] = net.move(self.grads.at[at, net.y], self.stay.at[d])

    def along_z(self, turns):
        for d in turns:
            self.ys[d].wait_recv()
            self.moves[d].wait()

            def add(at, state, step, d=d):
                self.stay[d, at] = (self.stay[d, at].astype(F32) + self.came[d, at].astype(F32)).astype(BF)
                return state

            in_steps(self.wrows, add)
            if d:
                self.zs[d] = self.net.send(self.stay.at[d], self.last.at[d - 1], self.net.z_at(d))

    def landed(self):
        for d in range(1, self.nj):
            self.zs[d].wait_recv()

    def halves(self, total, sums):
        self.landed()

        def collect(at, state, step):
            both = [self.stay[0, at].astype(F32), jnp.zeros((step, self.width), F32)]
            for d in range(1, self.nj):
                both[d % 2] = both[d % 2] + self.last[d - 1, at].astype(F32)
            for parity in range(2):
                total[parity, at] = both[parity]
                sq = both[parity] * both[parity]
                for r in range(0, step, 8):
                    state = state + sq[r : r + 8]
            return state

        square = in_steps(self.wrows, collect, jnp.zeros((8, self.width), F32))
        for parity in range(2):
            half = (self.net.zl + parity) % 2
            self.net.keep(total.at[parity], sums.at[:, pl.ds(pl.multiple_of(half * self.width, self.width), self.width)])
        return square

    def whole(self, out):
        self.landed()

        def collect(at, state, step):
            value = self.stay[0, at].astype(F32)
            for d in range(1, self.nj):
                value = value + self.last[d - 1, at].astype(F32)
            out[at] = value
            return state

        in_steps(self.wrows, collect)


def scatter_scratch(nj, wrows, width):
    return [
        pltpu.VMEM((nj, wrows, width), BF), pltpu.VMEM((nj, wrows, width), BF),
        pltpu.VMEM((nj - 1, wrows, width), BF),
    ]


def back_kernel(
    n_dp, n_mp, part, hid, att, gains, out_grad, live, grads,
    ghid, dg1, dg2, seq, sums, squares,
    near, r1, s2, r2, s3, r3, own, stay, came, last, total, ss, rs, ls,
):
    net = Net(n_dp, n_mp, ss, rs, ls)
    nj = n_dp // 2
    net.meet(pair_partners(net, True))
    rows = hid.shape[0]
    far = part.at[pl.ds(4, 4)]
    loaded = net.move(part.at[pl.ds(0, 4)], near)
    weight = Scatter(net, grads, stay, came, last)
    weight.along_y()
    last_sums = reduce_pair_steps(net, near, far, r1, s2, r2, s3, r3, rows, loaded)
    weight.along_z(weight.turns[:2])
    for copy in last_sums:
        copy.wait_recv()
    g1, g2 = 1.0 + gains[1:2], 1.0 + gains[2:3]

    def rows_back(at, state):
        grad = pair_sum(near, r1, r2, r3, at)
        part_hid, d2 = rms_back_rows(hid[at], g2, grad)
        grad_hidden = out_grad[at] * live[at] + part_hid
        ghid[at] = grad_hidden
        grad_att, d1 = rms_back_rows(att[at], g1, grad_hidden)
        own[at] = grad_att.astype(BF)
        return state[0] + d1, state[1] + d2

    zero = jnp.zeros((1, D), F32)
    done1, done2 = by_rows(rows, rows_back, (zero, zero))
    dg1[...] = done1
    dg2[...] = done2
    finish = gather_seq_steps(net, own, seq)
    weight.along_z(weight.turns[2:])
    finish()
    squares[...] = weight.halves(total, sums)
    net.close()


def back(n_dp, n_mp, part, hid, att, gains, out_grad, live, grads):
    rows = hid.shape[0]
    block = (rows, D)
    nj = n_dp // 2
    _, _, wrows, width = grads.shape
    count = 24 + 3 * nj
    return call(
        functools.partial(back_kernel, n_dp, n_mp),
        [
            jax.ShapeDtypeStruct(block, F32), jax.ShapeDtypeStruct((1, D), F32), jax.ShapeDtypeStruct((1, D), F32),
            jax.ShapeDtypeStruct((4,) + block, BF), jax.ShapeDtypeStruct((wrows, 2 * width), F32),
            jax.ShapeDtypeStruct((8, width), F32),
        ],
        [VMEM, VMEM, VMEM, ANY, ANY, VMEM], [ANY, VMEM, VMEM, VMEM, VMEM, VMEM, ANY],
        pair_scratch(rows) + scatter_scratch(nj, wrows, width)
        + [pltpu.VMEM((2, wrows, width), F32), dma(count), dma(count), dma(10 + nj)],
        5, 58,
    )(part, hid, att, gains, out_grad, live, grads)


def attend_back(q, k, v, gm, marks_col, marks_row, cosine, sine, dq, dk, dv, tiles):
    total = q.shape[0]
    heads, group = q.shape[1] // HEAD_WIDTH, q.shape[1] // k.shape[1]
    size = total // 4
    half = HEAD_WIDTH // 2
    scale = HEAD_WIDTH**-0.5

    def body(t, state):
        at = pl.ds(pl.multiple_of(t * size, size), size)
        allowed = allowed_tile(marks_col, marks_row, at)
        c, s = cosine[at], sine[at]
        for head in range(heads):
            kv = head // group
            cols = slice(head * HEAD_WIDTH, (head + 1) * HEAD_WIDTH)
            kv_at = slice(kv * HEAD_WIDTH, (kv + 1) * HEAD_WIDTH)
            bent, probs = tile_probs(q, k, allowed, at, head, group)
            grad = gm[at, cols]
            dv[:, kv_at] += mm_rows(probs.astype(BF), grad)
            gp = mm_cols(grad, v[:, kv_at])
            inner = jnp.sum(probs * gp, axis=-1, keepdims=True)
            ds = (probs * (gp - inner) * (1.0 - bent * bent)).astype(BF)
            dk[:, kv_at] += mm_rows(ds, q[at, cols]) * scale
            turned = mm(ds, k[:, kv_at]) * scale
            a, b = turned[:, :half], turned[:, half:]
            first = head * HEAD_WIDTH
            dq[at, first : first + half] = (a * c + b * s).astype(BF)
            dq[at, first + half : first + HEAD_WIDTH] = (b * c - a * s).astype(BF)
        return state

    lax.fori_loop(tiles[0], tiles[1], body, 0)


def weight_grad(tokens, grads, out):
    wide = D // 3
    for n in range(0, D, wide):
        out[n : n + wide] = mm_rows(tokens[:, n : n + wide], grads[...]).astype(BF)


def close_kernel(
    n_dp, n_mp, seq_grad, seq_normed, q, k, v, mixed, wo, wq, wkv, cosine, sine, marks_col, marks_row,
    inputs, gains, ghid, grads,
    gin, dg0, sum_q, sum_kv, sum_o, sums, squares,
    tokens, normed, wa, gm, dq, dk, dv, dkv, go, gq, gkv, got_q, got_kv, r1, r2,
    stay, came, last, total, ostay, ocame, olast, ss, rs, ls,
):
    net = Net(n_dp, n_mp, ss, rs, ls)
    p = net.place()
    right = (net.ring(p + 1), net.m)
    left = (net.ring(p + n_dp - 1), net.m)
    nj = n_dp // 2
    rows = inputs.shape[0]
    seq_len, wrows = tokens.shape[0], sum_q.shape[0]
    net.meet(
        [net.x_n, net.core_n] + [((net.i + t) % n_dp, net.m) for t in range(1, n_dp)]
    )
    weight = Scatter(net, grads, stay, came, last)
    weight.along_y()
    token_load = net.move(seq_grad, tokens)
    wa_load = net.move(wo, wa)
    normed_load = net.move(seq_normed, normed)
    ghid_load = net.move(ghid, gin)
    dk[...] = jnp.zeros_like(dk)
    dv[...] = jnp.zeros_like(dv)
    token_load.wait()
    wa_load.wait()

    def mix(at):
        gm[at] = mm(tokens[at], wa[...]).astype(BF)

    row_tiles(seq_len, seq_len // 2, mix)
    wa_load = net.move(wq, wa)
    weight_grad(tokens, mixed, go.reshape(D, go.shape[-1]))
    out = Scatter(net, go, ostay, ocame, olast)
    out.along_y()
    attend_back(q, k, v, gm, marks_col, marks_row, cosine, sine, dq, dk, dv, (0, 2))
    weight.along_z(weight.turns[:2])
    attend_back(q, k, v, gm, marks_col, marks_row, cosine, sine, dq, dk, dv, (2, 4))
    weight.along_z(weight.turns[2:])
    kv_cols = k.shape[1]
    half = HEAD_WIDTH // 2

    def turn_keys(at):
        c, s = cosine[at], sine[at]
        for h in range(0, kv_cols, HEAD_WIDTH):
            a, b = dk[at, h : h + half], dk[at, h + half : h + HEAD_WIDTH]
            dkv[at, h : h + half] = (a * c + b * s).astype(BF)
            dkv[at, h + half : h + HEAD_WIDTH] = (b * c - a * s).astype(BF)
        dkv[at, kv_cols:] = dv[at].astype(BF)

    row_tiles(seq_len, 128, turn_keys)
    normed_load.wait()
    weight_grad(normed, dq, gq)
    weight_grad(normed, dkv, gkv)

    def block(at):
        return pl.ds(pl.multiple_of(net.ring(p + 2 * n_dp + at) * wrows, 8), wrows)

    lanes = ((gq, got_q, sum_q, right, -1), (gkv, got_kv, sum_kv, left, 1))
    flight = [net.send(terms.at[block(way)], got.at[0], device) for terms, got, _, device, way in lanes]

    def hop(n):
        end = n == n_dp - 1
        for lane, (terms, got, result, device, way) in enumerate(lanes):
            flight[lane].wait_recv()
            first = net.ring(p + 2 * n_dp + way * (1 + n)) * wrows

            def add(t, state, step):
                at = pl.ds(pl.multiple_of(first + t * step, 8), step)
                here = pl.ds(pl.multiple_of(t * step, 8), step)
                value = got[n - 1, here].astype(F32) + terms[at].astype(F32)
                if end:
                    result[here] = value
                else:
                    terms[at] = value.astype(BF)
                return state

            step = 16 if wrows % 16 == 0 else 8
            lax.fori_loop(0, wrows // step, lambda t, state: add(t, state, step), 0)
            if not end:
                flight[lane] = net.send(terms.at[block(way * (1 + n))], got.at[n], device)

    wa_load.wait()
    wide = D // 3
    copies = []
    for pair in (1, 0):
        at = pl.ds(pair * 2 * rows, 2 * rows)
        for n in range(0, D, wide):
            tokens[at, n : n + wide] = (
                mm_cols(dq[at], wa[n : n + wide]) + mm_cols(dkv[at], wkv[n : n + wide])
            ).astype(BF)
        if pair:
            c1 = net.send(tokens.at[pl.ds(3 * rows, rows)], r1.at[1], net.core_n)
            c0 = net.send(tokens.at[pl.ds(2 * rows, rows)], r1.at[0], net.core_n)
            hop(1)
    c1.wait_recv()

    def add_far(at, state):
        here = pl.ds(pl.multiple_of(rows + at.start, ROWS), ROWS)
        tokens[here] = (tokens[here].astype(F32) + r1[1, at].astype(F32)).astype(BF)
        return state

    by_rows(rows, add_far)
    x = net.send(tokens.at[pl.ds(rows, rows)], r2, net.x_n)
    c0.wait_recv()
    hop(2)
    out.along_z(out.turns)
    hop(3)
    x.wait_recv()
    ghid_load.wait()
    g0 = 1.0 + gains[0:1]

    def rows_in(at, state):
        grad = tokens[at].astype(F32) + r1[0, at].astype(F32) + r2[at].astype(F32)
        part, d0 = rms_back_rows(inputs[at], g0, grad)
        gin[at] = gin[at] + part
        return state + d0

    dg0[...] = by_rows(rows, rows_in, jnp.zeros((1, D), F32))
    for n in range(4, n_dp - 1):
        hop(n)
    squares[...] = weight.halves(total, sums)
    hop(n_dp - 1)
    out.whole(sum_o)
    net.close()


def close(n_dp, n_mp, seq_grad, seq_normed, q, k, v, mixed, wo, wq, wkv, cosine, sine, marks_col, marks_row,
          inputs, gains, ghid, grads):
    rows = inputs.shape[0]
    nj = n_dp // 2
    _, _, wrows, width = grads.shape
    cols, kv_cols = q.shape[1], k.shape[1]
    seq_len = q.shape[0]
    count = 16 + 6 * nj + 2 * n_dp
    vm = lambda *shape: pltpu.VMEM(shape, BF)
    small = jax.ShapeDtypeStruct((wrows, cols), F32)
    return call(
        functools.partial(close_kernel, n_dp, n_mp),
        [
            jax.ShapeDtypeStruct((rows, D), F32), jax.ShapeDtypeStruct((1, D), F32), small,
            jax.ShapeDtypeStruct((wrows, 2 * kv_cols), F32), small,
            jax.ShapeDtypeStruct((wrows, 2 * width), F32), jax.ShapeDtypeStruct((8, width), F32),
        ],
        [VMEM] * 5 + [ANY, VMEM],
        [ANY, ANY] + [VMEM] * 4 + [ANY, ANY] + [VMEM] * 7 + [ANY, ANY],
        [
            vm(seq_len, D), vm(seq_len, D), vm(D, cols), vm(seq_len, cols), vm(seq_len, cols),
            pltpu.VMEM((seq_len, kv_cols), F32), pltpu.VMEM((seq_len, kv_cols), F32), vm(seq_len, 2 * kv_cols),
            vm(nj, 2, wrows, cols), vm(D, cols), vm(D, 2 * kv_cols),
            vm(n_dp - 1, wrows, cols), vm(n_dp - 1, wrows, 2 * kv_cols), vm(2, rows, D), vm(rows, D),
        ]
        + scatter_scratch(nj, wrows, width) + [pltpu.VMEM((2, wrows, width), F32)]
        + scatter_scratch(nj, wrows, cols) + [dma(count), dma(count), dma(10 + 2 * nj)],
        6, 60,
    )(seq_grad, seq_normed, q, k, v, mixed, wo, wq, wkv, cosine, sine, marks_col, marks_row,
      inputs, gains, ghid, grads)


def plain(kernel, grid, outs, out_specs, in_specs, mb, flops):
    return pl.pallas_call(
        kernel,
        out_shape=outs,
        grid=grid,
        in_specs=in_specs,
        out_specs=out_specs,
        compiler_params=pltpu.CompilerParams(
            dimension_semantics=("arbitrary",) * len(grid), vmem_limit_bytes=mb << 20
        ),
        cost_estimate=pl.CostEstimate(flops=flops, bytes_accessed=40 << 20, transcendentals=0),
    )


def whole(shape):
    return pl.BlockSpec(shape, lambda t: (0,) * len(shape), pipeline_mode=pl.Buffered(1))


def tile(rows, cols):
    return pl.BlockSpec((None, rows, cols), lambda t: (t, 0, 0))


GELU = math.sqrt(2.0 / math.pi)


def up_kernel(x, wg, wu, gate, up, act):
    g = mm(x[...], wg[...])
    u = mm(x[...], wu[...])
    gate[...] = g
    up[...] = u
    bend = jnp.tanh(GELU * (g + 0.044715 * (g * g * g)))
    act[...] = (0.5 * g * (1.0 + bend) * u).astype(BF)


def mlp_up(x, wg, wu):
    blocks, rows, _ = x.shape
    width = wg.shape[1]
    shape = (blocks, rows, width)
    return plain(
        up_kernel, (blocks,),
        [jax.ShapeDtypeStruct(shape, F32), jax.ShapeDtypeStruct(shape, F32), jax.ShapeDtypeStruct(shape, BF)],
        [tile(rows, width)] * 3, [tile(rows, D), whole(wg.shape), whole(wu.shape)], 48,
        4 * blocks * rows * D * width,
    )(x, wg, wu)


def down_kernel(act, wd, part):
    part[...] = mm_cols(act[...], wd[...]).astype(BF)


def mlp_down(act, wd):
    blocks, rows, width = act.shape
    return plain(
        down_kernel, (blocks,), jax.ShapeDtypeStruct((blocks, rows, D), BF),
        tile(rows, D), [tile(rows, width), whole(wd.shape)], 32, 2 * blocks * rows * D * width,
    )(act, wd)


def down_back_kernel(grad, gate, up, wg, wu, wd, dgate, dup, part):
    ga = mm(grad[...], wd[...])
    g = gate[...]
    square = g * g
    bend = jnp.tanh(GELU * (g + 0.044715 * (square * g)))
    halved = 0.5 * (1.0 + bend)
    slope = halved + (0.5 * GELU) * g * (1.0 - bend * bend) * (1.0 + (3.0 * 0.044715) * square)
    dg = (ga * up[...] * slope).astype(BF)
    du = (ga * (g * halved)).astype(BF)
    dgate[...] = dg
    dup[...] = du
    part[...] = (mm_cols(dg, wg[...]) + mm_cols(du, wu[...])).astype(BF)


def mlp_back(grad, gate, up, wg, wu, wd):
    blocks, rows, _ = grad.shape
    width = wg.shape[1]
    shape = (blocks, rows, width)
    return plain(
        down_back_kernel, (blocks,),
        [jax.ShapeDtypeStruct(shape, BF), jax.ShapeDtypeStruct(shape, BF), jax.ShapeDtypeStruct((blocks, rows, D), BF)],
        [tile(rows, width), tile(rows, width), tile(rows, D)],
        [tile(rows, D), tile(rows, width), tile(rows, width)] + [whole(wg.shape)] * 3, 56,
        6 * blocks * rows * D * width,
    )(grad, gate, up, wg, wu, wd)


def finish_kernel(n_dp, n_mp, terms, square, total_gain, total_square, got, sgot, mine, ss, rs, ls):
    net = Net(n_dp, n_mp, ss, rs, ls)
    others = everyone(n_dp, n_mp, net.i, net.m)
    net.meet(others)
    flat = net.i * n_mp + net.m
    copies = [
        net.send(terms.at[dp * n_mp + mp], got.at[flat], (dp, mp)) for dp, mp in others
    ]
    net.keep(terms.at[flat], got.at[flat])
    net.open.pop()()
    for copy in copies:
        copy.wait_recv()
    total = lax.fori_loop(0, n_dp * n_mp, lambda t, s: s + got[t], jnp.zeros(got.shape[1:], F32))
    total_gain[...] = total
    mine[...] = square[...] + jnp.sum(total * total) * (1.0 / (mine.shape[0] * mine.shape[1]))
    copies = [net.send(mine, sgot.at[flat], device) for device in others]
    net.keep(mine, sgot.at[flat])
    net.open.pop()()
    for copy in copies:
        copy.wait_recv()
    total_square[...] = lax.fori_loop(0, n_dp * n_mp, lambda t, s: s + sgot[t], jnp.zeros(mine.shape, F32))
    net.close()


def finish_all(n_dp, n_mp, terms, square):
    total = n_dp * n_mp
    shape = terms.shape[1:]
    return call(
        functools.partial(finish_kernel, n_dp, n_mp),
        [jax.ShapeDtypeStruct(shape, F32), jax.ShapeDtypeStruct(square.shape, F32)],
        [VMEM, VMEM], [VMEM, VMEM],
        [
            pltpu.VMEM((total,) + shape, F32), pltpu.VMEM((total,) + square.shape, F32),
            pltpu.VMEM(square.shape, F32), dma(2 * total), dma(2 * total), dma(2),
        ],
        7, 16,
    )(terms, square)


def build_local(n_dp, n_mp):
    nj = n_dp // 2

    def y_swap(value):
        return lax.ppermute(value, "dp", [(k, k ^ 1) for k in range(n_dp)])

    def z_shift(value, d):
        pairs = [(a * 2 + b, ((a + d) % nj) * 2 + b) for a in range(nj) for b in range(2)]
        return lax.ppermute(value, "dp", pairs)

    def scatter_first(grad, y):
        away = lax.dynamic_index_in_dim(grad, 1 - y, 1, keepdims=False)
        stay = lax.dynamic_index_in_dim(grad, y, 1, keepdims=False)
        return stay, y_swap(away)

    def scatter_second(stay, came, j):
        both = (stay.astype(F32) + came.astype(F32)).astype(BF)
        both = [lax.dynamic_index_in_dim(both, (j + d) % nj, 0, keepdims=False) for d in range(nj)]
        return both[0], [z_shift(both[d], d) for d in range(1, nj)]

    def local(
        inputs, out_grad, segment_ids, pad_mask, bit_sel, w_qo, w_kv, w_mlp, norm_gains,
        m_qo, m_kv, m_mlp, m_gains, v_qo, v_kv, v_mlp, v_gains,
    ):
        i, m = lax.axis_index("dp"), lax.axis_index("mp")
        y, j = i % 2, i // 2
        zl = j % 2
        rows = inputs.shape[0]
        seq_len = segment_ids.shape[1]
        wrows = w_qo.shape[1]

        gain_rows = spread(n_dp, n_mp, norm_gains.reshape(1, -1)).reshape(NORMS, D)
        low_q = quantize(w_qo[0], D, bit_sel[0])
        low_o = quantize(w_qo[1], QW, bit_sel[0])
        low_kv = jnp.concatenate([quantize(w_kv[0], D, bit_sel[1]), quantize(w_kv[1], D, bit_sel[1])], 1)
        low_up = quantize(w_mlp[:2], D, bit_sel[2])
        low_down = quantize(w_mlp[2], FF, bit_sel[2])
        norm_in = rms_norm(inputs, gain_rows[0]).astype(BF)
        wq, wkv, wo, seq_normed = head(n_dp, n_mp, low_q, low_kv, low_o, norm_in)
        wq = wq.reshape(D, -1)
        wkv = wkv.reshape(D, -1)
        wo = wo.reshape(D, -1)
        seq_normed = seq_normed.reshape(seq_len, D)

        seq_normed, low_down = lax.optimization_barrier((seq_normed, low_down))
        halves = low_down.reshape(wrows, 2, -1)
        same = jnp.where(zl == 0, halves[:, 0], halves[:, 1])
        other = jnp.where(zl == 0, halves[:, 1], halves[:, 0])
        down_blocks = {0: y_swap(same)}
        for d in range(1, nj):
            down_blocks[d] = z_shift(other if d % 2 else same, d)

        order = jnp.stack([m, m ^ 2, m ^ 1, m ^ 3])

        def in_order(vector):
            return vector.reshape(n_mp, rows)[order].reshape(-1)

        segments = segment_ids[0]
        positions = in_order(doc_positions(segments))
        slots = in_order(jnp.arange(seq_len, dtype=jnp.int32))
        segs = in_order(segments)
        pads = in_order(pad_mask[0])
        kv_cols = wkv.shape[1] // 2
        half_dim = HEAD_WIDTH // 2
        frequency = ROPE_BASE ** (-jnp.arange(half_dim, dtype=F32) * 2.0 / HEAD_WIDTH)
        angles = positions.astype(F32)[:, None] * frequency[None, :]
        cosine = jnp.cos(angles)
        sine = jnp.sin(angles)
        marks = jnp.stack([segs, slots, pads] + [segs] * 5)
        query_bf, key_bf, value_bf, mixed_bf, attended, hidden_in, group_ffn, w_gate, w_up = mid(
            n_dp, n_mp, seq_normed, wq, wkv, wo, cosine, sine, marks.T, marks, inputs, gain_rows, low_up
        )
        w_gate = w_gate.reshape(D, -1)
        w_up = w_up.reshape(D, -1)
        w_down = jnp.zeros((n_dp,) + same.shape, BF)

        def put(block, at):
            return lax.dynamic_update_index_in_dim(w_down, block, at, 0)

        w_down = put(same, i)
        w_down = put(down_blocks[0], i + 1 - 2 * y)
        for d in range(1, nj):
            got, group_ffn = lax.optimization_barrier((down_blocks[d], group_ffn))
            at = ((j + nj - d) % nj) * 2
            w_down = put(got, at + y)
            w_down = put(y_swap(got), at + 1 - y)
        w_down = w_down.reshape(D, -1)
        gate, up, activated = mlp_up(group_ffn, w_gate, w_up)
        part = mlp_down(activated, w_down)
        live = lax.dynamic_slice_in_dim(pad_mask[0], m * rows, rows).astype(F32)[:, None]
        outputs, grad_gain_three, group_grad = turn(
            n_dp, n_mp, part, hidden_in, gain_rows, out_grad, live
        )
        tokens = 8 * rows
        grad_down = mm_rows(group_grad.reshape(tokens, D), activated.reshape(tokens, -1))
        grad_down = grad_down.astype(BF).reshape(nj, 2, wrows, -1)
        grad_down, group_grad = lax.optimization_barrier((grad_down, group_grad))
        down_stay, down_came = scatter_first(grad_down, y)
        grad_gate, grad_up, part = mlp_back(group_grad, gate, up, w_gate, w_up, w_down)
        flat_ffn = group_ffn.reshape(tokens, D)
        grads_gate = mm_rows(flat_ffn, grad_gate.reshape(tokens, -1)).astype(BF).reshape(nj, 2, wrows, -1)
        grads_gate, grad_up, down_came = lax.optimization_barrier((grads_gate, grad_up, down_came))
        down_own, down_shifted = scatter_second(down_stay, down_came, j)
        grads_up = mm_rows(flat_ffn, grad_up.reshape(tokens, -1)).astype(BF).reshape(nj, 2, wrows, -1)
        grad_hidden, grad_gain_one, grad_gain_two, seq_grad, sum_gate, square_gate = back(
            n_dp, n_mp, part, hidden_in, attended, gain_rows, out_grad, live, grads_gate
        )
        seq_grad, down_shifted = lax.optimization_barrier((seq_grad, down_shifted))
        sums = [down_own.astype(F32), 0.0]
        for d in range(1, nj):
            sums[d % 2] = sums[d % 2] + down_shifted[d - 1].astype(F32)
        sum_down = jnp.concatenate(
            [jnp.where(zl == 0, sums[0], sums[1]), jnp.where(zl == 0, sums[1], sums[0])], 1
        )
        grad_in, grad_gain_zero, sum_q, sum_kv, sum_o, sum_up, square_up = close(
            n_dp, n_mp, seq_grad.reshape(seq_len, D), seq_normed, query_bf, key_bf, value_bf, mixed_bf,
            wo, wq, wkv, cosine, sine, marks.T, marks, inputs, gain_rows, grad_hidden, grads_up,
        )
        terms = jnp.concatenate([grad_gain_zero, grad_gain_one, grad_gain_two, grad_gain_three])
        square = jnp.sum(square_gate + square_up)
        for part in (sum_q, sum_kv, sum_o, sum_down):
            square = square + jnp.sum(part * part)
        square = jnp.broadcast_to(square * (1.0 / 1024.0), (8, 128))
        sum_gains, squares = finish_all(n_dp, n_mp, terms.reshape(n_dp * n_mp, 1, -1), square)
        grad_norm = jnp.sqrt(jnp.sum(squares)).reshape(1)
        factor = jnp.minimum(1.0, CLIP_SCALE * math.sqrt(PARAMS) / grad_norm[0])

        new_w_qo, new_m_qo, new_v_qo = adam_update(w_qo, m_qo, v_qo, jnp.stack([sum_q, sum_o]), factor)
        new_w_kv, new_m_kv, new_v_kv = adam_update(
            w_kv, m_kv, v_kv, jnp.stack([sum_kv[:, :kv_cols], sum_kv[:, kv_cols:]]), factor
        )
        new_w_mlp, new_m_mlp, new_v_mlp = adam_update(
            w_mlp, m_mlp, v_mlp, jnp.stack([sum_gate, sum_up, sum_down]), factor
        )
        new_gains, new_m_gains, new_v_gains = adam_update(
            norm_gains, m_gains, v_gains, sum_gains.reshape(-1), factor
        )
        return (
            outputs, grad_in, grad_norm, new_w_qo, new_w_kv, new_w_mlp, new_gains,
            new_m_qo, new_m_kv, new_m_mlp, new_m_gains, new_v_qo, new_v_kv, new_v_mlp, new_v_gains,
        )

    return local


def solution(mesh):
    tokens = P(("dp", "mp"), None)
    weight = P(None, "dp", "mp")
    flat = P(("dp", "mp"))
    per_weight = (weight, weight, weight, flat)
    return jax.shard_map(
        build_local(mesh.shape["dp"], mesh.shape["mp"]),
        mesh=mesh,
        in_specs=(tokens, tokens, P("dp", None), P("dp", None), P()) + per_weight * 3,
        out_specs=(tokens, tokens, P()) + per_weight * 3,
        check_vma=False,
    )
```

```python
import functools
import math

import jax
import jax.numpy as jnp
from jax import lax
from jax.experimental import pallas as pl
from jax.experimental.pallas import tpu as pltpu
from jax.sharding import PartitionSpec as P

D = 2304
HEAD_WIDTH = 256
FF = 9216
NORMS = 4
QW = 2048
PARAMS = 77865984

EPSILON = 1e-06
SOFT_CAP = 50.0
ROPE_BASE = 10000.0
MASKED_SCORE = -1e30
FIRST_DECAY = 0.9
SECOND_DECAY = 0.95
LEARN_RATE = 0.04
WEIGHT_DECAY = 0.1
ADAM_EPSILON = 1e-08
CLIP_SCALE = 0.5

BF = jnp.bfloat16
F32 = jnp.float32


def code_spacing(selector):
    return jnp.where(selector == 0, 1.0, jnp.where(selector == 1, 16.0, 64.0)).astype(F32)


def quantize_values(master, step, spacing):
    half = jnp.floor(spacing * 0.5)
    inverse = jnp.where(spacing > 32.0, 1.0 / 64.0, jnp.where(spacing > 8.0, 1.0 / 16.0, 1.0))
    codes = jnp.clip(jnp.floor(master / step + 0.5), -128.0, 127.0)
    top = 128.0 * inverse
    sliced = jnp.clip(jnp.floor((codes + half) * inverse), -top, top - 1.0)
    return (sliced * spacing) * step


def quantize(master, fan_in, selector):
    step = jnp.float32(1.0 / (32.0 * math.sqrt(fan_in)))
    return quantize_values(master, step, code_spacing(selector)).astype(BF)


def inv_root(values):
    return lax.rsqrt(jnp.mean(values * values, axis=-1, keepdims=True) + EPSILON)


def rms_norm(values, norm_gain):
    return values * inv_root(values) * (1.0 + norm_gain)


def rms_back(values, norm_gain, grad):
    root = inv_root(values)
    scaled = grad * (1.0 + norm_gain)
    dot = jnp.mean(values * scaled, axis=-1, keepdims=True)
    grad_values = root * scaled - values * (root * root * root * dot)
    grad_gain = jnp.sum(values * root * grad, axis=0)
    return grad_values, grad_gain


def doc_positions(segments):
    slot_index = jnp.arange(segments.shape[0], dtype=jnp.int32)
    previous = jnp.concatenate([segments[:1] - 1, segments[:-1]])
    starts = segments != previous
    doc_begin = lax.cummax(jnp.where(starts, slot_index, 0), axis=0)
    return slot_index - doc_begin


def rotate(values, cosine, sine):
    half_dim = HEAD_WIDTH // 2
    turned = jnp.concatenate([-values[..., half_dim:], values[..., :half_dim]], -1)
    return values * cosine + turned * sine


def rotate_back(grads, cosine, sine):
    half_dim = HEAD_WIDTH // 2
    scaled = grads * sine
    turned = jnp.concatenate([scaled[..., half_dim:], -scaled[..., :half_dim]], -1)
    return grads * cosine + turned


def mm(left, right):
    return lax.dot_general(left, right, (((1,), (0,)), ((), ())), preferred_element_type=F32)


def mm_rows(left, right):
    return lax.dot_general(left, right, (((0,), (0,)), ((), ())), preferred_element_type=F32)


def mm_cols(left, right):
    return lax.dot_general(left, right, (((1,), (1,)), ((), ())), preferred_element_type=F32)


def adam_update(master, first_moment, second_moment, gradient, factor):
    clipped = gradient * factor
    new_first = FIRST_DECAY * first_moment + (1.0 - FIRST_DECAY) * clipped
    new_second = SECOND_DECAY * second_moment + (1.0 - SECOND_DECAY) * clipped * clipped
    new_master = master - LEARN_RATE * (
        new_first / (jnp.sqrt(new_second) + ADAM_EPSILON) + WEIGHT_DECAY * master
    )
    return (new_master, new_first, new_second)


MESH = pl.DeviceIdType.MESH
ANY = pl.BlockSpec(memory_space=pl.ANY)
VMEM = pl.BlockSpec(memory_space=pltpu.VMEM)
ROWS = 32


class Net:
    def __init__(self, n_dp, n_mp, send_sems, recv_sems, local_sems=None):
        self.n_dp, self.n_mp = n_dp, n_mp
        self.send_sems, self.recv_sems, self.local_sems = send_sems, recv_sems, local_sems
        self.used, self.used_local, self.open = 0, 0, []
        self.i, self.m = lax.axis_index("dp"), lax.axis_index("mp")
        self.y, self.j = self.i % 2, self.i // 2
        self.zl = self.j % 2
        self.c, self.x = self.m % 2, self.m // 2
        self.core_n = (self.i, self.m + 1 - 2 * self.c)
        self.x_n = (self.i, (self.m + 2) % 4)
        self.y_n = (self.i + 1 - 2 * self.y, self.m)
        self.z_n = (self.i + 2 - 4 * self.zl, self.m)

    def z_at(self, d):
        nj = self.n_dp // 2
        return (((self.j + d) % nj) * 2 + self.y, self.m)

    def place(self):
        return (1 - self.y) * self.j + self.y * (self.n_dp - 1 - self.j)

    def ring(self, at):
        n, nj = self.n_dp, self.n_dp // 2
        at = at % n
        late = at // nj
        return (1 - late) * 2 * at + late * (2 * (n - 1 - at) + 1)

    def meet(self, devices):
        barrier = pltpu.get_barrier_semaphore()
        for device in devices:
            pl.semaphore_signal(barrier, inc=1, device_id=device, device_id_type=MESH)
        pl.semaphore_wait(barrier, len(devices))

    def send(self, src, dst, device):
        at = self.used
        self.used += 1
        copy = pltpu.make_async_remote_copy(
            src_ref=src, dst_ref=dst, send_sem=self.send_sems.at[at], recv_sem=self.recv_sems.at[at],
            device_id=device, device_id_type=MESH,
        )
        copy.start()
        self.open.append((copy, copy.wait_send))
        return copy

    def sent(self, copy):
        copy.wait_send()
        self.open = [entry for entry in self.open if entry[0] is not copy]

    def move(self, src, dst):
        at = self.used_local
        self.used_local += 1
        copy = pltpu.make_async_copy(src, dst, self.local_sems.at[at])
        copy.start()
        return copy

    def keep(self, src, dst):
        copy = self.move(src, dst)
        self.open.append((copy, copy.wait))

    def close(self):
        for _, wait in self.open:
            wait()


def upper(count):
    return count // 16 * 8


def dma(n):
    return pltpu.SemaphoreType.DMA((n,))


def call(kernel, outs, out_specs, in_specs, scratch, cid, mb, flops=0):
    return pl.pallas_call(
        kernel,
        out_shape=outs,
        in_specs=in_specs,
        out_specs=out_specs,
        scratch_shapes=scratch,
        compiler_params=pltpu.CompilerParams(
            collective_id=cid, has_side_effects=True, vmem_limit_bytes=mb << 20
        ),
    )


def by_rows(total, body, carry=0):
    return lax.fori_loop(
        0, total // ROWS, lambda t, state: body(pl.ds(pl.multiple_of(t * ROWS, ROWS), ROWS), state), carry
    )


def everyone(n_dp, n_mp, i, m):
    flat = i * n_mp + m
    total = n_dp * n_mp
    return [(((flat + t) % total) // n_mp, (flat + t) % n_mp) for t in range(1, total)]


def gather_seq_steps(net, own, seq):
    far = net.send(own, seq.at[1], net.x_n)
    near = net.send(own, seq.at[2], net.core_n)
    net.keep(own, seq.at[0])

    def finish():
        far.wait_recv()
        both = net.send(seq.at[1], seq.at[3], net.core_n)
        near.wait_recv()
        both.wait_recv()

    return finish


def gather_pair_steps(net, own, group, split=False):
    far = net.send(own, group.at[2], net.x_n)
    zed = net.send(own, group.at[1], net.z_n)
    near = net.send(own, group.at[4], net.core_n)
    net.keep(own, group.at[0])

    def finish(between=lambda: None):
        head = pl.ds(0, D // 2) if split else pl.ds(0, D)
        rest = pl.ds(D // 2, D // 2)
        zed.wait_recv()
        both = net.send(group.at[1, :, head], group.at[3, :, head], net.x_n)
        far.wait_recv()
        if split:
            other = net.send(group.at[2, :, rest], group.at[3, :, rest], net.z_n)
        near_z = net.send(group.at[1], group.at[5], net.core_n)
        near_x = net.send(group.at[2], group.at[6], net.core_n)
        between()
        both.wait_recv()
        if split:
            other.wait_recv()
        near_both = net.send(group.at[3], group.at[7], net.core_n)
        for copy in (near, near_z, near_x, near_both):
            copy.wait_recv()

    return finish


def pair_partners(net, with_y):
    nj = net.n_dp // 2
    zs = [net.z_at(d) for d in range(1, nj)] if with_y else [net.z_n]
    return [net.core_n, net.x_n] + zs + ([net.y_n] if with_y else [])


def row_tiles(total, size, body):
    lax.fori_loop(
        0, total // size, lambda t, state: (body(pl.ds(pl.multiple_of(t * size, size), size)), state)[1], 0
    )


def project(seq, wq, wkv, cosine, sine, q, k, v):
    total = seq.shape[0]
    kv_cols = k.shape[1]
    half = HEAD_WIDTH // 2

    def body(at):
        tokens = seq[at]
        c, s = cosine[at], sine[at]

        def turn(lin, out, cols):
            for h in range(0, cols, HEAD_WIDTH):
                a, b = lin[:, h : h + half], lin[:, h + half : h + HEAD_WIDTH]
                out[at, h : h + half] = (a * c - b * s).astype(BF)
                out[at, h + half : h + HEAD_WIDTH] = (b * c + a * s).astype(BF)

        turn(mm(tokens, wq[...]), q, q.shape[1])
        lin = mm(tokens, wkv[...])
        turn(lin, k, kv_cols)
        v[at] = lin[:, kv_cols:].astype(BF)

    row_tiles(total, total // 2, body)


def allowed_tile(marks_col, marks_row, at):
    segs, slots = marks_col[at, 0:1], marks_col[at, 1:2]
    seg_row, slot_row, pad_row = marks_row[0:1], marks_row[1:2], marks_row[2:3]
    same_slot = slot_row == slots
    return (seg_row == segs) & (slot_row <= slots) & ((pad_row == 1) | same_slot)


def tile_probs(q, k, allowed, at, head, group):
    cols = slice(head * HEAD_WIDTH, (head + 1) * HEAD_WIDTH)
    kv = head // group
    kv_at = slice(kv * HEAD_WIDTH, (kv + 1) * HEAD_WIDTH)
    bent = jnp.tanh(mm_cols(q[at, cols], k[:, kv_at]) * (HEAD_WIDTH**-0.5 / SOFT_CAP))
    raised = jnp.where(allowed, jnp.exp(SOFT_CAP * bent), 0.0)
    return bent, raised * (1.0 / jnp.sum(raised, axis=-1, keepdims=True))


def attend(q, k, v, marks_col, marks_row, mixed):
    total = q.shape[0]
    heads, group = q.shape[1] // HEAD_WIDTH, q.shape[1] // k.shape[1]

    def body(at):
        allowed = allowed_tile(marks_col, marks_row, at)
        for head in range(heads):
            _, probs = tile_probs(q, k, allowed, at, head, group)
            kv = head // group
            kv_at = slice(kv * HEAD_WIDTH, (kv + 1) * HEAD_WIDTH)
            mixed[at, head * HEAD_WIDTH : (head + 1) * HEAD_WIDTH] = mm(
                probs.astype(BF), v[:, kv_at]
            ).astype(BF)

    row_tiles(total, 128, body)


def out_project(mixed, wo, part):
    blocks, rows, _ = part.shape
    wide = D // 3
    for pair in range(blocks // 2 - 1, -1, -1):
        for n in range(0, D, wide):
            got = mm_cols(mixed[pair * 2 * rows : (pair + 1) * 2 * rows], wo[n : n + wide]).astype(BF)
            part[pair * 2, :, n : n + wide] = got[:rows]
            part[pair * 2 + 1, :, n : n + wide] = got[rows:]


def chunks(wrows):
    if wrows % 48 == 0:
        return tuple((n * wrows // 3, wrows // 3) for n in range(3))
    return ((0, upper(wrows)), (upper(wrows), wrows - upper(wrows)))


def two_parts(wrows):
    return ((0, upper(wrows)), (upper(wrows), wrows - upper(wrows)))


class Gather:
    def __init__(self, net, pieces):
        self.net, self.pieces, self.nj = net, pieces, net.n_dp // 2
        self.flight, self.relays, self.own = {}, {}, {}

    def out(self, n):
        net = self.net
        source, place, parity = self.pieces[n]
        self.own[n] = net.move(source(net.zl), place(net.i))
        self.relays[n] = [net.send(source(net.zl), place(net.i), net.y_n)]
        for d in range(1, self.nj):
            self.flight[n, d] = net.send(source((net.j + d) % self.nj % 2), place(net.i), net.z_at(d))

    def on(self, n):
        net = self.net
        _, place, _ = self.pieces[n]
        for d in range(1, self.nj):
            self.flight[n, d].wait_recv()
            at = ((net.j + self.nj - d) % self.nj) * 2 + net.y
            self.relays[n].append(net.send(place(at), place(at), net.y_n))

    def done(self, n):
        self.own.pop(n).wait()
        for copy in self.relays.pop(n):
            copy.wait_recv()


def all_of_dp(net):
    return [net.x_n, net.core_n] + [((net.i + t) % net.n_dp, net.m) for t in range(1, net.n_dp)]


def open_kernel(
    n_dp, n_mp, low_q, low_kv, low_o, w_mlp, width_mlp, cosine, sine, marks_col, marks_row, inputs, own_gains,
    q, k, v, mixed, att, hid, gains, group, full0, full1, full2, out_q, out_kv, out_o, out_seq,
    wq, wkv, wo, seq, part, r1, r2, own, got_gains, masters, lows, ss, rs, ls,
):
    net = Net(n_dp, n_mp, ss, rs, ls)
    p = net.place()
    right = (net.ring(p + 1), net.m)
    left = (net.ring(p + n_dp - 1), net.m)
    rows = inputs.shape[0]
    wrows, width = full0.shape[1:]
    others = everyone(n_dp, n_mp, net.i, net.m)
    net.meet(others)
    flat = net.i * n_mp + net.m
    loads = [net.move(w_mlp.at[n], masters.at[n]) for n in range(3)]

    def block(ref, at):
        return ref.at[pl.ds(pl.multiple_of(at * wrows, 8), wrows)]

    def lot(n):
        return seq.at[pl.ds(n * rows, rows)]

    def piece(ref, at, part):
        first, count = part
        return ref.at[pl.ds(pl.multiple_of(at * wrows + first, 8), count)]

    parts = two_parts(wrows)
    flight = {}
    for cut in parts:
        for lane, (ref, low, device) in enumerate(((wq, low_q, right), (wkv, low_kv, left))):
            flight[cut, lane] = net.send(low.at[pl.ds(*cut)], piece(ref, net.i, cut), device)
    spread = [net.send(own_gains, got_gains.at[flat], device) for device in others]
    net.move(own_gains, got_gains.at[flat]).wait()
    for copy in spread:
        copy.wait_recv()
    per_norm = n_dp * n_mp // NORMS
    for n in range(NORMS):
        gains[n : n + 1] = jnp.concatenate([got_gains[n * per_norm + t] for t in range(per_norm)], 1)
    g0 = 1.0 + gains[0:1]

    def norm_rows(at, state):
        own[at] = (inputs[at] * inv_root(inputs[at]) * g0).astype(BF)
        return state

    by_rows(rows, norm_rows)
    far = net.send(own, lot(1), net.x_n)
    near = net.send(own, lot(2), net.core_n)

    def quantize_part(n):
        loads[n].wait()
        spacing = width_mlp[...]
        step = jnp.float32(1.0 / (32.0 * math.sqrt(FF if n == 2 else D)))

        def body(at, state, count):
            lows[n, at] = quantize_values(masters[n, at], step, spacing).astype(BF)
            return state

        in_steps(wrows, body)

    own_parts = [net.move(own, lot(0)), net.move(low_q, block(wq, net.i)), net.move(low_kv, block(wkv, net.i))]
    half = lambda which: pl.ds(pl.multiple_of(which * width, width), width)
    pieces = [(lambda which: low_o, lambda at: block(wo, at), 1)]

    def add_piece(ref, full, first, count):
        rows_at = pl.ds(first, count)
        pieces.append((lambda which: ref.at[rows_at, half(which)], lambda at: full.at[at, rows_at], 2))

    for ref, full in ((lows.at[0], full0), (lows.at[1], full1), (lows.at[2], full2)):
        for first, count in chunks(wrows):
            add_piece(ref, full, first, count)
    weights = Gather(net, pieces)
    for hop in range(1, n_dp):
        from_right, from_left = net.ring(p + n_dp - hop), net.ring(p + hop)
        for cut in parts:
            for lane, (ref, at, device) in enumerate(((wq, from_right, right), (wkv, from_left, left))):
                flight[cut, lane].wait_recv()
                if hop < n_dp - 1:
                    flight[cut, lane] = net.send(piece(ref, at, cut), piece(ref, at, cut), device)
        if hop == n_dp // 2:
            far.wait_recv()
            both = net.send(lot(1), lot(3), net.core_n)
        if hop in (1, 2, 3):
            quantize_part(hop - 1)
        if hop == n_dp - 2:
            weights.out(0)
    weights.out(1)
    weights.out(2)
    near.wait_recv()
    both.wait_recv()
    for copy in own_parts:
        copy.wait()
    net.sent(far)
    net.sent(near)
    for ref, result in ((wq, out_q), (wkv, out_kv), (seq, out_seq)):
        net.keep(ref, result)
    project(seq, wq, wkv, cosine, sine, q, k, v)
    attend(q, k, v, marks_col, marks_row, mixed)
    def step(n):
        if n < len(pieces):
            weights.on(n)
            if n + 3 < len(pieces):
                weights.out(n + 3)

    step(0)
    weights.done(0)
    net.keep(wo, out_o)
    out_project(mixed, wo, part)
    c1 = net.send(part.at[3], r1.at[1], net.core_n)
    c0 = net.send(part.at[2], r1.at[0], net.core_n)
    c1.wait_recv()

    def first_rows(at, state):
        part[1, at] = (part[1, at].astype(F32) + r1[1, at].astype(F32)).astype(BF)
        return state

    by_rows(rows, first_rows)
    x = net.send(part.at[1], r2, net.x_n)
    c0.wait_recv()
    step(1)
    x.wait_recv()
    g1, g2 = 1.0 + gains[1:2], 1.0 + gains[2:3]

    def second(at, state):
        total = part[0, at].astype(F32) + r1[0, at].astype(F32) + r2[at].astype(F32)
        att[at] = total
        hidden = inputs[at] + total * inv_root(total) * g1
        hid[at] = hidden
        own[at] = (hidden * inv_root(hidden) * g2).astype(BF)
        return state

    by_rows(rows, second)
    finish = gather_pair_steps(net, own, group)
    step(2)
    step(3)
    finish(lambda: (step(4), step(5)))
    for n in range(6, len(pieces)):
        step(n)
    for n in range(1, len(pieces)):
        weights.done(n)
    net.close()


def open_layer(n_dp, n_mp, low_q, low_kv, low_o, w_mlp, width_mlp, cosine, sine, marks_col, marks_row, inputs, gains):
    rows = inputs.shape[0]
    nj = n_dp // 2
    total_devices = n_dp * n_mp
    count = 24 + 4 * n_dp + 20 * nj + total_devices
    block = (rows, D)
    wrows, width = w_mlp.shape[1], w_mlp.shape[2] // 2
    cols, kv_cols = low_q.shape[1], low_kv.shape[1] // 2
    vm = lambda *shape: pltpu.VMEM(shape, BF)
    bf = lambda *shape: jax.ShapeDtypeStruct(shape, BF)
    total = 4 * rows
    f32 = jax.ShapeDtypeStruct(block, F32)
    full = bf(n_dp, wrows, width)
    return call(
        functools.partial(open_kernel, n_dp, n_mp),
        [
            bf(total, cols), bf(total, kv_cols), bf(total, kv_cols), bf(total, cols), f32, f32,
            jax.ShapeDtypeStruct((NORMS, D), F32),
            bf(8, *block), full, full, full, bf(D, cols), bf(D, 2 * kv_cols), bf(D, cols), bf(total, D),
        ],
        [VMEM] * 7 + [ANY] * 8, [ANY] * 4 + [VMEM] * 7,
        [
            vm(D, cols), vm(D, 2 * kv_cols), vm(D, cols), vm(total, D), vm(4, *block), vm(2, *block), vm(*block),
            vm(*block), pltpu.VMEM((total_devices,) + gains.shape, F32), pltpu.VMEM(w_mlp.shape, F32),
            vm(*w_mlp.shape), dma(count), dma(count), dma(32),
        ],
        2, 60,
    )(low_q, low_kv, low_o, w_mlp, width_mlp, cosine, sine, marks_col, marks_row, inputs, gains)


def reduce_pair_steps(net, near, far, r1, s2, r2, s3, r3, rows, loaded, split=False, hooks=()):
    cores = {k: net.send(far.at[k], r1.at[k], net.core_n) for k in (3, 2, 1, 0)}
    plan = [(pl.ds(0, D // 2 if split else D), (3, 2), net.x_n, 1, net.z_n)]
    if split:
        plan.append((pl.ds(D // 2, D // 2), (3, 1), net.z_n, 2, net.x_n))
    firsts = {}
    loaded.wait()
    for k in (3, 2, 1) if split else (3, 2):
        cores[k].wait_recv()
        for part, (cols, blocks, device, _, _) in enumerate(plan):
            if k not in blocks:
                continue
            at_block = blocks.index(k)

            def add(at, state, k=k, cols=cols, at_block=at_block):
                s2[at_block, at, cols] = (near[k, at, cols].astype(F32) + r1[k, at, cols].astype(F32)).astype(BF)
                return state

            by_rows(rows, add)
            firsts[part, at_block] = net.send(s2.at[at_block, :, cols], r2.at[at_block, :, cols], device)
    for k in (0,) if split else (1, 0):
        cores[k].wait_recv()
    last = []
    if hooks:
        hooks[0]()
    for part, (cols, blocks, _, second, device) in enumerate(plan):
        firsts[part, 0].wait_recv()

        def add(at, state, cols=cols, second=second):
            s3[at, cols] = (
                near[second, at, cols].astype(F32) + r1[second, at, cols].astype(F32) + r2[0, at, cols].astype(F32)
            ).astype(BF)
            return state

        by_rows(rows, add)
        last.append(net.send(s3.at[:, cols], r3.at[:, cols], device))
    if hooks:
        hooks[1]()
    for part in range(len(plan)):
        firsts[part, 1].wait_recv()
    return last


def pair_sum(near, r1, r2, r3, at):
    return near[0, at].astype(F32) + r1[0, at].astype(F32) + r2[1, at].astype(F32) + r3[at].astype(F32)


def pair_scratch(rows):
    block = (rows, D)
    return [
        pltpu.VMEM((4,) + block, BF),
        pltpu.VMEM((4,) + block, BF), pltpu.VMEM((2,) + block, BF), pltpu.VMEM((2,) + block, BF),
        pltpu.VMEM(block, BF), pltpu.VMEM(block, BF), pltpu.VMEM(block, BF),
    ]


def rms_back_rows(values, gain, grad):
    root = inv_root(values)
    scaled = grad * gain
    dot = jnp.mean(values * scaled, axis=-1, keepdims=True)
    return root * scaled - values * (root * root * root * dot), jnp.sum(values * root * grad, axis=0, keepdims=True)


def turn_kernel(
    n_dp, n_mp, part, hid, gains, out_grad, live, outputs, dgain, group,
    near, r1, s2, r2, s3, r3, own, ss, rs, ls,
):
    net = Net(n_dp, n_mp, ss, rs, ls)
    net.meet(pair_partners(net, False))
    rows = hid.shape[0]
    far = part.at[pl.ds(4, 4)]
    loaded = net.move(part.at[pl.ds(0, 4)], near)
    for copy in reduce_pair_steps(net, near, far, r1, s2, r2, s3, r3, rows, loaded, True):
        copy.wait_recv()
    g3 = 1.0 + gains[3:4]

    def last(at, state):
        total = pair_sum(near, r1, r2, r3, at)
        outputs[at] = hid[at] + total * inv_root(total) * g3
        grad, dg = rms_back_rows(total, g3, out_grad[at] * live[at])
        own[at] = grad.astype(BF)
        return state + dg

    dgain[...] = by_rows(rows, last, jnp.zeros((1, D), F32))
    gather_pair_steps(net, own, group, True)()
    net.close()


def turn(n_dp, n_mp, part, hid, gains, out_grad, live):
    rows = hid.shape[0]
    block = (rows, D)
    return call(
        functools.partial(turn_kernel, n_dp, n_mp),
        [jax.ShapeDtypeStruct(block, F32), jax.ShapeDtypeStruct((1, D), F32), jax.ShapeDtypeStruct((8,) + block, BF)],
        [VMEM, VMEM, ANY], [ANY, VMEM, VMEM, VMEM, VMEM],
        pair_scratch(rows) + [dma(32), dma(32), dma(4)], 4, 48,
    )(part, hid, gains, out_grad, live)


def in_steps(count, body, carry=0, first=0):
    step = 16 if count % 16 == 0 else 8
    return lax.fori_loop(
        0, count // step,
        lambda t, state: body(pl.ds(pl.multiple_of(first + t * step, 8), step), state, step), carry,
    )


class Scatter:
    def __init__(self, net, grads, stay, came, last):
        self.net, self.grads, self.stay, self.came, self.last = net, grads, stay, came, last
        self.nj, self.wrows, self.width = came.shape
        self.turns = sorted(range(1, self.nj), key=lambda d: abs(d - self.nj // 2)) + [0]
        self.ys, self.moves, self.zs = {}, {}, {}

    def along_y(self, turns=None):
        net = self.net
        for d in self.turns if turns is None else turns:
            at = (net.j + d) % self.nj
            self.ys[d] = net.send(self.grads.at[at, 1 - net.y], self.came.at[d], net.y_n)
            self.moves[d] = net.move(self.grads.at[at, net.y], self.stay.at[d])

    def along_z(self, turns):
        for d in turns:
            self.ys[d].wait_recv()
            self.moves[d].wait()

            def add(at, state, step, d=d):
                self.stay[d, at] = (self.stay[d, at].astype(F32) + self.came[d, at].astype(F32)).astype(BF)
                return state

            in_steps(self.wrows, add)
            if d:
                self.zs[d] = self.net.send(self.stay.at[d], self.last.at[d - 1], self.net.z_at(d))

    def landed(self):
        for d in range(1, self.nj):
            self.zs[d].wait_recv()

    def halves(self, total, sums):
        self.landed()

        def collect(at, state, step):
            both = [self.stay[0, at].astype(F32), jnp.zeros((step, self.width), F32)]
            for d in range(1, self.nj):
                both[d % 2] = both[d % 2] + self.last[d - 1, at].astype(F32)
            for parity in range(2):
                total[parity, at] = both[parity]
            return state

        in_steps(self.wrows, collect)
        for parity in range(2):
            half = (self.net.zl + parity) % 2
            self.net.keep(total.at[parity], sums.at[:, pl.ds(pl.multiple_of(half * self.width, self.width), self.width)])

    def whole(self, out):
        self.landed()

        def collect(at, state, step):
            value = self.stay[0, at].astype(F32)
            for d in range(1, self.nj):
                value = value + self.last[d - 1, at].astype(F32)
            out[at] = value
            return state

        in_steps(self.wrows, collect)


def scatter_scratch(nj, wrows, width):
    return [
        pltpu.VMEM((nj, wrows, width), BF), pltpu.VMEM((nj, wrows, width), BF),
        pltpu.VMEM((nj - 1, wrows, width), BF),
    ]


def back_kernel(
    n_dp, n_mp, part, hid, att, gains, out_grad, live, grads, grads_up,
    ghid, dg1, dg2, seq, sums, sums_up,
    near, r1, s2, r2, s3, r3, own, stay, came, last, ustay, ucame, ulast, total, ss, rs, ls,
):
    net = Net(n_dp, n_mp, ss, rs, ls)
    nj = n_dp // 2
    net.meet(pair_partners(net, True))
    rows = hid.shape[0]
    far = part.at[pl.ds(4, 4)]
    loaded = net.move(part.at[pl.ds(0, 4)], near)
    weight = Scatter(net, grads, stay, came, last)
    weight_up = Scatter(net, grads_up, ustay, ucame, ulast)
    weight.along_y()
    last_sums = reduce_pair_steps(
        net, near, far, r1, s2, r2, s3, r3, rows, loaded, False,
        (lambda: weight.along_z(weight.turns[:1]), lambda: weight.along_z(weight.turns[1:2])),
    )
    weight_up.along_y()
    for copy in last_sums:
        copy.wait_recv()
    g1, g2 = 1.0 + gains[1:2], 1.0 + gains[2:3]

    def rows_back(at, state):
        grad = pair_sum(near, r1, r2, r3, at)
        part_hid, d2 = rms_back_rows(hid[at], g2, grad)
        grad_hidden = out_grad[at] * live[at] + part_hid
        ghid[at] = grad_hidden
        grad_att, d1 = rms_back_rows(att[at], g1, grad_hidden)
        own[at] = grad_att.astype(BF)
        return state[0] + d1, state[1] + d2

    zero = jnp.zeros((1, D), F32)
    done1, done2 = by_rows(rows, rows_back, (zero, zero))
    dg1[...] = done1
    dg2[...] = done2
    finish = gather_seq_steps(net, own, seq)
    weight.along_z(weight.turns[2:])
    weight_up.along_z(weight_up.turns[:1])
    finish()
    weight_up.along_z(weight_up.turns[1:2])
    weight.halves(total.at[0], sums)
    weight_up.along_z(weight_up.turns[2:])
    weight_up.halves(total.at[1], sums_up)
    net.close()


def back(n_dp, n_mp, part, hid, att, gains, out_grad, live, grads, grads_up):
    rows = hid.shape[0]
    block = (rows, D)
    nj = n_dp // 2
    _, _, wrows, width = grads.shape
    count = 24 + 6 * nj
    return call(
        functools.partial(back_kernel, n_dp, n_mp),
        [
            jax.ShapeDtypeStruct(block, F32), jax.ShapeDtypeStruct((1, D), F32), jax.ShapeDtypeStruct((1, D), F32),
            jax.ShapeDtypeStruct((4,) + block, BF), jax.ShapeDtypeStruct((wrows, 2 * width), F32),
            jax.ShapeDtypeStruct((wrows, 2 * width), F32),
        ],
        [VMEM, VMEM, VMEM, ANY, ANY, ANY], [ANY, VMEM, VMEM, VMEM, VMEM, VMEM, ANY, ANY],
        pair_scratch(rows) + scatter_scratch(nj, wrows, width) * 2
        + [pltpu.VMEM((2, 2, wrows, width), F32), dma(count), dma(count), dma(12 + 2 * nj)],
        5, 60,
    )(part, hid, att, gains, out_grad, live, grads, grads_up)


def attend_back(q, k, v, gm, marks_col, marks_row, cosine, sine, dq, dk, dv, tiles):
    total = q.shape[0]
    heads, group = q.shape[1] // HEAD_WIDTH, q.shape[1] // k.shape[1]
    size = total // 4
    half = HEAD_WIDTH // 2
    scale = HEAD_WIDTH**-0.5

    def body(t, state):
        at = pl.ds(pl.multiple_of(t * size, size), size)
        allowed = allowed_tile(marks_col, marks_row, at)
        c, s = cosine[at], sine[at]
        for head in range(heads):
            kv = head // group
            cols = slice(head * HEAD_WIDTH, (head + 1) * HEAD_WIDTH)
            kv_at = slice(kv * HEAD_WIDTH, (kv + 1) * HEAD_WIDTH)
            bent, probs = tile_probs(q, k, allowed, at, head, group)
            grad = gm[at, cols]
            dv[:, kv_at] += mm_rows(probs.astype(BF), grad)
            gp = mm_cols(grad, v[:, kv_at])
            inner = jnp.sum(probs * gp, axis=-1, keepdims=True)
            ds = (probs * (gp - inner) * (1.0 - bent * bent)).astype(BF)
            dk[:, kv_at] += mm_rows(ds, q[at, cols]) * scale
            turned = mm(ds, k[:, kv_at]) * scale
            a, b = turned[:, :half], turned[:, half:]
            first = head * HEAD_WIDTH
            dq[at, first : first + half] = (a * c + b * s).astype(BF)
            dq[at, first + half : first + HEAD_WIDTH] = (b * c - a * s).astype(BF)
        return state

    lax.fori_loop(tiles[0], tiles[1], body, 0)


def weight_grad(tokens, grads, out):
    wide = D // 3
    for n in range(0, D, wide):
        out[n : n + wide] = mm_rows(tokens[:, n : n + wide], grads[...]).astype(BF)


def close_kernel(
    n_dp, n_mp, seq_grad, seq_normed, q, k, v, mixed, wo, wq, wkv, cosine, sine, marks_col, marks_row,
    inputs, gains, ghid,
    gin, dg0, sum_q, sum_kv, sum_o,
    tokens, normed, wa, gm, dq, dk, dv, dkv, go, gq, gkv, got_q, got_kv, r1, r2,
    ostay, ocame, olast, ss, rs, ls,
):
    net = Net(n_dp, n_mp, ss, rs, ls)
    p = net.place()
    right = (net.ring(p + 1), net.m)
    left = (net.ring(p + n_dp - 1), net.m)
    nj = n_dp // 2
    rows = inputs.shape[0]
    seq_len, wrows = tokens.shape[0], sum_q.shape[0]
    net.meet(all_of_dp(net))
    token_load = net.move(seq_grad, tokens)
    wa_load = net.move(wo, wa)
    normed_load = net.move(seq_normed, normed)
    ghid_load = net.move(ghid, gin)
    dk[...] = jnp.zeros_like(dk)
    dv[...] = jnp.zeros_like(dv)
    token_load.wait()
    wa_load.wait()

    def mix(at):
        gm[at] = mm(tokens[at], wa[...]).astype(BF)

    row_tiles(seq_len, seq_len // 2, mix)
    wa_load = net.move(wq, wa)
    weight_grad(tokens, mixed, go.reshape(D, go.shape[-1]))
    out = Scatter(net, go, ostay, ocame, olast)
    out.along_y()
    attend_back(q, k, v, gm, marks_col, marks_row, cosine, sine, dq, dk, dv, (0, 2))
    out.along_z(out.turns[:1])
    attend_back(q, k, v, gm, marks_col, marks_row, cosine, sine, dq, dk, dv, (2, 4))
    out.along_z(out.turns[1:])
    kv_cols = k.shape[1]
    half = HEAD_WIDTH // 2

    def turn_keys(at):
        c, s = cosine[at], sine[at]
        for h in range(0, kv_cols, HEAD_WIDTH):
            a, b = dk[at, h : h + half], dk[at, h + half : h + HEAD_WIDTH]
            dkv[at, h : h + half] = (a * c + b * s).astype(BF)
            dkv[at, h + half : h + HEAD_WIDTH] = (b * c - a * s).astype(BF)
        dkv[at, kv_cols:] = dv[at].astype(BF)

    row_tiles(seq_len, 128, turn_keys)
    normed_load.wait()
    weight_grad(normed, dq, gq)
    weight_grad(normed, dkv, gkv)

    def block(at, part):
        return pl.ds(pl.multiple_of(net.ring(p + 2 * n_dp + at) * wrows + part[0], 8), part[1])

    lanes = ((gq, got_q, sum_q, right, -1), (gkv, got_kv, sum_kv, left, 1))
    parts = two_parts(wrows)
    flight = {}
    for part in parts:
        for lane, (terms, got, _, device, way) in enumerate(lanes):
            flight[lane, part] = net.send(terms.at[block(way, part)], got.at[0, pl.ds(*part)], device)

    def hop(n):
        end = n == n_dp - 1
        for part in parts:
            for lane, (terms, got, result, device, way) in enumerate(lanes):
                flight[lane, part].wait_recv()
                first = net.ring(p + 2 * n_dp + way * (1 + n)) * wrows

                def add(here, state, step, first=first, terms=terms, got=got, result=result):
                    at = pl.ds(pl.multiple_of(first + here.start, 8), step)
                    value = got[n - 1, here].astype(F32) + terms[at].astype(F32)
                    if end:
                        result[here] = value
                    else:
                        terms[at] = value.astype(BF)
                    return state

                in_steps(part[1], add, 0, part[0])
                if not end:
                    flight[lane, part] = net.send(
                        terms.at[block(way * (1 + n), part)], got.at[n, pl.ds(*part)], device
                    )

    wa_load.wait()
    wide = D // 3
    copies = []
    for pair in (1, 0):
        at = pl.ds(pair * 2 * rows, 2 * rows)
        for n in range(0, D, wide):
            tokens[at, n : n + wide] = (
                mm_cols(dq[at], wa[n : n + wide]) + mm_cols(dkv[at], wkv[n : n + wide])
            ).astype(BF)
        if pair:
            c1 = net.send(tokens.at[pl.ds(3 * rows, rows)], r1.at[1], net.core_n)
            c0 = net.send(tokens.at[pl.ds(2 * rows, rows)], r1.at[0], net.core_n)
            hop(1)
    c1.wait_recv()

    def add_far(at, state):
        here = pl.ds(pl.multiple_of(rows + at.start, ROWS), ROWS)
        tokens[here] = (tokens[here].astype(F32) + r1[1, at].astype(F32)).astype(BF)
        return state

    by_rows(rows, add_far)
    x = net.send(tokens.at[pl.ds(rows, rows)], r2, net.x_n)
    c0.wait_recv()
    hop(2)
    hop(3)
    x.wait_recv()
    ghid_load.wait()
    g0 = 1.0 + gains[0:1]

    def rows_in(at, state):
        grad = tokens[at].astype(F32) + r1[0, at].astype(F32) + r2[at].astype(F32)
        part, d0 = rms_back_rows(inputs[at], g0, grad)
        gin[at] = gin[at] + part
        return state + d0

    dg0[...] = by_rows(rows, rows_in, jnp.zeros((1, D), F32))
    for n in range(4, n_dp - 1):
        hop(n)
    out.whole(sum_o)
    hop(n_dp - 1)
    net.close()


def close(n_dp, n_mp, seq_grad, seq_normed, q, k, v, mixed, wo, wq, wkv, cosine, sine, marks_col, marks_row,
          inputs, gains, ghid):
    rows = inputs.shape[0]
    nj = n_dp // 2
    wrows = D // n_dp
    cols, kv_cols = q.shape[1], k.shape[1]
    seq_len = q.shape[0]
    count = 16 + 6 * nj + 4 * n_dp
    vm = lambda *shape: pltpu.VMEM(shape, BF)
    small = jax.ShapeDtypeStruct((wrows, cols), F32)
    return call(
        functools.partial(close_kernel, n_dp, n_mp),
        [
            jax.ShapeDtypeStruct((rows, D), F32), jax.ShapeDtypeStruct((1, D), F32), small,
            jax.ShapeDtypeStruct((wrows, 2 * kv_cols), F32), small,
        ],
        [VMEM] * 5,
        [ANY, ANY] + [VMEM] * 4 + [ANY, ANY] + [VMEM] * 7 + [ANY],
        [
            vm(seq_len, D), vm(seq_len, D), vm(D, cols), vm(seq_len, cols), vm(seq_len, cols),
            pltpu.VMEM((seq_len, kv_cols), F32), pltpu.VMEM((seq_len, kv_cols), F32), vm(seq_len, 2 * kv_cols),
            vm(nj, 2, wrows, cols), vm(D, cols), vm(D, 2 * kv_cols),
            vm(n_dp - 1, wrows, cols), vm(n_dp - 1, wrows, 2 * kv_cols), vm(2, rows, D), vm(rows, D),
        ]
        + scatter_scratch(nj, wrows, cols) + [dma(count), dma(count), dma(10 + 2 * nj)],
        6, 60,
    )(seq_grad, seq_normed, q, k, v, mixed, wo, wq, wkv, cosine, sine, marks_col, marks_row,
      inputs, gains, ghid)


def plain(kernel, grid, outs, out_specs, in_specs, mb, flops):
    return pl.pallas_call(
        kernel,
        out_shape=outs,
        grid=grid,
        in_specs=in_specs,
        out_specs=out_specs,
        compiler_params=pltpu.CompilerParams(
            dimension_semantics=("arbitrary",) * len(grid), vmem_limit_bytes=mb << 20
        ),
        cost_estimate=pl.CostEstimate(flops=flops, bytes_accessed=40 << 20, transcendentals=0),
    )


def whole(shape):
    return pl.BlockSpec(shape, lambda t: (0,) * len(shape), pipeline_mode=pl.Buffered(1))


def tile(rows, cols):
    return pl.BlockSpec((None, rows, cols), lambda t: (t, 0, 0))


GELU = math.sqrt(2.0 / math.pi)


def mlp_kernel(x, wg, wu, wd, gate, up, act, part):
    g = mm(x[...], wg[...])
    u = mm(x[...], wu[...])
    gate[...] = g
    up[...] = u
    bend = jnp.tanh(GELU * (g + 0.044715 * (g * g * g)))
    a = (0.5 * g * (1.0 + bend) * u).astype(BF)
    act[...] = a
    part[...] = mm_cols(a, wd[...]).astype(BF)


def mlp(x, wg, wu, wd):
    blocks, rows, _ = x.shape
    width = wg.shape[1]
    shape = (blocks, rows, width)
    return plain(
        mlp_kernel, (blocks,),
        [
            jax.ShapeDtypeStruct(shape, F32), jax.ShapeDtypeStruct(shape, F32), jax.ShapeDtypeStruct(shape, BF),
            jax.ShapeDtypeStruct((blocks, rows, D), BF),
        ],
        [tile(rows, width)] * 3 + [tile(rows, D)], [tile(rows, D)] + [whole(wg.shape)] * 3, 56,
        6 * blocks * rows * D * width,
    )(x, wg, wu, wd)


def down_back_kernel(grad, gate, up, wg, wu, wd, dgate, dup, part):
    ga = mm(grad[...], wd[...])
    g = gate[...]
    square = g * g
    bend = jnp.tanh(GELU * (g + 0.044715 * (square * g)))
    halved = 0.5 * (1.0 + bend)
    slope = halved + (0.5 * GELU) * g * (1.0 - bend * bend) * (1.0 + (3.0 * 0.044715) * square)
    dg = (ga * up[...] * slope).astype(BF)
    du = (ga * (g * halved)).astype(BF)
    dgate[...] = dg
    dup[...] = du
    part[...] = (mm_cols(dg, wg[...]) + mm_cols(du, wu[...])).astype(BF)


def mlp_back(grad, gate, up, wg, wu, wd):
    blocks, rows, _ = grad.shape
    width = wg.shape[1]
    shape = (blocks, rows, width)
    return plain(
        down_back_kernel, (blocks,),
        [jax.ShapeDtypeStruct(shape, BF), jax.ShapeDtypeStruct(shape, BF), jax.ShapeDtypeStruct((blocks, rows, D), BF)],
        [tile(rows, width), tile(rows, width), tile(rows, D)],
        [tile(rows, D), tile(rows, width), tile(rows, width)] + [whole(wg.shape)] * 3, 56,
        6 * blocks * rows * D * width,
    )(grad, gate, up, wg, wu, wd)


def norm_kernel(
    n_dp, n_mp, terms, g_gate, g_up, g_down, g_q, g_o, g_kv, gain_sum, norm, *refs,
):
    grads, (got, sgot, mine, ss, rs, ls) = refs[:6], refs[6:]
    net = Net(n_dp, n_mp, ss, rs, ls)
    others = everyone(n_dp, n_mp, net.i, net.m)
    loads = [net.move(src, dst) for src, dst in zip((g_gate, g_up, g_down, g_q, g_o, g_kv), grads)]
    net.meet(others)
    flat = net.i * n_mp + net.m
    copies = [net.send(terms.at[dp * n_mp + mp], got.at[flat], (dp, mp)) for dp, mp in others]
    own = net.move(terms.at[flat], got.at[flat])
    square = jnp.zeros((8, 128), F32)
    for load, grad in zip(loads, grads):
        load.wait()
        rows, cols = grad.shape

        def add(t, state, grad=grad, cols=cols):
            value = grad[pl.ds(pl.multiple_of(t * 8, 8), 8)]
            value = value * value
            for n in range(0, cols, 128):
                state = state + value[:, n : n + 128]
            return state

        square = lax.fori_loop(0, rows // 8, add, square)
    own.wait()
    for copy in copies:
        copy.wait_recv()
    gain = lax.fori_loop(0, n_dp * n_mp, lambda t, s: s + got[t], jnp.zeros(got.shape[1:], F32))
    gain_sum[...] = gain
    mine[...] = square + jnp.sum(gain * gain) * (1.0 / 1024.0)
    copies = [net.send(mine, sgot.at[flat], device) for device in others]
    own = net.move(mine, sgot.at[flat])
    own.wait()
    for copy in copies:
        copy.wait_recv()
    total = lax.fori_loop(0, n_dp * n_mp, lambda t, s: s + sgot[t], jnp.zeros((8, 128), F32))
    norm[...] = jnp.broadcast_to(jnp.sqrt(jnp.sum(total, axis=(0, 1), keepdims=True)), (8, 128))
    net.close()


def norm_all(n_dp, n_mp, terms, grads):
    total = n_dp * n_mp
    shape = terms.shape[1:]
    return call(
        functools.partial(norm_kernel, n_dp, n_mp),
        [jax.ShapeDtypeStruct(shape, F32), jax.ShapeDtypeStruct((8, 128), F32)],
        [VMEM] * 2, [VMEM] + [ANY] * 6,
        [pltpu.VMEM(a.shape, F32) for a in grads]
        + [
            pltpu.VMEM((total,) + shape, F32), pltpu.VMEM((total, 8, 128), F32), pltpu.VMEM((8, 128), F32),
            dma(2 * total), dma(2 * total), dma(8),
        ],
        7, 32,
    )(terms, *grads)


def adam_kernel(norm, gain_grad, gw, gm, gv, g_gate, g_up, g_down, g_q, g_o, g_kv, *refs):
    ins, gain_outs, outs = refs[:9], refs[9:12], refs[12:]
    factor = jnp.minimum(1.0, CLIP_SCALE * math.sqrt(PARAMS) / norm[0:1, 0:1])
    news = adam_update(gw[...], gm[...], gv[...], gain_grad[...], factor)
    for out, new in zip(gain_outs, news):
        out[...] = new
    kv_cols = ins[6].shape[2]
    grads = (
        (lambda: g_gate[...], lambda: g_up[...], lambda: g_down[...]),
        (lambda: g_q[...], lambda: g_o[...]),
        (lambda: g_kv[:, :kv_cols], lambda: g_kv[:, kv_cols:]),
    )
    for n, group in enumerate(grads):
        w, m, v = ins[3 * n : 3 * n + 3]
        for k, grad in enumerate(group):
            news = adam_update(w[k], m[k], v[k], grad(), factor)
            for out, new in zip(outs[3 * n : 3 * n + 3], news):
                out[k] = new


def adam_all(norm, gain_grad, gains, grads, states):
    wrows = grads[0].shape[0]
    step = 16 if wrows % 16 == 0 else 8
    like = lambda a: jax.ShapeDtypeStruct(a.shape, F32)
    fixed = lambda a: pl.BlockSpec(a.shape, lambda t: (0, 0))
    flat = lambda a: pl.BlockSpec((step, a.shape[1]), lambda t: (t, 0))
    deep = lambda a: pl.BlockSpec((a.shape[0], step, a.shape[2]), lambda t: (0, t, 0))
    return plain(
        adam_kernel, (wrows // step,), [like(a) for a in gains] + [like(a) for a in states],
        [fixed(a) for a in gains] + [deep(a) for a in states],
        [fixed(a) for a in (norm, gain_grad) + tuple(gains)] + [flat(a) for a in grads] + [deep(a) for a in states],
        32, 100,
    )(norm, gain_grad, *gains, *grads, *states)


def build_local(n_dp, n_mp):
    nj = n_dp // 2

    def y_swap(value):
        return lax.ppermute(value, "dp", [(k, k ^ 1) for k in range(n_dp)])

    def z_shift(value, d):
        pairs = [(a * 2 + b, ((a + d) % nj) * 2 + b) for a in range(nj) for b in range(2)]
        return lax.ppermute(value, "dp", pairs)

    def scatter_first(grad, y):
        away = lax.dynamic_index_in_dim(grad, 1 - y, 1, keepdims=False)
        stay = lax.dynamic_index_in_dim(grad, y, 1, keepdims=False)
        return stay, y_swap(away)

    def scatter_second(stay, came, j):
        both = (stay.astype(F32) + came.astype(F32)).astype(BF)
        both = [lax.dynamic_index_in_dim(both, (j + d) % nj, 0, keepdims=False) for d in range(nj)]
        return both[0], [z_shift(both[d], d) for d in range(1, nj)]

    def local(
        inputs, out_grad, segment_ids, pad_mask, bit_sel, w_qo, w_kv, w_mlp, norm_gains,
        m_qo, m_kv, m_mlp, m_gains, v_qo, v_kv, v_mlp, v_gains,
    ):
        i, m = lax.axis_index("dp"), lax.axis_index("mp")
        y, j = i % 2, i // 2
        zl = j % 2
        rows = inputs.shape[0]
        seq_len = segment_ids.shape[1]
        wrows = w_qo.shape[1]

        low_q = quantize(w_qo[0], D, bit_sel[0])
        low_o = quantize(w_qo[1], QW, bit_sel[0])
        low_kv = jnp.concatenate([quantize(w_kv[0], D, bit_sel[1]), quantize(w_kv[1], D, bit_sel[1])], 1)
        order = jnp.stack([m, m ^ 2, m ^ 1, m ^ 3])

        def in_order(vector):
            return vector.reshape(n_mp, rows)[order].reshape(-1)

        segments = segment_ids[0]
        positions = in_order(doc_positions(segments))
        slots = in_order(jnp.arange(seq_len, dtype=jnp.int32))
        segs = in_order(segments)
        pads = in_order(pad_mask[0])
        kv_cols = w_kv.shape[2]
        half_dim = HEAD_WIDTH // 2
        frequency = ROPE_BASE ** (-jnp.arange(half_dim, dtype=F32) * 2.0 / HEAD_WIDTH)
        angles = positions.astype(F32)[:, None] * frequency[None, :]
        cosine = jnp.cos(angles)
        sine = jnp.sin(angles)
        marks = jnp.stack([segs, slots, pads] + [segs] * 5)
        (
            query_bf, key_bf, value_bf, mixed_bf, attended, hidden_in, gain_rows, group_ffn, w_gate, w_up, w_down,
            wq, wkv, wo, seq_normed,
        ) = open_layer(
            n_dp, n_mp, low_q, low_kv, low_o, w_mlp, code_spacing(bit_sel[2]).reshape(1, 1), cosine, sine,
            marks.T, marks, inputs, norm_gains.reshape(1, -1),
        )
        w_gate, w_up, w_down = w_gate.reshape(D, -1), w_up.reshape(D, -1), w_down.reshape(D, -1)
        gate, up, activated, part = mlp(group_ffn, w_gate, w_up, w_down)
        live = lax.dynamic_slice_in_dim(pad_mask[0], m * rows, rows).astype(F32)[:, None]
        outputs, grad_gain_three, group_grad = turn(
            n_dp, n_mp, part, hidden_in, gain_rows, out_grad, live
        )
        tokens = 8 * rows
        grad_down = mm_rows(group_grad.reshape(tokens, D), activated.reshape(tokens, -1))
        grad_down = grad_down.astype(BF).reshape(nj, 2, wrows, -1)
        grad_down, group_grad = lax.optimization_barrier((grad_down, group_grad))
        down_stay, down_came = scatter_first(grad_down, y)
        grad_gate, grad_up, part = mlp_back(group_grad, gate, up, w_gate, w_up, w_down)
        flat_ffn = group_ffn.reshape(tokens, D)
        grads_gate = mm_rows(flat_ffn, grad_gate.reshape(tokens, -1)).astype(BF).reshape(nj, 2, wrows, -1)
        grads_gate, grad_up, down_came = lax.optimization_barrier((grads_gate, grad_up, down_came))
        down_own, down_shifted = scatter_second(down_stay, down_came, j)
        grads_up = mm_rows(flat_ffn, grad_up.reshape(tokens, -1)).astype(BF).reshape(nj, 2, wrows, -1)
        grad_hidden, grad_gain_one, grad_gain_two, seq_grad, sum_gate, sum_up = back(
            n_dp, n_mp, part, hidden_in, attended, gain_rows, out_grad, live, grads_gate, grads_up
        )
        seq_grad, down_shifted = lax.optimization_barrier((seq_grad, down_shifted))
        sums = [down_own.astype(F32), 0.0]
        for d in range(1, nj):
            sums[d % 2] = sums[d % 2] + down_shifted[d - 1].astype(F32)
        sum_down = jnp.concatenate(
            [jnp.where(zl == 0, sums[0], sums[1]), jnp.where(zl == 0, sums[1], sums[0])], 1
        )
        grad_in, grad_gain_zero, sum_q, sum_kv, sum_o = close(
            n_dp, n_mp, seq_grad.reshape(seq_len, D), seq_normed, query_bf, key_bf, value_bf, mixed_bf,
            wo, wq, wkv, cosine, sine, marks.T, marks, inputs, gain_rows, grad_hidden,
        )
        terms = jnp.concatenate([grad_gain_zero, grad_gain_one, grad_gain_two, grad_gain_three])
        flat_gains = [a.reshape(1, -1) for a in (norm_gains, m_gains, v_gains)]
        sums = [sum_gate, sum_up, sum_down, sum_q, sum_o, sum_kv]
        sum_gains, norm = norm_all(n_dp, n_mp, terms.reshape(n_dp * n_mp, 1, -1), sums)
        news = adam_all(
            norm, sum_gains, flat_gains, sums, [w_mlp, m_mlp, v_mlp, w_qo, m_qo, v_qo, w_kv, m_kv, v_kv]
        )
        grad_norm = norm[0, :1]
        new_gains, new_m_gains, new_v_gains = [a.reshape(-1) for a in news[:3]]
        new_w_mlp, new_m_mlp, new_v_mlp, new_w_qo, new_m_qo, new_v_qo, new_w_kv, new_m_kv, new_v_kv = news[3:]
        return (
            outputs, grad_in, grad_norm, new_w_qo, new_w_kv, new_w_mlp, new_gains,
            new_m_qo, new_m_kv, new_m_mlp, new_m_gains, new_v_qo, new_v_kv, new_v_mlp, new_v_gains,
        )

    return local


def solution(mesh):
    tokens = P(("dp", "mp"), None)
    weight = P(None, "dp", "mp")
    flat = P(("dp", "mp"))
    per_weight = (weight, weight, weight, flat)
    return jax.shard_map(
        build_local(mesh.shape["dp"], mesh.shape["mp"]),
        mesh=mesh,
        in_specs=(tokens, tokens, P("dp", None), P("dp", None), P()) + per_weight * 3,
        out_specs=(tokens, tokens, P()) + per_weight * 3,
        check_vma=False,
    )
```

```python
import functools
import math

import jax
import jax.numpy as jnp
from jax import lax
from jax.experimental import pallas as pl
from jax.experimental.pallas import tpu as pltpu
from jax.sharding import PartitionSpec as P

D = 2304
HEAD_WIDTH = 256
FF = 9216
NORMS = 4
QW = 2048
PARAMS = 77865984

EPSILON = 1e-06
SOFT_CAP = 50.0
ROPE_BASE = 10000.0
MASKED_SCORE = -1e30
FIRST_DECAY = 0.9
SECOND_DECAY = 0.95
LEARN_RATE = 0.04
WEIGHT_DECAY = 0.1
ADAM_EPSILON = 1e-08
CLIP_SCALE = 0.5

BF = jnp.bfloat16
F32 = jnp.float32


def code_spacing(selector):
    return jnp.where(selector == 0, 1.0, jnp.where(selector == 1, 16.0, 64.0)).astype(F32)


def quantize_values(master, step, spacing):
    half = jnp.floor(spacing * 0.5)
    inverse = jnp.where(spacing > 32.0, 1.0 / 64.0, jnp.where(spacing > 8.0, 1.0 / 16.0, 1.0))
    codes = jnp.clip(jnp.floor(master / step + 0.5), -128.0, 127.0)
    top = 128.0 * inverse
    sliced = jnp.clip(jnp.floor((codes + half) * inverse), -top, top - 1.0)
    return (sliced * spacing) * step


def quantize(master, fan_in, selector):
    step = jnp.float32(1.0 / (32.0 * math.sqrt(fan_in)))
    return quantize_values(master, step, code_spacing(selector)).astype(BF)


def inv_root(values):
    return lax.rsqrt(jnp.mean(values * values, axis=-1, keepdims=True) + EPSILON)


def rms_norm(values, norm_gain):
    return values * inv_root(values) * (1.0 + norm_gain)


def rms_back(values, norm_gain, grad):
    root = inv_root(values)
    scaled = grad * (1.0 + norm_gain)
    dot = jnp.mean(values * scaled, axis=-1, keepdims=True)
    grad_values = root * scaled - values * (root * root * root * dot)
    grad_gain = jnp.sum(values * root * grad, axis=0)
    return grad_values, grad_gain


def doc_positions(segments):
    slot_index = jnp.arange(segments.shape[0], dtype=jnp.int32)
    previous = jnp.concatenate([segments[:1] - 1, segments[:-1]])
    starts = segments != previous
    doc_begin = lax.cummax(jnp.where(starts, slot_index, 0), axis=0)
    return slot_index - doc_begin


def rotate(values, cosine, sine):
    half_dim = HEAD_WIDTH // 2
    turned = jnp.concatenate([-values[..., half_dim:], values[..., :half_dim]], -1)
    return values * cosine + turned * sine


def rotate_back(grads, cosine, sine):
    half_dim = HEAD_WIDTH // 2
    scaled = grads * sine
    turned = jnp.concatenate([scaled[..., half_dim:], -scaled[..., :half_dim]], -1)
    return grads * cosine + turned


def mm(left, right):
    return lax.dot_general(left, right, (((1,), (0,)), ((), ())), preferred_element_type=F32)


def mm_rows(left, right):
    return lax.dot_general(left, right, (((0,), (0,)), ((), ())), preferred_element_type=F32)


def mm_cols(left, right):
    return lax.dot_general(left, right, (((1,), (1,)), ((), ())), preferred_element_type=F32)


def adam_update(master, first_moment, second_moment, gradient, factor):
    clipped = gradient * factor
    new_first = FIRST_DECAY * first_moment + (1.0 - FIRST_DECAY) * clipped
    new_second = SECOND_DECAY * second_moment + (1.0 - SECOND_DECAY) * clipped * clipped
    new_master = master - LEARN_RATE * (
        new_first / (jnp.sqrt(new_second) + ADAM_EPSILON) + WEIGHT_DECAY * master
    )
    return (new_master, new_first, new_second)


MESH = pl.DeviceIdType.MESH
ANY = pl.BlockSpec(memory_space=pl.ANY)
VMEM = pl.BlockSpec(memory_space=pltpu.VMEM)
ROWS = 32


class Net:
    def __init__(self, n_dp, n_mp, send_sems, recv_sems, local_sems=None):
        self.n_dp, self.n_mp = n_dp, n_mp
        self.send_sems, self.recv_sems, self.local_sems = send_sems, recv_sems, local_sems
        self.used, self.used_local, self.open = 0, 0, []
        self.i, self.m = lax.axis_index("dp"), lax.axis_index("mp")
        self.y, self.j = self.i % 2, self.i // 2
        self.zl = self.j % 2
        self.c, self.x = self.m % 2, self.m // 2
        self.core_n = (self.i, self.m + 1 - 2 * self.c)
        self.x_n = (self.i, (self.m + 2) % 4)
        self.y_n = (self.i + 1 - 2 * self.y, self.m)
        self.z_n = (self.i + 2 - 4 * self.zl, self.m)

    def z_at(self, d):
        nj = self.n_dp // 2
        return (((self.j + d) % nj) * 2 + self.y, self.m)

    def place(self):
        return (1 - self.y) * self.j + self.y * (self.n_dp - 1 - self.j)

    def ring(self, at):
        n, nj = self.n_dp, self.n_dp // 2
        at = at % n
        late = at // nj
        return (1 - late) * 2 * at + late * (2 * (n - 1 - at) + 1)

    def meet(self, devices):
        barrier = pltpu.get_barrier_semaphore()
        for device in devices:
            pl.semaphore_signal(barrier, inc=1, device_id=device, device_id_type=MESH)
        pl.semaphore_wait(barrier, len(devices))

    def send(self, src, dst, device):
        at = self.used
        self.used += 1
        copy = pltpu.make_async_remote_copy(
            src_ref=src, dst_ref=dst, send_sem=self.send_sems.at[at], recv_sem=self.recv_sems.at[at],
            device_id=device, device_id_type=MESH,
        )
        copy.start()
        self.open.append((copy, copy.wait_send))
        return copy

    def family(self, count, make):
        base = self.used
        self.used += count

        def copy_of(k):
            return make(k, self.send_sems.at[base + k], self.recv_sems.at[base + k])

        for k in range(count):
            copy = copy_of(k)
            self.open.append((copy, copy.wait_send))
        return copy_of

    def locals(self, count):
        base = self.used_local
        self.used_local += count
        return base

    def sent(self, copy):
        copy.wait_send()
        self.open = [entry for entry in self.open if entry[0] is not copy]

    def move(self, src, dst):
        at = self.used_local
        self.used_local += 1
        copy = pltpu.make_async_copy(src, dst, self.local_sems.at[at])
        copy.start()
        return copy

    def keep(self, src, dst):
        copy = self.move(src, dst)
        self.open.append((copy, copy.wait))

    def close(self):
        for _, wait in self.open:
            wait()


def upper(count):
    return count // 16 * 8


def dma(n):
    return pltpu.SemaphoreType.DMA((n,))


def call(kernel, outs, out_specs, in_specs, scratch, cid, mb, flops=0):
    return pl.pallas_call(
        kernel,
        out_shape=outs,
        in_specs=in_specs,
        out_specs=out_specs,
        scratch_shapes=scratch,
        compiler_params=pltpu.CompilerParams(
            collective_id=cid, has_side_effects=True, vmem_limit_bytes=mb << 20
        ),
    )


def by_rows(total, body, carry=0):
    return lax.fori_loop(
        0, total // ROWS, lambda t, state: body(pl.ds(pl.multiple_of(t * ROWS, ROWS), ROWS), state), carry
    )


def everyone(n_dp, n_mp, i, m):
    flat = i * n_mp + m
    total = n_dp * n_mp
    return [(((flat + t) % total) // n_mp, (flat + t) % n_mp) for t in range(1, total)]


def gather_seq_steps(net, own, seq):
    far = net.send(own, seq.at[1], net.x_n)
    near = net.send(own, seq.at[2], net.core_n)
    net.keep(own, seq.at[0])

    def finish():
        far.wait_recv()
        both = net.send(seq.at[1], seq.at[3], net.core_n)
        near.wait_recv()
        both.wait_recv()

    return finish


def gather_pair_steps(net, own, group, split=False):
    far = net.send(own, group.at[2], net.x_n)
    zed = net.send(own, group.at[1], net.z_n)
    near = net.send(own, group.at[4], net.core_n)
    net.keep(own, group.at[0])

    def finish(between=lambda: None):
        head = pl.ds(0, D // 2) if split else pl.ds(0, D)
        rest = pl.ds(D // 2, D // 2)
        zed.wait_recv()
        both = net.send(group.at[1, :, head], group.at[3, :, head], net.x_n)
        far.wait_recv()
        if split:
            other = net.send(group.at[2, :, rest], group.at[3, :, rest], net.z_n)
        near_z = net.send(group.at[1], group.at[5], net.core_n)
        near_x = net.send(group.at[2], group.at[6], net.core_n)
        between()
        both.wait_recv()
        if split:
            other.wait_recv()
        near_both = net.send(group.at[3], group.at[7], net.core_n)
        for copy in (near, near_z, near_x, near_both):
            copy.wait_recv()

    return finish


def pair_partners(net, with_y):
    nj = net.n_dp // 2
    zs = [net.z_at(d) for d in range(1, nj)] if with_y else [net.z_n]
    return [net.core_n, net.x_n] + zs + ([net.y_n] if with_y else [])


def row_tiles(total, size, body):
    lax.fori_loop(
        0, total // size, lambda t, state: (body(pl.ds(pl.multiple_of(t * size, size), size)), state)[1], 0
    )


def project(seq, wq, wkv, cosine, sine, q, k, v):
    total = seq.shape[0]
    kv_cols = k.shape[1]
    half = HEAD_WIDTH // 2

    def body(at):
        tokens = seq[at]
        c, s = cosine[at], sine[at]

        def turn(lin, out, cols):
            for h in range(0, cols, HEAD_WIDTH):
                a, b = lin[:, h : h + half], lin[:, h + half : h + HEAD_WIDTH]
                out[at, h : h + half] = (a * c - b * s).astype(BF)
                out[at, h + half : h + HEAD_WIDTH] = (b * c + a * s).astype(BF)

        turn(mm(tokens, wq[...]), q, q.shape[1])
        lin = mm(tokens, wkv[...])
        turn(lin, k, kv_cols)
        v[at] = lin[:, kv_cols:].astype(BF)

    row_tiles(total, total // 2, body)


def allowed_tile(marks_col, marks_row, at):
    segs, slots = marks_col[at, 0:1], marks_col[at, 1:2]
    seg_row, slot_row, pad_row = marks_row[0:1], marks_row[1:2], marks_row[2:3]
    same_slot = slot_row == slots
    return (seg_row == segs) & (slot_row <= slots) & ((pad_row == 1) | same_slot)


def tile_probs(q, k, allowed, at, head, group):
    cols = slice(head * HEAD_WIDTH, (head + 1) * HEAD_WIDTH)
    kv = head // group
    kv_at = slice(kv * HEAD_WIDTH, (kv + 1) * HEAD_WIDTH)
    bent = jnp.tanh(mm_cols(q[at, cols], k[:, kv_at]) * (HEAD_WIDTH**-0.5 / SOFT_CAP))
    raised = jnp.where(allowed, jnp.exp(SOFT_CAP * bent), 0.0)
    return bent, raised * (1.0 / jnp.sum(raised, axis=-1, keepdims=True))


def attend(q, k, v, marks_col, marks_row, mixed):
    total = q.shape[0]
    heads, group = q.shape[1] // HEAD_WIDTH, q.shape[1] // k.shape[1]

    def body(at):
        allowed = allowed_tile(marks_col, marks_row, at)
        for head in range(heads):
            _, probs = tile_probs(q, k, allowed, at, head, group)
            kv = head // group
            kv_at = slice(kv * HEAD_WIDTH, (kv + 1) * HEAD_WIDTH)
            mixed[at, head * HEAD_WIDTH : (head + 1) * HEAD_WIDTH] = mm(
                probs.astype(BF), v[:, kv_at]
            ).astype(BF)

    row_tiles(total, 128, body)


def out_project(mixed, wo, part):
    blocks, rows, _ = part.shape
    wide = D // 3
    for pair in range(blocks // 2 - 1, -1, -1):
        for n in range(0, D, wide):
            got = mm_cols(mixed[pair * 2 * rows : (pair + 1) * 2 * rows], wo[n : n + wide]).astype(BF)
            part[pair * 2, :, n : n + wide] = got[:rows]
            part[pair * 2 + 1, :, n : n + wide] = got[rows:]


def chunks(wrows):
    if wrows % 48 == 0:
        return tuple((n * wrows // 3, wrows // 3) for n in range(3))
    return ((0, upper(wrows)), (upper(wrows), wrows - upper(wrows)))


def two_parts(wrows):
    return ((0, upper(wrows)), (upper(wrows), wrows - upper(wrows)))


class Gather:
    def __init__(self, net, pieces):
        self.net, self.pieces, self.nj = net, pieces, net.n_dp // 2
        self.flight, self.relays, self.own = {}, {}, {}

    def out(self, n):
        net = self.net
        source, place, parity = self.pieces[n]
        self.own[n] = net.move(source(net.zl), place(net.i))
        self.relays[n] = [net.send(source(net.zl), place(net.i), net.y_n)]
        for d in range(1, self.nj):
            self.flight[n, d] = net.send(source((net.j + d) % self.nj % 2), place(net.i), net.z_at(d))

    def on(self, n):
        net = self.net
        _, place, _ = self.pieces[n]
        for d in range(1, self.nj):
            self.flight[n, d].wait_recv()
            at = ((net.j + self.nj - d) % self.nj) * 2 + net.y
            self.relays[n].append(net.send(place(at), place(at), net.y_n))

    def done(self, n):
        self.own.pop(n).wait()
        for copy in self.relays.pop(n):
            copy.wait_recv()


def all_of_dp(net):
    return [net.x_n, net.core_n] + [((net.i + t) % net.n_dp, net.m) for t in range(1, net.n_dp)]


def open_kernel(
    n_dp, n_mp, low_q, low_kv, low_o, w_mlp, width_mlp, cosine, sine, marks_col, marks_row, inputs, own_gains,
    q, k, v, mixed, att, hid, gains, group, full0, full1, full2, out_q, out_kv, out_o, out_seq,
    wq, wkv, wo, seq, part, r1, r2, own, got_gains, masters, lows, ss, rs, ls,
):
    net = Net(n_dp, n_mp, ss, rs, ls)
    p = net.place()
    right = (net.ring(p + 1), net.m)
    left = (net.ring(p + n_dp - 1), net.m)
    rows = inputs.shape[0]
    wrows, width = full0.shape[1:]
    others = everyone(n_dp, n_mp, net.i, net.m)
    net.meet(others)
    flat = net.i * n_mp + net.m
    loads = [net.move(w_mlp.at[n], masters.at[n]) for n in range(3)]

    def block(ref, at):
        return ref.at[pl.ds(pl.multiple_of(at * wrows, 8), wrows)]

    def lot(n):
        return seq.at[pl.ds(n * rows, rows)]

    def piece(ref, at, part):
        first, count = part
        return ref.at[pl.ds(pl.multiple_of(at * wrows + first, 8), count)]

    parts = two_parts(wrows)
    flight = {}
    for cut in parts:
        for lane, (ref, low, device) in enumerate(((wq, low_q, right), (wkv, low_kv, left))):
            flight[cut, lane] = net.send(low.at[pl.ds(*cut)], piece(ref, net.i, cut), device)
    spread = [net.send(own_gains, got_gains.at[flat], device) for device in others]
    net.move(own_gains, got_gains.at[flat]).wait()
    for copy in spread:
        copy.wait_recv()
    per_norm = n_dp * n_mp // NORMS
    for n in range(NORMS):
        gains[n : n + 1] = jnp.concatenate([got_gains[n * per_norm + t] for t in range(per_norm)], 1)
    g0 = 1.0 + gains[0:1]

    def norm_rows(at, state):
        own[at] = (inputs[at] * inv_root(inputs[at]) * g0).astype(BF)
        return state

    by_rows(rows, norm_rows)
    far = net.send(own, lot(1), net.x_n)
    near = net.send(own, lot(2), net.core_n)

    def quantize_part(n):
        loads[n].wait()
        spacing = width_mlp[...]
        step = jnp.float32(1.0 / (32.0 * math.sqrt(FF if n == 2 else D)))

        def body(at, state, count):
            lows[n, at] = quantize_values(masters[n, at], step, spacing).astype(BF)
            return state

        in_steps(wrows, body)

    own_parts = [net.move(own, lot(0)), net.move(low_q, block(wq, net.i)), net.move(low_kv, block(wkv, net.i))]
    half = lambda which: pl.ds(pl.multiple_of(which * width, width), width)
    pieces = [(lambda which: low_o, lambda at: block(wo, at), 1)]

    def add_piece(ref, full, first, count):
        rows_at = pl.ds(first, count)
        pieces.append((lambda which: ref.at[rows_at, half(which)], lambda at: full.at[at, rows_at], 2))

    for ref, full in ((lows.at[0], full0), (lows.at[1], full1), (lows.at[2], full2)):
        for first, count in chunks(wrows):
            add_piece(ref, full, first, count)
    weights = Gather(net, pieces)
    for hop in range(1, n_dp):
        from_right, from_left = net.ring(p + n_dp - hop), net.ring(p + hop)
        for cut in parts:
            for lane, (ref, at, device) in enumerate(((wq, from_right, right), (wkv, from_left, left))):
                flight[cut, lane].wait_recv()
                if hop < n_dp - 1:
                    flight[cut, lane] = net.send(piece(ref, at, cut), piece(ref, at, cut), device)
        if hop == n_dp // 2:
            far.wait_recv()
            both = net.send(lot(1), lot(3), net.core_n)
        if hop in (1, 2, 3):
            quantize_part(hop - 1)
        if hop == n_dp - 2:
            weights.out(0)
    weights.out(1)
    weights.out(2)
    weights.out(3)
    near.wait_recv()
    both.wait_recv()
    for copy in own_parts:
        copy.wait()
    net.sent(far)
    net.sent(near)
    for ref, result in ((wq, out_q), (wkv, out_kv), (seq, out_seq)):
        net.keep(ref, result)
    project(seq, wq, wkv, cosine, sine, q, k, v)
    attend(q, k, v, marks_col, marks_row, mixed)
    def step(n):
        if n < len(pieces):
            weights.on(n)
            if n + 4 < len(pieces):
                weights.out(n + 4)

    step(0)
    weights.done(0)
    net.keep(wo, out_o)
    out_project(mixed, wo, part)
    c1 = net.send(part.at[3], r1.at[1], net.core_n)
    c0 = net.send(part.at[2], r1.at[0], net.core_n)
    c1.wait_recv()

    def first_rows(at, state):
        part[1, at] = (part[1, at].astype(F32) + r1[1, at].astype(F32)).astype(BF)
        return state

    by_rows(rows, first_rows)
    x = net.send(part.at[1], r2, net.x_n)
    c0.wait_recv()
    step(1)
    x.wait_recv()
    g1, g2 = 1.0 + gains[1:2], 1.0 + gains[2:3]

    def second(at, state):
        total = part[0, at].astype(F32) + r1[0, at].astype(F32) + r2[at].astype(F32)
        att[at] = total
        hidden = inputs[at] + total * inv_root(total) * g1
        hid[at] = hidden
        own[at] = (hidden * inv_root(hidden) * g2).astype(BF)
        return state

    by_rows(rows, second)
    finish = gather_pair_steps(net, own, group)
    step(2)
    step(3)
    finish(lambda: (step(4), step(5)))
    for n in range(6, len(pieces)):
        step(n)
    for n in range(1, len(pieces)):
        weights.done(n)
    net.close()


def open_layer(n_dp, n_mp, low_q, low_kv, low_o, w_mlp, width_mlp, cosine, sine, marks_col, marks_row, inputs, gains):
    rows = inputs.shape[0]
    nj = n_dp // 2
    total_devices = n_dp * n_mp
    count = 24 + 4 * n_dp + 20 * nj + total_devices
    block = (rows, D)
    wrows, width = w_mlp.shape[1], w_mlp.shape[2] // 2
    cols, kv_cols = low_q.shape[1], low_kv.shape[1] // 2
    vm = lambda *shape: pltpu.VMEM(shape, BF)
    bf = lambda *shape: jax.ShapeDtypeStruct(shape, BF)
    total = 4 * rows
    f32 = jax.ShapeDtypeStruct(block, F32)
    full = bf(n_dp, wrows, width)
    return call(
        functools.partial(open_kernel, n_dp, n_mp),
        [
            bf(total, cols), bf(total, kv_cols), bf(total, kv_cols), bf(total, cols), f32, f32,
            jax.ShapeDtypeStruct((NORMS, D), F32),
            bf(8, *block), full, full, full, bf(D, cols), bf(D, 2 * kv_cols), bf(D, cols), bf(total, D),
        ],
        [VMEM] * 7 + [ANY] * 8, [ANY] * 4 + [VMEM] * 7,
        [
            vm(D, cols), vm(D, 2 * kv_cols), vm(D, cols), vm(total, D), vm(4, *block), vm(2, *block), vm(*block),
            vm(*block), pltpu.VMEM((total_devices,) + gains.shape, F32), pltpu.VMEM(w_mlp.shape, F32),
            vm(*w_mlp.shape), dma(count), dma(count), dma(32),
        ],
        2, 60,
    )(low_q, low_kv, low_o, w_mlp, width_mlp, cosine, sine, marks_col, marks_row, inputs, gains)


def reduce_pair_steps(net, near, cores, r1, r2, r3, rows, split=False, compute=None, hooks=None):
    plan = [(pl.ds(0, D // 2 if split else D), (3, 2), net.x_n, 1, net.z_n)]
    if split:
        plan.append((pl.ds(D // 2, D // 2), (3, 1), net.z_n, 2, net.x_n))
    firsts = {}
    for k in (3, 2, 1) if split else (3, 2):
        compute(k)
        cores(k).wait_recv()
        for part, (cols, blocks, device, _, _) in enumerate(plan):
            if k not in blocks:
                continue
            at_block = blocks.index(k)

            def add(at, state, k=k, cols=cols):
                near[k, at, cols] = (near[k, at, cols].astype(F32) + r1[k, at, cols].astype(F32)).astype(BF)
                return state

            by_rows(rows, add)
            firsts[part, at_block] = net.send(near.at[k, :, cols], r2.at[at_block, :, cols], device)
    for k in (0,) if split else (1, 0):
        compute(k)
        cores(k).wait_recv()
    last = []
    if hooks:
        hooks[0]()
    for part, (cols, blocks, _, second, device) in enumerate(plan):
        firsts[part, 0].wait_recv()

        def add(at, state, cols=cols, second=second):
            near[second, at, cols] = (
                near[second, at, cols].astype(F32) + r1[second, at, cols].astype(F32) + r2[0, at, cols].astype(F32)
            ).astype(BF)
            return state

        by_rows(rows, add)
        last.append(net.send(near.at[second, :, cols], r3.at[:, cols], device))
    if hooks:
        hooks[1]()
    for part in range(len(plan)):
        firsts[part, 1].wait_recv()
    return last


def pair_sum(near, r1, r2, r3, at):
    return near[0, at].astype(F32) + r1[0, at].astype(F32) + r2[1, at].astype(F32) + r3[at].astype(F32)


def pair_scratch(rows, blocks=8):
    block = (rows, D)
    return [
        pltpu.VMEM((blocks,) + block, BF), pltpu.VMEM((4,) + block, BF), pltpu.VMEM((2,) + block, BF),
        pltpu.VMEM(block, BF), pltpu.VMEM(block, BF),
    ]


def core_family(net, parts, r1):
    return net.family(
        4,
        lambda k, send, recv: pltpu.make_async_remote_copy(
            src_ref=parts.at[4 + k], dst_ref=r1.at[k], send_sem=send, recv_sem=recv,
            device_id=net.core_n, device_id_type=MESH,
        ),
    )


def block_at(t):
    return 7 - t // 2 - 4 * (t % 2)


class Stream:
    def __init__(self, net, pairs, inward):
        self.net, self.pairs, self.inward = net, pairs, inward
        self.base = net.locals(2 * len(pairs))

    def copies(self, t):
        slot = t % 2
        for n, (far, held) in enumerate(self.pairs):
            ends = (far.at[block_at(t)], held.at[slot])
            yield pltpu.make_async_copy(
                *(ends if self.inward else ends[::-1]), self.net.local_sems.at[self.base + 2 * n + slot]
            )

    def start(self, t):
        for copy in self.copies(t):
            copy.start()

    def wait(self, t):
        for copy in self.copies(t):
            copy.wait()


def rms_back_rows(values, gain, grad):
    root = inv_root(values)
    scaled = grad * gain
    dot = jnp.mean(values * scaled, axis=-1, keepdims=True)
    return root * scaled - values * (root * root * root * dot), jnp.sum(values * root * grad, axis=0, keepdims=True)


def turn_kernel(
    n_dp, n_mp, ffn, w_gate, w_up, w_down, hid, gains, out_grad, live,
    outputs, dgain, gate, up, act, group,
    parts, r1, r2, r3, own, wg, wu, wd, tokens, gate_b, up_b, act_b, ss, rs, ls,
):
    net = Net(n_dp, n_mp, ss, rs, ls)
    loads = [net.move(src, dst) for src, dst in ((w_gate, wg), (w_up, wu), (w_down, wd))]
    rows = hid.shape[0]
    incoming = Stream(net, [(ffn, tokens)], True)
    outgoing = Stream(net, [(gate, gate_b), (up, up_b), (act, act_b)], False)
    cores = core_family(net, parts, r1)
    incoming.start(0)
    net.meet(pair_partners(net, False))
    for load in loads:
        load.wait()

    def block(t, state):
        slot, at = t % 2, block_at(t)
        incoming.wait(t)

        @pl.when(t < 7)
        def _():
            incoming.start(t + 1)

        g = mm(tokens[slot], wg[...])
        u = mm(tokens[slot], wu[...])
        bend = jnp.tanh(GELU * (g + 0.044715 * (g * g * g)))
        a = (0.5 * g * (1.0 + bend) * u).astype(BF)

        @pl.when(t >= 2)
        def _():
            outgoing.wait(t - 2)

        gate_b[slot] = g
        up_b[slot] = u
        act_b[slot] = a
        outgoing.start(t)
        parts[at] = mm_cols(a, wd[...]).astype(BF)
        return state

    def compute(k):
        def both(t, state):
            block(t, state)

            @pl.when(t % 2 == 0)
            def _():
                cores(k).start()

            return state

        lax.fori_loop(6 - 2 * k, 8 - 2 * k, both, 0)

    last_sums = reduce_pair_steps(net, parts, cores, r1, r2, r3, rows, True, compute)
    outgoing.wait(6)
    outgoing.wait(7)
    for copy in last_sums:
        copy.wait_recv()
    g3 = 1.0 + gains[3:4]

    def last(at, state):
        total = pair_sum(parts, r1, r2, r3, at)
        outputs[at] = hid[at] + total * inv_root(total) * g3
        grad, dg = rms_back_rows(total, g3, out_grad[at] * live[at])
        own[at] = grad.astype(BF)
        return state + dg

    dgain[...] = by_rows(rows, last, jnp.zeros((1, D), F32))
    gather_pair_steps(net, own, group, True)()
    net.close()


def turn(n_dp, n_mp, ffn, w_gate, w_up, w_down, hid, gains, out_grad, live):
    rows = hid.shape[0]
    block = (rows, D)
    width = w_gate.shape[1]
    vm = lambda *shape: pltpu.VMEM(shape, BF)
    return call(
        functools.partial(turn_kernel, n_dp, n_mp),
        [
            jax.ShapeDtypeStruct(block, F32), jax.ShapeDtypeStruct((1, D), F32),
            jax.ShapeDtypeStruct((8, rows, width), F32), jax.ShapeDtypeStruct((8, rows, width), F32),
            jax.ShapeDtypeStruct((8, rows, width), BF), jax.ShapeDtypeStruct((8,) + block, BF),
        ],
        [VMEM, VMEM] + [ANY] * 4, [ANY] * 4 + [VMEM] * 4,
        pair_scratch(rows)
        + [
            vm(D, width), vm(D, width), vm(D, width), vm(2, *block),
            pltpu.VMEM((2, rows, width), F32), pltpu.VMEM((2, rows, width), F32), vm(2, rows, width),
            dma(32), dma(32), dma(16),
        ],
        4, 60,
    )(ffn, w_gate, w_up, w_down, hid, gains, out_grad, live)


def in_steps(count, body, carry=0, first=0):
    step = 16 if count % 16 == 0 else 8
    return lax.fori_loop(
        0, count // step,
        lambda t, state: body(pl.ds(pl.multiple_of(first + t * step, 8), step), state, step), carry,
    )


class Scatter:
    def __init__(self, net, grads, stay, came, last):
        self.net, self.grads, self.stay, self.came, self.last = net, grads, stay, came, last
        self.nj, self.wrows, self.width = came.shape
        self.turns = sorted(range(1, self.nj), key=lambda d: abs(d - self.nj // 2)) + [0]
        self.ys, self.moves, self.zs = {}, {}, {}

    def along_y(self, turns=None):
        net = self.net
        for d in self.turns if turns is None else turns:
            at = (net.j + d) % self.nj
            self.ys[d] = net.send(self.grads.at[at, 1 - net.y], self.came.at[d], net.y_n)
            self.moves[d] = net.move(self.grads.at[at, net.y], self.stay.at[d])

    def along_z(self, turns):
        for d in turns:
            self.ys[d].wait_recv()
            self.moves[d].wait()

            def add(at, state, step, d=d):
                self.stay[d, at] = (self.stay[d, at].astype(F32) + self.came[d, at].astype(F32)).astype(BF)
                return state

            in_steps(self.wrows, add)
            if d:
                self.zs[d] = self.net.send(self.stay.at[d], self.last.at[d - 1], self.net.z_at(d))

    def landed(self):
        for d in range(1, self.nj):
            self.zs[d].wait_recv()

    def halves(self, total, sums):
        self.landed()

        def collect(at, state, step):
            both = [self.stay[0, at].astype(F32), jnp.zeros((step, self.width), F32)]
            for d in range(1, self.nj):
                both[d % 2] = both[d % 2] + self.last[d - 1, at].astype(F32)
            for parity in range(2):
                total[parity, at] = both[parity]
            return state

        in_steps(self.wrows, collect)
        copies = []
        for parity in range(2):
            half = (self.net.zl + parity) % 2
            copies.append(self.net.move(total.at[parity], sums.at[:, pl.ds(pl.multiple_of(half * self.width, self.width), self.width)]))
        return copies

    def whole(self, out):
        self.landed()

        def collect(at, state, step):
            value = self.stay[0, at].astype(F32)
            for d in range(1, self.nj):
                value = value + self.last[d - 1, at].astype(F32)
            out[at] = value
            return state

        in_steps(self.wrows, collect)


def scatter_scratch(nj, wrows, width):
    return [
        pltpu.VMEM((nj, wrows, width), BF), pltpu.VMEM((nj, wrows, width), BF),
        pltpu.VMEM((nj - 1, wrows, width), BF),
    ]


def back_kernel(
    n_dp, n_mp, part, hid, att, gains, out_grad, live, grads, grads_up,
    ghid, dg1, dg2, seq, sums, sums_up,
    near, r1, r2, r3, own, stay, came, last, ustay, ucame, ulast, total, ss, rs, ls,
):
    net = Net(n_dp, n_mp, ss, rs, ls)
    loaded = net.move(part.at[pl.ds(0, 4)], near)
    cores = core_family(net, part, r1)
    net.meet(pair_partners(net, True))
    rows = hid.shape[0]
    for k in (3, 2, 1, 0):
        cores(k).start()
    weight = Scatter(net, grads, stay, came, last)
    weight_up = Scatter(net, grads_up, ustay, ucame, ulast)
    weight.along_y()
    loaded.wait()
    last_sums = reduce_pair_steps(
        net, near, cores, r1, r2, r3, rows, False, lambda k: None,
        (lambda: weight.along_z(weight.turns[:1]), lambda: weight.along_z(weight.turns[1:2])),
    )
    weight_up.along_y()
    for copy in last_sums:
        copy.wait_recv()
    g1, g2 = 1.0 + gains[1:2], 1.0 + gains[2:3]

    def rows_back(at, state):
        grad = pair_sum(near, r1, r2, r3, at)
        part_hid, d2 = rms_back_rows(hid[at], g2, grad)
        grad_hidden = out_grad[at] * live[at] + part_hid
        ghid[at] = grad_hidden
        grad_att, d1 = rms_back_rows(att[at], g1, grad_hidden)
        own[at] = grad_att.astype(BF)
        return state[0] + d1, state[1] + d2

    zero = jnp.zeros((1, D), F32)
    done1, done2 = by_rows(rows, rows_back, (zero, zero))
    dg1[...] = done1
    dg2[...] = done2
    finish = gather_seq_steps(net, own, seq)
    weight.along_z(weight.turns[2:])
    weight_up.along_z(weight_up.turns[:1])
    finish()
    weight_up.along_z(weight_up.turns[1:2])
    first_out = weight.halves(total, sums)
    weight_up.along_z(weight_up.turns[2:])
    for copy in first_out:
        copy.wait()
    for copy in weight_up.halves(total, sums_up):
        copy.wait()
    net.close()


def back(n_dp, n_mp, part, hid, att, gains, out_grad, live, grads, grads_up):
    rows = hid.shape[0]
    block = (rows, D)
    nj = n_dp // 2
    _, _, wrows, width = grads.shape
    count = 24 + 6 * nj
    return call(
        functools.partial(back_kernel, n_dp, n_mp),
        [
            jax.ShapeDtypeStruct(block, F32), jax.ShapeDtypeStruct((1, D), F32), jax.ShapeDtypeStruct((1, D), F32),
            jax.ShapeDtypeStruct((4,) + block, BF), jax.ShapeDtypeStruct((wrows, 2 * width), F32),
            jax.ShapeDtypeStruct((wrows, 2 * width), F32),
        ],
        [VMEM, VMEM, VMEM, ANY, ANY, ANY], [ANY] + [VMEM] * 5 + [ANY, ANY],
        pair_scratch(rows, 4) + scatter_scratch(nj, wrows, width) * 2
        + [pltpu.VMEM((2, wrows, width), F32), dma(count), dma(count), dma(16 + 2 * nj)],
        5, 60,
    )(part, hid, att, gains, out_grad, live, grads, grads_up)


def attend_back(q, k, v, gm, marks_col, marks_row, cosine, sine, dq, dk, dv, tiles):
    total = q.shape[0]
    heads, group = q.shape[1] // HEAD_WIDTH, q.shape[1] // k.shape[1]
    size = total // 4
    half = HEAD_WIDTH // 2
    scale = HEAD_WIDTH**-0.5

    def body(t, state):
        at = pl.ds(pl.multiple_of(t * size, size), size)
        allowed = allowed_tile(marks_col, marks_row, at)
        c, s = cosine[at], sine[at]
        for head in range(heads):
            kv = head // group
            cols = slice(head * HEAD_WIDTH, (head + 1) * HEAD_WIDTH)
            kv_at = slice(kv * HEAD_WIDTH, (kv + 1) * HEAD_WIDTH)
            bent, probs = tile_probs(q, k, allowed, at, head, group)
            grad = gm[at, cols]
            dv[:, kv_at] += mm_rows(probs.astype(BF), grad)
            gp = mm_cols(grad, v[:, kv_at])
            inner = jnp.sum(probs * gp, axis=-1, keepdims=True)
            ds = (probs * (gp - inner) * (1.0 - bent * bent)).astype(BF)
            dk[:, kv_at] += mm_rows(ds, q[at, cols]) * scale
            turned = mm(ds, k[:, kv_at]) * scale
            a, b = turned[:, :half], turned[:, half:]
            first = head * HEAD_WIDTH
            dq[at, first : first + half] = (a * c + b * s).astype(BF)
            dq[at, first + half : first + HEAD_WIDTH] = (b * c - a * s).astype(BF)
        return state

    lax.fori_loop(tiles[0], tiles[1], body, 0)


def weight_grad(tokens, grads, out):
    wide = D // 3
    for n in range(0, D, wide):
        out[n : n + wide] = mm_rows(tokens[:, n : n + wide], grads[...]).astype(BF)


def close_kernel(
    n_dp, n_mp, seq_grad, seq_normed, q, k, v, mixed, wo, wq, wkv, cosine, sine, marks_col, marks_row,
    inputs, gains, ghid,
    gin, dg0, sum_q, sum_kv, sum_o,
    tokens, normed, wa, gm, dq, dk, dv, dkv, go, gq, gkv, got_q, got_kv, r1, r2,
    ostay, ocame, olast, ss, rs, ls,
):
    net = Net(n_dp, n_mp, ss, rs, ls)
    p = net.place()
    right = (net.ring(p + 1), net.m)
    left = (net.ring(p + n_dp - 1), net.m)
    nj = n_dp // 2
    rows = inputs.shape[0]
    seq_len, wrows = tokens.shape[0], sum_q.shape[0]
    net.meet(all_of_dp(net))
    token_load = net.move(seq_grad, tokens)
    wa_load = net.move(wo, wa)
    normed_load = net.move(seq_normed, normed)
    ghid_load = net.move(ghid, gin)
    dk[...] = jnp.zeros_like(dk)
    dv[...] = jnp.zeros_like(dv)
    token_load.wait()
    wa_load.wait()

    def mix(at):
        gm[at] = mm(tokens[at], wa[...]).astype(BF)

    row_tiles(seq_len, seq_len // 2, mix)
    wa_load = net.move(wq, wa)
    weight_grad(tokens, mixed, go.reshape(D, go.shape[-1]))
    out = Scatter(net, go, ostay, ocame, olast)
    out.along_y()
    attend_back(q, k, v, gm, marks_col, marks_row, cosine, sine, dq, dk, dv, (0, 2))
    out.along_z(out.turns[:1])
    attend_back(q, k, v, gm, marks_col, marks_row, cosine, sine, dq, dk, dv, (2, 4))
    out.along_z(out.turns[1:])
    kv_cols = k.shape[1]
    half = HEAD_WIDTH // 2

    def turn_keys(at):
        c, s = cosine[at], sine[at]
        for h in range(0, kv_cols, HEAD_WIDTH):
            a, b = dk[at, h : h + half], dk[at, h + half : h + HEAD_WIDTH]
            dkv[at, h : h + half] = (a * c + b * s).astype(BF)
            dkv[at, h + half : h + HEAD_WIDTH] = (b * c - a * s).astype(BF)
        dkv[at, kv_cols:] = dv[at].astype(BF)

    row_tiles(seq_len, 128, turn_keys)
    normed_load.wait()
    weight_grad(normed, dq, gq)
    weight_grad(normed, dkv, gkv)

    def block(at, part):
        return pl.ds(pl.multiple_of(net.ring(p + 2 * n_dp + at) * wrows + part[0], 8), part[1])

    lanes = ((gq, got_q, sum_q, right, -1), (gkv, got_kv, sum_kv, left, 1))
    parts = two_parts(wrows)
    flight = {}
    for part in parts:
        for lane, (terms, got, _, device, way) in enumerate(lanes):
            flight[lane, part] = net.send(terms.at[block(way, part)], got.at[0, pl.ds(*part)], device)

    def hop(n):
        end = n == n_dp - 1
        for part in parts:
            for lane, (terms, got, result, device, way) in enumerate(lanes):
                flight[lane, part].wait_recv()
                first = net.ring(p + 2 * n_dp + way * (1 + n)) * wrows

                def add(here, state, step, first=first, terms=terms, got=got, result=result):
                    at = pl.ds(pl.multiple_of(first + here.start, 8), step)
                    value = got[n - 1, here].astype(F32) + terms[at].astype(F32)
                    if end:
                        result[here] = value
                    else:
                        terms[at] = value.astype(BF)
                    return state

                in_steps(part[1], add, 0, part[0])
                if not end:
                    flight[lane, part] = net.send(
                        terms.at[block(way * (1 + n), part)], got.at[n, pl.ds(*part)], device
                    )

    wa_load.wait()
    wide = D // 3
    copies = []
    for pair in (1, 0):
        at = pl.ds(pair * 2 * rows, 2 * rows)
        for n in range(0, D, wide):
            tokens[at, n : n + wide] = (
                mm_cols(dq[at], wa[n : n + wide]) + mm_cols(dkv[at], wkv[n : n + wide])
            ).astype(BF)
        if pair:
            c1 = net.send(tokens.at[pl.ds(3 * rows, rows)], r1.at[1], net.core_n)
            c0 = net.send(tokens.at[pl.ds(2 * rows, rows)], r1.at[0], net.core_n)
            hop(1)
    c1.wait_recv()

    def add_far(at, state):
        here = pl.ds(pl.multiple_of(rows + at.start, ROWS), ROWS)
        tokens[here] = (tokens[here].astype(F32) + r1[1, at].astype(F32)).astype(BF)
        return state

    by_rows(rows, add_far)
    x = net.send(tokens.at[pl.ds(rows, rows)], r2, net.x_n)
    c0.wait_recv()
    hop(2)
    hop(3)
    x.wait_recv()
    ghid_load.wait()
    g0 = 1.0 + gains[0:1]

    def rows_in(at, state):
        grad = tokens[at].astype(F32) + r1[0, at].astype(F32) + r2[at].astype(F32)
        part, d0 = rms_back_rows(inputs[at], g0, grad)
        gin[at] = gin[at] + part
        return state + d0

    dg0[...] = by_rows(rows, rows_in, jnp.zeros((1, D), F32))
    for n in range(4, n_dp - 1):
        hop(n)
    out.whole(sum_o)
    hop(n_dp - 1)
    net.close()


def close(n_dp, n_mp, seq_grad, seq_normed, q, k, v, mixed, wo, wq, wkv, cosine, sine, marks_col, marks_row,
          inputs, gains, ghid):
    rows = inputs.shape[0]
    nj = n_dp // 2
    wrows = D // n_dp
    cols, kv_cols = q.shape[1], k.shape[1]
    seq_len = q.shape[0]
    count = 16 + 6 * nj + 4 * n_dp
    vm = lambda *shape: pltpu.VMEM(shape, BF)
    small = jax.ShapeDtypeStruct((wrows, cols), F32)
    return call(
        functools.partial(close_kernel, n_dp, n_mp),
        [
            jax.ShapeDtypeStruct((rows, D), F32), jax.ShapeDtypeStruct((1, D), F32), small,
            jax.ShapeDtypeStruct((wrows, 2 * kv_cols), F32), small,
        ],
        [VMEM] * 5,
        [ANY, ANY] + [VMEM] * 4 + [ANY, ANY] + [VMEM] * 7 + [ANY],
        [
            vm(seq_len, D), vm(seq_len, D), vm(D, cols), vm(seq_len, cols), vm(seq_len, cols),
            pltpu.VMEM((seq_len, kv_cols), F32), pltpu.VMEM((seq_len, kv_cols), F32), vm(seq_len, 2 * kv_cols),
            vm(nj, 2, wrows, cols), vm(D, cols), vm(D, 2 * kv_cols),
            vm(n_dp - 1, wrows, cols), vm(n_dp - 1, wrows, 2 * kv_cols), vm(2, rows, D), vm(rows, D),
        ]
        + scatter_scratch(nj, wrows, cols) + [dma(count), dma(count), dma(10 + 2 * nj)],
        6, 60,
    )(seq_grad, seq_normed, q, k, v, mixed, wo, wq, wkv, cosine, sine, marks_col, marks_row,
      inputs, gains, ghid)


def plain(kernel, grid, outs, out_specs, in_specs, mb, flops):
    return pl.pallas_call(
        kernel,
        out_shape=outs,
        grid=grid,
        in_specs=in_specs,
        out_specs=out_specs,
        compiler_params=pltpu.CompilerParams(
            dimension_semantics=("arbitrary",) * len(grid), vmem_limit_bytes=mb << 20
        ),
        cost_estimate=pl.CostEstimate(flops=flops, bytes_accessed=40 << 20, transcendentals=0),
    )


def whole(shape):
    return pl.BlockSpec(shape, lambda t: (0,) * len(shape), pipeline_mode=pl.Buffered(1))


def tile(rows, cols):
    return pl.BlockSpec((None, rows, cols), lambda t: (t, 0, 0))


GELU = math.sqrt(2.0 / math.pi)


def down_back_kernel(grad, gate, up, wg, wu, wd, dgate, dup, part):
    ga = mm(grad[...], wd[...])
    g = gate[...]
    square = g * g
    bend = jnp.tanh(GELU * (g + 0.044715 * (square * g)))
    halved = 0.5 * (1.0 + bend)
    slope = halved + (0.5 * GELU) * g * (1.0 - bend * bend) * (1.0 + (3.0 * 0.044715) * square)
    dg = (ga * up[...] * slope).astype(BF)
    du = (ga * (g * halved)).astype(BF)
    dgate[...] = dg
    dup[...] = du
    part[...] = (mm_cols(dg, wg[...]) + mm_cols(du, wu[...])).astype(BF)


def mlp_back(grad, gate, up, wg, wu, wd):
    blocks, rows, _ = grad.shape
    width = wg.shape[1]
    shape = (blocks, rows, width)
    return plain(
        down_back_kernel, (blocks,),
        [jax.ShapeDtypeStruct(shape, BF), jax.ShapeDtypeStruct(shape, BF), jax.ShapeDtypeStruct((blocks, rows, D), BF)],
        [tile(rows, width), tile(rows, width), tile(rows, D)],
        [tile(rows, D), tile(rows, width), tile(rows, width)] + [whole(wg.shape)] * 3, 56,
        6 * blocks * rows * D * width,
    )(grad, gate, up, wg, wu, wd)


def norm_kernel(
    n_dp, n_mp, terms, g_gate, g_up, g_down, g_q, g_o, g_kv, gain_sum, norm, *refs,
):
    grads, (got, sgot, mine, ss, rs, ls) = refs[:6], refs[6:]
    net = Net(n_dp, n_mp, ss, rs, ls)
    others = everyone(n_dp, n_mp, net.i, net.m)
    loads = [net.move(src, dst) for src, dst in zip((g_gate, g_up, g_down, g_q, g_o, g_kv), grads)]
    net.meet(others)
    flat = net.i * n_mp + net.m
    copies = [net.send(terms.at[dp * n_mp + mp], got.at[flat], (dp, mp)) for dp, mp in others]
    own = net.move(terms.at[flat], got.at[flat])
    square = jnp.zeros((8, 128), F32)
    for load, grad in zip(loads, grads):
        load.wait()
        rows, cols = grad.shape

        def add(t, state, grad=grad, cols=cols):
            value = grad[pl.ds(pl.multiple_of(t * 8, 8), 8)]
            value = value * value
            for n in range(0, cols, 128):
                state = state + value[:, n : n + 128]
            return state

        square = lax.fori_loop(0, rows // 8, add, square)
    own.wait()
    for copy in copies:
        copy.wait_recv()
    gain = lax.fori_loop(0, n_dp * n_mp, lambda t, s: s + got[t], jnp.zeros(got.shape[1:], F32))
    gain_sum[...] = gain
    mine[...] = square + jnp.sum(gain * gain) * (1.0 / 1024.0)
    copies = [net.send(mine, sgot.at[flat], device) for device in others]
    own = net.move(mine, sgot.at[flat])
    own.wait()
    for copy in copies:
        copy.wait_recv()
    total = lax.fori_loop(0, n_dp * n_mp, lambda t, s: s + sgot[t], jnp.zeros((8, 128), F32))
    norm[...] = jnp.broadcast_to(jnp.sqrt(jnp.sum(total, axis=(0, 1), keepdims=True)), (8, 128))
    net.close()


def norm_all(n_dp, n_mp, terms, grads):
    total = n_dp * n_mp
    shape = terms.shape[1:]
    return call(
        functools.partial(norm_kernel, n_dp, n_mp),
        [jax.ShapeDtypeStruct(shape, F32), jax.ShapeDtypeStruct((8, 128), F32)],
        [VMEM] * 2, [VMEM] + [ANY] * 6,
        [pltpu.VMEM(a.shape, F32) for a in grads]
        + [
            pltpu.VMEM((total,) + shape, F32), pltpu.VMEM((total, 8, 128), F32), pltpu.VMEM((8, 128), F32),
            dma(2 * total), dma(2 * total), dma(8),
        ],
        7, 32,
    )(terms, *grads)


def adam_kernel(norm, gain_grad, gw, gm, gv, g_gate, g_up, g_down, g_q, g_o, g_kv, *refs):
    ins, gain_outs, outs = refs[:9], refs[9:12], refs[12:]
    factor = jnp.minimum(1.0, CLIP_SCALE * math.sqrt(PARAMS) / norm[0:1, 0:1])
    news = adam_update(gw[...], gm[...], gv[...], gain_grad[...], factor)
    for out, new in zip(gain_outs, news):
        out[...] = new
    kv_cols = ins[6].shape[2]
    grads = (
        (lambda: g_gate[...], lambda: g_up[...], lambda: g_down[...]),
        (lambda: g_q[...], lambda: g_o[...]),
        (lambda: g_kv[:, :kv_cols], lambda: g_kv[:, kv_cols:]),
    )
    for n, group in enumerate(grads):
        w, m, v = ins[3 * n : 3 * n + 3]
        for k, grad in enumerate(group):
            news = adam_update(w[k], m[k], v[k], grad(), factor)
            for out, new in zip(outs[3 * n : 3 * n + 3], news):
                out[k] = new


def adam_all(norm, gain_grad, gains, grads, states):
    wrows = grads[0].shape[0]
    step = 48 if wrows % 48 == 0 else 8
    like = lambda a: jax.ShapeDtypeStruct(a.shape, F32)
    fixed = lambda a: pl.BlockSpec(a.shape, lambda t: (0, 0))
    flat = lambda a: pl.BlockSpec((step, a.shape[1]), lambda t: (t, 0))
    deep = lambda a: pl.BlockSpec((a.shape[0], step, a.shape[2]), lambda t: (0, t, 0))
    return plain(
        adam_kernel, (wrows // step,), [like(a) for a in gains] + [like(a) for a in states],
        [fixed(a) for a in gains] + [deep(a) for a in states],
        [fixed(a) for a in (norm, gain_grad) + tuple(gains)] + [flat(a) for a in grads] + [deep(a) for a in states],
        56, 100,
    )(norm, gain_grad, *gains, *grads, *states)


def build_local(n_dp, n_mp):
    nj = n_dp // 2

    def y_swap(value):
        return lax.ppermute(value, "dp", [(k, k ^ 1) for k in range(n_dp)])

    def z_shift(value, d):
        pairs = [(a * 2 + b, ((a + d) % nj) * 2 + b) for a in range(nj) for b in range(2)]
        return lax.ppermute(value, "dp", pairs)

    def scatter_first(grad, y):
        away = lax.dynamic_index_in_dim(grad, 1 - y, 1, keepdims=False)
        stay = lax.dynamic_index_in_dim(grad, y, 1, keepdims=False)
        return stay, y_swap(away)

    def scatter_second(stay, came, j):
        both = (stay.astype(F32) + came.astype(F32)).astype(BF)
        both = [lax.dynamic_index_in_dim(both, (j + d) % nj, 0, keepdims=False) for d in range(nj)]
        return both[0], [z_shift(both[d], d) for d in range(1, nj)]

    def local(
        inputs, out_grad, segment_ids, pad_mask, bit_sel, w_qo, w_kv, w_mlp, norm_gains,
        m_qo, m_kv, m_mlp, m_gains, v_qo, v_kv, v_mlp, v_gains,
    ):
        i, m = lax.axis_index("dp"), lax.axis_index("mp")
        y, j = i % 2, i // 2
        zl = j % 2
        rows = inputs.shape[0]
        seq_len = segment_ids.shape[1]
        wrows = w_qo.shape[1]

        low_q = quantize(w_qo[0], D, bit_sel[0])
        low_o = quantize(w_qo[1], QW, bit_sel[0])
        low_kv = jnp.concatenate([quantize(w_kv[0], D, bit_sel[1]), quantize(w_kv[1], D, bit_sel[1])], 1)
        order = jnp.stack([m, m ^ 2, m ^ 1, m ^ 3])

        def in_order(vector):
            return vector.reshape(n_mp, rows)[order].reshape(-1)

        segments = segment_ids[0]
        positions = in_order(doc_positions(segments))
        slots = in_order(jnp.arange(seq_len, dtype=jnp.int32))
        segs = in_order(segments)
        pads = in_order(pad_mask[0])
        kv_cols = w_kv.shape[2]
        half_dim = HEAD_WIDTH // 2
        frequency = ROPE_BASE ** (-jnp.arange(half_dim, dtype=F32) * 2.0 / HEAD_WIDTH)
        angles = positions.astype(F32)[:, None] * frequency[None, :]
        cosine = jnp.cos(angles)
        sine = jnp.sin(angles)
        marks = jnp.stack([segs, slots, pads] + [segs] * 5)
        (
            query_bf, key_bf, value_bf, mixed_bf, attended, hidden_in, gain_rows, group_ffn, w_gate, w_up, w_down,
            wq, wkv, wo, seq_normed,
        ) = open_layer(
            n_dp, n_mp, low_q, low_kv, low_o, w_mlp, code_spacing(bit_sel[2]).reshape(1, 1), cosine, sine,
            marks.T, marks, inputs, norm_gains.reshape(1, -1),
        )
        w_gate, w_up, w_down = w_gate.reshape(D, -1), w_up.reshape(D, -1), w_down.reshape(D, -1)
        live = lax.dynamic_slice_in_dim(pad_mask[0], m * rows, rows).astype(F32)[:, None]
        outputs, grad_gain_three, gate, up, activated, group_grad = turn(
            n_dp, n_mp, group_ffn, w_gate, w_up, w_down, hidden_in, gain_rows, out_grad, live
        )
        tokens = 8 * rows
        grad_down = mm_rows(group_grad.reshape(tokens, D), activated.reshape(tokens, -1))
        grad_down = grad_down.astype(BF).reshape(nj, 2, wrows, -1)
        grad_down, group_grad = lax.optimization_barrier((grad_down, group_grad))
        down_stay, down_came = scatter_first(grad_down, y)
        grad_gate, grad_up, part = mlp_back(group_grad, gate, up, w_gate, w_up, w_down)
        flat_ffn = group_ffn.reshape(tokens, D)
        grads_gate = mm_rows(flat_ffn, grad_gate.reshape(tokens, -1)).astype(BF).reshape(nj, 2, wrows, -1)
        grads_gate, grad_up, down_came = lax.optimization_barrier((grads_gate, grad_up, down_came))
        down_own, down_shifted = scatter_second(down_stay, down_came, j)
        grads_up = mm_rows(flat_ffn, grad_up.reshape(tokens, -1)).astype(BF).reshape(nj, 2, wrows, -1)
        grad_hidden, grad_gain_one, grad_gain_two, seq_grad, sum_gate, sum_up = back(
            n_dp, n_mp, part, hidden_in, attended, gain_rows, out_grad, live,
            grads_gate, grads_up
        )
        seq_grad, down_shifted = lax.optimization_barrier((seq_grad, down_shifted))
        sums = [down_own.astype(F32), 0.0]
        for d in range(1, nj):
            sums[d % 2] = sums[d % 2] + down_shifted[d - 1].astype(F32)
        sum_down = jnp.concatenate(
            [jnp.where(zl == 0, sums[0], sums[1]), jnp.where(zl == 0, sums[1], sums[0])], 1
        )
        grad_in, grad_gain_zero, sum_q, sum_kv, sum_o = close(
            n_dp, n_mp, seq_grad.reshape(seq_len, D), seq_normed, query_bf, key_bf, value_bf, mixed_bf,
            wo, wq, wkv, cosine, sine, marks.T, marks, inputs, gain_rows, grad_hidden,
        )
        terms = jnp.concatenate([grad_gain_zero, grad_gain_one, grad_gain_two, grad_gain_three])
        flat_gains = [a.reshape(1, -1) for a in (norm_gains, m_gains, v_gains)]
        sums = [sum_gate, sum_up, sum_down, sum_q, sum_o, sum_kv]
        sum_gains, norm = norm_all(n_dp, n_mp, terms.reshape(n_dp * n_mp, 1, -1), sums)
        news = adam_all(
            norm, sum_gains, flat_gains, sums, [w_mlp, m_mlp, v_mlp, w_qo, m_qo, v_qo, w_kv, m_kv, v_kv]
        )
        grad_norm = norm[0, :1]
        new_gains, new_m_gains, new_v_gains = [a.reshape(-1) for a in news[:3]]
        new_w_mlp, new_m_mlp, new_v_mlp, new_w_qo, new_m_qo, new_v_qo, new_w_kv, new_m_kv, new_v_kv = news[3:]
        return (
            outputs, grad_in, grad_norm, new_w_qo, new_w_kv, new_w_mlp, new_gains,
            new_m_qo, new_m_kv, new_m_mlp, new_m_gains, new_v_qo, new_v_kv, new_v_mlp, new_v_gains,
        )

    return local


def solution(mesh):
    tokens = P(("dp", "mp"), None)
    weight = P(None, "dp", "mp")
    flat = P(("dp", "mp"))
    per_weight = (weight, weight, weight, flat)
    return jax.shard_map(
        build_local(mesh.shape["dp"], mesh.shape["mp"]),
        mesh=mesh,
        in_specs=(tokens, tokens, P("dp", None), P("dp", None), P()) + per_weight * 3,
        out_specs=(tokens, tokens, P()) + per_weight * 3,
        check_vma=False,
    )
```

```python
import functools
import math

import jax
import jax.numpy as jnp
from jax import lax
from jax.experimental import pallas as pl
from jax.experimental.pallas import tpu as pltpu
from jax.sharding import PartitionSpec as P

D = 2304
HEAD_WIDTH = 256
FF = 9216
NORMS = 4
QW = 2048
PARAMS = 77865984

EPSILON = 1e-06
SOFT_CAP = 50.0
ROPE_BASE = 10000.0
MASKED_SCORE = -1e30
FIRST_DECAY = 0.9
SECOND_DECAY = 0.95
LEARN_RATE = 0.04
WEIGHT_DECAY = 0.1
ADAM_EPSILON = 1e-08
CLIP_SCALE = 0.5

BF = jnp.bfloat16
F32 = jnp.float32


def code_spacing(selector):
    return jnp.where(selector == 0, 1.0, jnp.where(selector == 1, 16.0, 64.0)).astype(F32)


def quantize_values(master, step, spacing):
    half = jnp.floor(spacing * 0.5)
    inverse = jnp.where(spacing > 32.0, 1.0 / 64.0, jnp.where(spacing > 8.0, 1.0 / 16.0, 1.0))
    codes = jnp.clip(jnp.floor(master / step + 0.5), -128.0, 127.0)
    top = 128.0 * inverse
    sliced = jnp.clip(jnp.floor((codes + half) * inverse), -top, top - 1.0)
    return (sliced * spacing) * step


def quantize(master, fan_in, selector):
    step = jnp.float32(1.0 / (32.0 * math.sqrt(fan_in)))
    return quantize_values(master, step, code_spacing(selector)).astype(BF)


def inv_root(values):
    return lax.rsqrt(jnp.mean(values * values, axis=-1, keepdims=True) + EPSILON)


def rms_norm(values, norm_gain):
    return values * inv_root(values) * (1.0 + norm_gain)


def rms_back(values, norm_gain, grad):
    root = inv_root(values)
    scaled = grad * (1.0 + norm_gain)
    dot = jnp.mean(values * scaled, axis=-1, keepdims=True)
    grad_values = root * scaled - values * (root * root * root * dot)
    grad_gain = jnp.sum(values * root * grad, axis=0)
    return grad_values, grad_gain


def mm(left, right):
    return lax.dot_general(left, right, (((1,), (0,)), ((), ())), preferred_element_type=F32)


def mm_rows(left, right):
    return lax.dot_general(left, right, (((0,), (0,)), ((), ())), preferred_element_type=F32)


def mm_cols(left, right):
    return lax.dot_general(left, right, (((1,), (1,)), ((), ())), preferred_element_type=F32)


def adam_update(master, first_moment, second_moment, gradient, factor):
    clipped = gradient * factor
    new_first = FIRST_DECAY * first_moment + (1.0 - FIRST_DECAY) * clipped
    new_second = SECOND_DECAY * second_moment + (1.0 - SECOND_DECAY) * clipped * clipped
    new_master = master - LEARN_RATE * (
        new_first / (jnp.sqrt(new_second) + ADAM_EPSILON) + WEIGHT_DECAY * master
    )
    return (new_master, new_first, new_second)


MESH = pl.DeviceIdType.MESH
ANY = pl.BlockSpec(memory_space=pl.ANY)
VMEM = pl.BlockSpec(memory_space=pltpu.VMEM)
ROWS = 32


class Net:
    def __init__(self, n_dp, n_mp, send_sems, recv_sems, local_sems=None):
        self.n_dp, self.n_mp = n_dp, n_mp
        self.send_sems, self.recv_sems, self.local_sems = send_sems, recv_sems, local_sems
        self.used, self.used_local, self.open = 0, 0, []
        self.i, self.m = lax.axis_index("dp"), lax.axis_index("mp")
        self.y, self.j = self.i % 2, self.i // 2
        self.zl = self.j % 2
        self.c, self.x = self.m % 2, self.m // 2
        self.core_n = (self.i, self.m + 1 - 2 * self.c)
        self.x_n = (self.i, (self.m + 2) % 4)
        self.y_n = (self.i + 1 - 2 * self.y, self.m)
        self.z_n = (self.i + 2 - 4 * self.zl, self.m)

    def z_at(self, d):
        nj = self.n_dp // 2
        return (((self.j + d) % nj) * 2 + self.y, self.m)

    def place(self):
        return (1 - self.y) * self.j + self.y * (self.n_dp - 1 - self.j)

    def ring(self, at):
        n, nj = self.n_dp, self.n_dp // 2
        at = at % n
        late = at // nj
        return (1 - late) * 2 * at + late * (2 * (n - 1 - at) + 1)

    def meet(self, devices):
        barrier = pltpu.get_barrier_semaphore()
        for device in devices:
            pl.semaphore_signal(barrier, inc=1, device_id=device, device_id_type=MESH)
        pl.semaphore_wait(barrier, len(devices))

    def send(self, src, dst, device):
        at = self.used
        self.used += 1
        copy = pltpu.make_async_remote_copy(
            src_ref=src, dst_ref=dst, send_sem=self.send_sems.at[at], recv_sem=self.recv_sems.at[at],
            device_id=device, device_id_type=MESH,
        )
        copy.start()
        self.open.append((copy, copy.wait_send))
        return copy

    def family(self, count, make):
        base = self.used
        self.used += count

        def copy_of(k):
            return make(k, self.send_sems.at[base + k], self.recv_sems.at[base + k])

        for k in range(count):
            copy = copy_of(k)
            self.open.append((copy, copy.wait_send))
        return copy_of

    def locals(self, count):
        base = self.used_local
        self.used_local += count
        return base

    def sent(self, copy):
        copy.wait_send()
        self.open = [entry for entry in self.open if entry[0] is not copy]

    def move(self, src, dst):
        at = self.used_local
        self.used_local += 1
        copy = pltpu.make_async_copy(src, dst, self.local_sems.at[at])
        copy.start()
        return copy

    def keep(self, src, dst):
        copy = self.move(src, dst)
        self.open.append((copy, copy.wait))

    def close(self):
        for _, wait in self.open:
            wait()


def upper(count):
    return count // 16 * 8


def dma(n):
    return pltpu.SemaphoreType.DMA((n,))


def call(kernel, outs, out_specs, in_specs, scratch, cid, mb, flops=0):
    return pl.pallas_call(
        kernel,
        out_shape=outs,
        in_specs=in_specs,
        out_specs=out_specs,
        scratch_shapes=scratch,
        compiler_params=pltpu.CompilerParams(
            collective_id=cid, has_side_effects=True, vmem_limit_bytes=mb << 20
        ),
    )


def by_rows(total, body, carry=0):
    return lax.fori_loop(
        0, total // ROWS, lambda t, state: body(pl.ds(pl.multiple_of(t * ROWS, ROWS), ROWS), state), carry
    )


def everyone(n_dp, n_mp, i, m):
    flat = i * n_mp + m
    total = n_dp * n_mp
    return [(((flat + t) % total) // n_mp, (flat + t) % n_mp) for t in range(1, total)]


def gather_seq_steps(net, own, seq):
    far = net.send(own, seq.at[1], net.x_n)
    near = net.send(own, seq.at[2], net.core_n)
    net.keep(own, seq.at[0])

    def finish():
        far.wait_recv()
        both = net.send(seq.at[1], seq.at[3], net.core_n)
        near.wait_recv()
        both.wait_recv()

    return finish


def gather_pair_steps(net, own, group, split=False):
    far = net.send(own, group.at[2], net.x_n)
    zed = net.send(own, group.at[1], net.z_n)
    near = net.send(own, group.at[4], net.core_n)
    net.keep(own, group.at[0])

    def finish(between=lambda: None):
        head = pl.ds(0, D // 2) if split else pl.ds(0, D)
        rest = pl.ds(D // 2, D // 2)
        zed.wait_recv()
        both = net.send(group.at[1, :, head], group.at[3, :, head], net.x_n)
        far.wait_recv()
        if split:
            other = net.send(group.at[2, :, rest], group.at[3, :, rest], net.z_n)
        near_z = net.send(group.at[1], group.at[5], net.core_n)
        near_x = net.send(group.at[2], group.at[6], net.core_n)
        between()
        both.wait_recv()
        if split:
            other.wait_recv()
        near_both = net.send(group.at[3], group.at[7], net.core_n)
        for copy in (near, near_z, near_x, near_both):
            copy.wait_recv()

    return finish


def pair_partners(net, with_y):
    nj = net.n_dp // 2
    zs = [net.z_at(d) for d in range(1, nj)] if with_y else [net.z_n]
    return [net.core_n, net.x_n] + zs + ([net.y_n] if with_y else [])


def row_tiles(total, size, body):
    lax.fori_loop(
        0, total // size, lambda t, state: (body(pl.ds(pl.multiple_of(t * size, size), size)), state)[1], 0
    )


def project(seq, wq, wkv, cosine, sine, q, k, v):
    total = seq.shape[0]
    kv_cols = k.shape[1]
    half = HEAD_WIDTH // 2

    def body(at):
        tokens = seq[at]
        c, s = cosine[at], sine[at]

        def turn(lin, out, cols):
            for h in range(0, cols, HEAD_WIDTH):
                a, b = lin[:, h : h + half], lin[:, h + half : h + HEAD_WIDTH]
                out[at, h : h + half] = (a * c - b * s).astype(BF)
                out[at, h + half : h + HEAD_WIDTH] = (b * c + a * s).astype(BF)

        turn(mm(tokens, wq[...]), q, q.shape[1])
        lin = mm(tokens, wkv[...])
        turn(lin, k, kv_cols)
        v[at] = lin[:, kv_cols:].astype(BF)

    row_tiles(total, total // 2, body)


def allowed_tile(marks_col, marks_row, at):
    segs, slots = marks_col[at, 0:1], marks_col[at, 1:2]
    seg_row, slot_row, pad_row = marks_row[0:1], marks_row[1:2], marks_row[2:3]
    same_slot = slot_row == slots
    return (seg_row == segs) & (slot_row <= slots) & ((pad_row == 1) | same_slot)


def tile_probs(q, k, allowed, at, head, group):
    cols = slice(head * HEAD_WIDTH, (head + 1) * HEAD_WIDTH)
    kv = head // group
    kv_at = slice(kv * HEAD_WIDTH, (kv + 1) * HEAD_WIDTH)
    bent = jnp.tanh(mm_cols(q[at, cols], k[:, kv_at]) * (HEAD_WIDTH**-0.5 / SOFT_CAP))
    raised = jnp.where(allowed, jnp.exp(SOFT_CAP * bent), 0.0)
    return bent, raised * (1.0 / jnp.sum(raised, axis=-1, keepdims=True))


def attend(q, k, v, marks_col, marks_row, mixed):
    total = q.shape[0]
    heads, group = q.shape[1] // HEAD_WIDTH, q.shape[1] // k.shape[1]

    def body(at):
        allowed = allowed_tile(marks_col, marks_row, at)
        for head in range(heads):
            _, probs = tile_probs(q, k, allowed, at, head, group)
            kv = head // group
            kv_at = slice(kv * HEAD_WIDTH, (kv + 1) * HEAD_WIDTH)
            mixed[at, head * HEAD_WIDTH : (head + 1) * HEAD_WIDTH] = mm(
                probs.astype(BF), v[:, kv_at]
            ).astype(BF)

    row_tiles(total, 128, body)


def out_project(mixed, wo, part):
    blocks, rows, _ = part.shape
    wide = D // 3
    for pair in range(blocks // 2 - 1, -1, -1):
        for n in range(0, D, wide):
            got = mm_cols(mixed[pair * 2 * rows : (pair + 1) * 2 * rows], wo[n : n + wide]).astype(BF)
            part[pair * 2, :, n : n + wide] = got[:rows]
            part[pair * 2 + 1, :, n : n + wide] = got[rows:]


def chunks(wrows):
    if wrows % 48 == 0:
        return tuple((n * wrows // 3, wrows // 3) for n in range(3))
    return ((0, upper(wrows)), (upper(wrows), wrows - upper(wrows)))


def two_parts(wrows):
    return ((0, upper(wrows)), (upper(wrows), wrows - upper(wrows)))


class Gather:
    def __init__(self, net, pieces):
        self.net, self.pieces, self.nj = net, pieces, net.n_dp // 2
        self.flight, self.relays, self.own = {}, {}, {}

    def out(self, n):
        net = self.net
        source, place, parity = self.pieces[n]
        self.own[n] = net.move(source(net.zl), place(net.i))
        self.relays[n] = [net.send(source(net.zl), place(net.i), net.y_n)]
        for d in range(1, self.nj):
            self.flight[n, d] = net.send(source((net.j + d) % self.nj % 2), place(net.i), net.z_at(d))

    def on(self, n):
        net = self.net
        _, place, _ = self.pieces[n]
        for d in range(1, self.nj):
            self.flight[n, d].wait_recv()
            at = ((net.j + self.nj - d) % self.nj) * 2 + net.y
            self.relays[n].append(net.send(place(at), place(at), net.y_n))

    def done(self, n):
        self.own.pop(n).wait()
        for copy in self.relays.pop(n):
            copy.wait_recv()


def all_of_dp(net):
    return [net.x_n, net.core_n] + [((net.i + t) % net.n_dp, net.m) for t in range(1, net.n_dp)]


def open_kernel(
    n_dp, n_mp, low_q, low_kv, low_o, w_mlp, width_mlp, cosine, sine, marks_col, marks_row, inputs, own_gains,
    q, k, v, mixed, att, hid, gains, group, full0, full1, full2, out_q, out_kv, out_o, out_seq,
    wq, wkv, wo, seq, part, r1, r2, own, got_gains, masters, lows, ss, rs, ls,
):
    net = Net(n_dp, n_mp, ss, rs, ls)
    p = net.place()
    right = (net.ring(p + 1), net.m)
    left = (net.ring(p + n_dp - 1), net.m)
    rows = inputs.shape[0]
    wrows, width = full0.shape[1:]
    others = everyone(n_dp, n_mp, net.i, net.m)
    net.meet(others)
    flat = net.i * n_mp + net.m
    loads = [net.move(w_mlp.at[n], masters.at[n]) for n in range(3)]

    def block(ref, at):
        return ref.at[pl.ds(pl.multiple_of(at * wrows, 8), wrows)]

    def lot(n):
        return seq.at[pl.ds(n * rows, rows)]

    def piece(ref, at, part):
        first, count = part
        return ref.at[pl.ds(pl.multiple_of(at * wrows + first, 8), count)]

    parts = two_parts(wrows)
    flight = {}
    for cut in parts:
        for lane, (ref, low, device) in enumerate(((wq, low_q, right), (wkv, low_kv, left))):
            flight[cut, lane] = net.send(low.at[pl.ds(*cut)], piece(ref, net.i, cut), device)
    spread = [net.send(own_gains, got_gains.at[flat], device) for device in others]
    net.move(own_gains, got_gains.at[flat]).wait()
    for copy in spread:
        copy.wait_recv()
    per_norm = n_dp * n_mp // NORMS
    for n in range(NORMS):
        gains[n : n + 1] = jnp.concatenate([got_gains[n * per_norm + t] for t in range(per_norm)], 1)
    g0 = 1.0 + gains[0:1]

    def norm_rows(at, state):
        own[at] = (inputs[at] * inv_root(inputs[at]) * g0).astype(BF)
        return state

    by_rows(rows, norm_rows)
    far = net.send(own, lot(1), net.x_n)
    near = net.send(own, lot(2), net.core_n)

    def quantize_part(n):
        loads[n].wait()
        spacing = width_mlp[...]
        step = jnp.float32(1.0 / (32.0 * math.sqrt(FF if n == 2 else D)))

        def body(at, state, count):
            lows[n, at] = quantize_values(masters[n, at], step, spacing).astype(BF)
            return state

        in_steps(wrows, body)

    own_parts = [net.move(own, lot(0)), net.move(low_q, block(wq, net.i)), net.move(low_kv, block(wkv, net.i))]
    half = lambda which: pl.ds(pl.multiple_of(which * width, width), width)
    pieces = [(lambda which: low_o, lambda at: block(wo, at), 1)]

    def add_piece(ref, full, first, count):
        rows_at = pl.ds(first, count)
        pieces.append((lambda which: ref.at[rows_at, half(which)], lambda at: full.at[at, rows_at], 2))

    for ref, full in ((lows.at[0], full0), (lows.at[1], full1), (lows.at[2], full2)):
        for first, count in chunks(wrows):
            add_piece(ref, full, first, count)
    weights = Gather(net, pieces)
    for hop in range(1, n_dp):
        from_right, from_left = net.ring(p + n_dp - hop), net.ring(p + hop)
        for cut in parts:
            for lane, (ref, at, device) in enumerate(((wq, from_right, right), (wkv, from_left, left))):
                flight[cut, lane].wait_recv()
                if hop < n_dp - 1:
                    flight[cut, lane] = net.send(piece(ref, at, cut), piece(ref, at, cut), device)
        if hop == n_dp // 2:
            far.wait_recv()
            both = net.send(lot(1), lot(3), net.core_n)
        if hop in (1, 2, 3):
            quantize_part(hop - 1)
        if hop == n_dp - 2:
            weights.out(0)
    weights.out(1)
    weights.out(2)
    weights.out(3)
    near.wait_recv()
    both.wait_recv()
    for copy in own_parts:
        copy.wait()
    net.sent(far)
    net.sent(near)
    for ref, result in ((wq, out_q), (wkv, out_kv), (seq, out_seq)):
        net.keep(ref, result)
    project(seq, wq, wkv, cosine, sine, q, k, v)
    attend(q, k, v, marks_col, marks_row, mixed)
    def step(n):
        if n < len(pieces):
            weights.on(n)
            if n + 4 < len(pieces):
                weights.out(n + 4)

    step(0)
    weights.done(0)
    net.keep(wo, out_o)
    out_project(mixed, wo, part)
    c1 = net.send(part.at[3], r1.at[1], net.core_n)
    c0 = net.send(part.at[2], r1.at[0], net.core_n)
    c1.wait_recv()

    def first_rows(at, state):
        part[1, at] = (part[1, at].astype(F32) + r1[1, at].astype(F32)).astype(BF)
        return state

    by_rows(rows, first_rows)
    x = net.send(part.at[1], r2, net.x_n)
    c0.wait_recv()
    step(1)
    x.wait_recv()
    g1, g2 = 1.0 + gains[1:2], 1.0 + gains[2:3]

    def second(at, state):
        total = part[0, at].astype(F32) + r1[0, at].astype(F32) + r2[at].astype(F32)
        att[at] = total
        hidden = inputs[at] + total * inv_root(total) * g1
        hid[at] = hidden
        own[at] = (hidden * inv_root(hidden) * g2).astype(BF)
        return state

    by_rows(rows, second)
    finish = gather_pair_steps(net, own, group)
    step(2)
    step(3)
    finish(lambda: (step(4), step(5)))
    for n in range(6, len(pieces)):
        step(n)
    for n in range(1, len(pieces)):
        weights.done(n)
    net.close()


def open_layer(n_dp, n_mp, low_q, low_kv, low_o, w_mlp, width_mlp, cosine, sine, marks_col, marks_row, inputs, gains):
    rows = inputs.shape[0]
    nj = n_dp // 2
    total_devices = n_dp * n_mp
    count = 24 + 4 * n_dp + 20 * nj + total_devices
    block = (rows, D)
    wrows, width = w_mlp.shape[1], w_mlp.shape[2] // 2
    cols, kv_cols = low_q.shape[1], low_kv.shape[1] // 2
    vm = lambda *shape: pltpu.VMEM(shape, BF)
    bf = lambda *shape: jax.ShapeDtypeStruct(shape, BF)
    total = 4 * rows
    f32 = jax.ShapeDtypeStruct(block, F32)
    full = bf(n_dp, wrows, width)
    return call(
        functools.partial(open_kernel, n_dp, n_mp),
        [
            bf(total, cols), bf(total, kv_cols), bf(total, kv_cols), bf(total, cols), f32, f32,
            jax.ShapeDtypeStruct((NORMS, D), F32),
            bf(8, *block), full, full, full, bf(D, cols), bf(D, 2 * kv_cols), bf(D, cols), bf(total, D),
        ],
        [VMEM] * 7 + [ANY] * 8, [ANY] * 4 + [VMEM] * 7,
        [
            vm(D, cols), vm(D, 2 * kv_cols), vm(D, cols), vm(total, D), vm(4, *block), vm(2, *block), vm(*block),
            vm(*block), pltpu.VMEM((total_devices,) + gains.shape, F32), pltpu.VMEM(w_mlp.shape, F32),
            vm(*w_mlp.shape), dma(count), dma(count), dma(32),
        ],
        2, 60,
    )(low_q, low_kv, low_o, w_mlp, width_mlp, cosine, sine, marks_col, marks_row, inputs, gains)


def reduce_pair_steps(net, near, cores, r1, r2, r3, rows, split=False, compute=None, hooks=None):
    plan = [(pl.ds(0, D // 2 if split else D), (3, 2), net.x_n, 1, net.z_n)]
    if split:
        plan.append((pl.ds(D // 2, D // 2), (3, 1), net.z_n, 2, net.x_n))
    firsts = {}
    for k in (3, 2, 1) if split else (3, 2):
        compute(k)
        cores(k).wait_recv()
        for part, (cols, blocks, device, _, _) in enumerate(plan):
            if k not in blocks:
                continue
            at_block = blocks.index(k)

            def add(at, state, k=k, cols=cols):
                near[k, at, cols] = (near[k, at, cols].astype(F32) + r1[k, at, cols].astype(F32)).astype(BF)
                return state

            by_rows(rows, add)
            firsts[part, at_block] = net.send(near.at[k, :, cols], r2.at[at_block, :, cols], device)
    for k in (0,) if split else (1, 0):
        compute(k)
        cores(k).wait_recv()
    last = []
    if hooks:
        hooks[0]()
    for part, (cols, blocks, _, second, device) in enumerate(plan):
        firsts[part, 0].wait_recv()

        def add(at, state, cols=cols, second=second):
            near[second, at, cols] = (
                near[second, at, cols].astype(F32) + r1[second, at, cols].astype(F32) + r2[0, at, cols].astype(F32)
            ).astype(BF)
            return state

        by_rows(rows, add)
        last.append(net.send(near.at[second, :, cols], r3.at[:, cols], device))
    if hooks:
        hooks[1]()
    for part in range(len(plan)):
        firsts[part, 1].wait_recv()
    return last


def pair_sum(near, r1, r2, r3, at):
    return near[0, at].astype(F32) + r1[0, at].astype(F32) + r2[1, at].astype(F32) + r3[at].astype(F32)


def pair_scratch(rows, blocks=8):
    block = (rows, D)
    return [
        pltpu.VMEM((blocks,) + block, BF), pltpu.VMEM((4,) + block, BF), pltpu.VMEM((2,) + block, BF),
        pltpu.VMEM(block, BF), pltpu.VMEM(block, BF),
    ]


def core_family(net, parts, r1):
    return net.family(
        4,
        lambda k, send, recv: pltpu.make_async_remote_copy(
            src_ref=parts.at[4 + k], dst_ref=r1.at[k], send_sem=send, recv_sem=recv,
            device_id=net.core_n, device_id_type=MESH,
        ),
    )


def block_at(t):
    return 7 - t // 2 - 4 * (t % 2)


class Stream:
    def __init__(self, net, pairs, inward):
        self.net, self.pairs, self.inward = net, pairs, inward
        self.base = net.locals(2 * len(pairs))

    def copies(self, t):
        slot = t % 2
        for n, (far, held) in enumerate(self.pairs):
            ends = (far.at[block_at(t)], held.at[slot])
            yield pltpu.make_async_copy(
                *(ends if self.inward else ends[::-1]), self.net.local_sems.at[self.base + 2 * n + slot]
            )

    def start(self, t):
        for copy in self.copies(t):
            copy.start()

    def wait(self, t):
        for copy in self.copies(t):
            copy.wait()


def rms_back_rows(values, gain, grad):
    root = inv_root(values)
    scaled = grad * gain
    dot = jnp.mean(values * scaled, axis=-1, keepdims=True)
    return root * scaled - values * (root * root * root * dot), jnp.sum(values * root * grad, axis=0, keepdims=True)


def turn_kernel(
    n_dp, n_mp, ffn, w_gate, w_up, w_down, hid, gains, out_grad, live,
    outputs, dgain, gate, up, act, group,
    parts, r1, r2, r3, own, wg, wu, wd, tokens, gate_b, up_b, act_b, ss, rs, ls,
):
    net = Net(n_dp, n_mp, ss, rs, ls)
    loads = [net.move(src, dst) for src, dst in ((w_gate, wg), (w_up, wu), (w_down, wd))]
    rows = hid.shape[0]
    incoming = Stream(net, [(ffn, tokens)], True)
    outgoing = Stream(net, [(gate, gate_b), (up, up_b), (act, act_b)], False)
    cores = core_family(net, parts, r1)
    incoming.start(0)
    net.meet(pair_partners(net, False))
    for load in loads:
        load.wait()

    def block(t, state):
        slot, at = t % 2, block_at(t)
        incoming.wait(t)

        @pl.when(t < 7)
        def _():
            incoming.start(t + 1)

        g = mm(tokens[slot], wg[...])
        u = mm(tokens[slot], wu[...])
        bend = jnp.tanh(GELU * (g + 0.044715 * (g * g * g)))
        a = (0.5 * g * (1.0 + bend) * u).astype(BF)

        @pl.when(t >= 2)
        def _():
            outgoing.wait(t - 2)

        gate_b[slot] = g
        up_b[slot] = u
        act_b[slot] = a
        outgoing.start(t)
        parts[at] = mm_cols(a, wd[...]).astype(BF)
        return state

    def compute(k):
        def both(t, state):
            block(t, state)

            @pl.when(t % 2 == 0)
            def _():
                cores(k).start()

            return state

        lax.fori_loop(6 - 2 * k, 8 - 2 * k, both, 0)

    last_sums = reduce_pair_steps(net, parts, cores, r1, r2, r3, rows, True, compute)
    outgoing.wait(6)
    outgoing.wait(7)
    for copy in last_sums:
        copy.wait_recv()
    g3 = 1.0 + gains[3:4]

    def last(at, state):
        total = pair_sum(parts, r1, r2, r3, at)
        outputs[at] = hid[at] + total * inv_root(total) * g3
        grad, dg = rms_back_rows(total, g3, out_grad[at] * live[at])
        own[at] = grad.astype(BF)
        return state + dg

    dgain[...] = by_rows(rows, last, jnp.zeros((1, D), F32))
    gather_pair_steps(net, own, group, True)()
    net.close()


def turn(n_dp, n_mp, ffn, w_gate, w_up, w_down, hid, gains, out_grad, live):
    rows = hid.shape[0]
    block = (rows, D)
    width = w_gate.shape[1]
    vm = lambda *shape: pltpu.VMEM(shape, BF)
    return call(
        functools.partial(turn_kernel, n_dp, n_mp),
        [
            jax.ShapeDtypeStruct(block, F32), jax.ShapeDtypeStruct((1, D), F32),
            jax.ShapeDtypeStruct((8, rows, width), F32), jax.ShapeDtypeStruct((8, rows, width), F32),
            jax.ShapeDtypeStruct((8, rows, width), BF), jax.ShapeDtypeStruct((8,) + block, BF),
        ],
        [VMEM, VMEM] + [ANY] * 4, [ANY] * 4 + [VMEM] * 4,
        pair_scratch(rows)
        + [
            vm(D, width), vm(D, width), vm(D, width), vm(2, *block),
            pltpu.VMEM((2, rows, width), F32), pltpu.VMEM((2, rows, width), F32), vm(2, rows, width),
            dma(32), dma(32), dma(16),
        ],
        4, 60,
    )(ffn, w_gate, w_up, w_down, hid, gains, out_grad, live)


def in_steps(count, body, carry=0, first=0):
    step = 16 if count % 16 == 0 else 8
    return lax.fori_loop(
        0, count // step,
        lambda t, state: body(pl.ds(pl.multiple_of(first + t * step, 8), step), state, step), carry,
    )


def square_tile(value):
    value = value * value
    total = jnp.zeros((8, 128), F32)
    for r in range(0, value.shape[0], 8):
        for c in range(0, value.shape[1], 128):
            total = total + value[r : r + 8, c : c + 128]
    return total


class Scatter:
    def __init__(self, net, grads, stay, came, last):
        self.net, self.grads, self.stay, self.came, self.last = net, grads, stay, came, last
        self.nj, self.wrows, self.width = came.shape
        self.turns = sorted(range(1, self.nj), key=lambda d: abs(d - self.nj // 2)) + [0]
        self.ys, self.moves, self.zs = {}, {}, {}

    def along_y(self, turns=None):
        net = self.net
        for d in self.turns if turns is None else turns:
            at = (net.j + d) % self.nj
            self.ys[d] = net.send(self.grads.at[at, 1 - net.y], self.came.at[d], net.y_n)
            self.moves[d] = net.move(self.grads.at[at, net.y], self.stay.at[d])

    def along_z(self, turns):
        for d in turns:
            self.ys[d].wait_recv()
            self.moves[d].wait()

            def add(at, state, step, d=d):
                self.stay[d, at] = (self.stay[d, at].astype(F32) + self.came[d, at].astype(F32)).astype(BF)
                return state

            in_steps(self.wrows, add)
            if d:
                self.zs[d] = self.net.send(self.stay.at[d], self.last.at[d - 1], self.net.z_at(d))

    def landed(self):
        for d in range(1, self.nj):
            self.zs[d].wait_recv()

    def halves(self, total, sums):
        self.landed()

        def collect(at, state, step):
            both = [self.stay[0, at].astype(F32), jnp.zeros((step, self.width), F32)]
            for d in range(1, self.nj):
                both[d % 2] = both[d % 2] + self.last[d - 1, at].astype(F32)
            for parity in range(2):
                total[parity, at] = both[parity]
                state = state + square_tile(both[parity])
            return state

        square = in_steps(self.wrows, collect, jnp.zeros((8, 128), F32))
        copies = []
        for parity in range(2):
            half = (self.net.zl + parity) % 2
            copies.append(self.net.move(total.at[parity], sums.at[:, pl.ds(pl.multiple_of(half * self.width, self.width), self.width)]))
        return copies, square

    def whole(self, out):
        self.landed()

        def collect(at, state, step):
            value = self.stay[0, at].astype(F32)
            for d in range(1, self.nj):
                value = value + self.last[d - 1, at].astype(F32)
            out[at] = value
            return state

        in_steps(self.wrows, collect)


def scatter_scratch(nj, wrows, width):
    return [
        pltpu.VMEM((nj, wrows, width), BF), pltpu.VMEM((nj, wrows, width), BF),
        pltpu.VMEM((nj - 1, wrows, width), BF),
    ]


def back_kernel(
    n_dp, n_mp, part, hid, att, gains, out_grad, live, grads, grads_up,
    ghid, dg1, dg2, seq, sums, sums_up, squares,
    near, r1, r2, r3, own, stay, came, last, ustay, ucame, ulast, total, ss, rs, ls,
):
    net = Net(n_dp, n_mp, ss, rs, ls)
    loaded = net.move(part.at[pl.ds(0, 4)], near)
    cores = core_family(net, part, r1)
    net.meet(pair_partners(net, True))
    rows = hid.shape[0]
    for k in (3, 2, 1, 0):
        cores(k).start()
    weight = Scatter(net, grads, stay, came, last)
    weight_up = Scatter(net, grads_up, ustay, ucame, ulast)
    weight.along_y()
    loaded.wait()
    last_sums = reduce_pair_steps(
        net, near, cores, r1, r2, r3, rows, False, lambda k: None,
        (lambda: weight.along_z(weight.turns[:1]), lambda: weight.along_z(weight.turns[1:2])),
    )
    weight_up.along_y()
    for copy in last_sums:
        copy.wait_recv()
    g1, g2 = 1.0 + gains[1:2], 1.0 + gains[2:3]

    def rows_back(at, state):
        grad = pair_sum(near, r1, r2, r3, at)
        part_hid, d2 = rms_back_rows(hid[at], g2, grad)
        grad_hidden = out_grad[at] * live[at] + part_hid
        ghid[at] = grad_hidden
        grad_att, d1 = rms_back_rows(att[at], g1, grad_hidden)
        own[at] = grad_att.astype(BF)
        return state[0] + d1, state[1] + d2

    zero = jnp.zeros((1, D), F32)
    done1, done2 = by_rows(rows, rows_back, (zero, zero))
    dg1[...] = done1
    dg2[...] = done2
    finish = gather_seq_steps(net, own, seq)
    weight.along_z(weight.turns[2:])
    weight_up.along_z(weight_up.turns[:1])
    finish()
    weight_up.along_z(weight_up.turns[1:2])
    first_out, square = weight.halves(total, sums)
    weight_up.along_z(weight_up.turns[2:])
    for copy in first_out:
        copy.wait()
    last_out, square_up = weight_up.halves(total, sums_up)
    squares[...] = square + square_up
    for copy in last_out:
        copy.wait()
    net.close()


def back(n_dp, n_mp, part, hid, att, gains, out_grad, live, grads, grads_up):
    rows = hid.shape[0]
    block = (rows, D)
    nj = n_dp // 2
    _, _, wrows, width = grads.shape
    count = 24 + 6 * nj
    return call(
        functools.partial(back_kernel, n_dp, n_mp),
        [
            jax.ShapeDtypeStruct(block, F32), jax.ShapeDtypeStruct((1, D), F32), jax.ShapeDtypeStruct((1, D), F32),
            jax.ShapeDtypeStruct((4,) + block, BF), jax.ShapeDtypeStruct((wrows, 2 * width), F32),
            jax.ShapeDtypeStruct((wrows, 2 * width), F32), jax.ShapeDtypeStruct((8, 128), F32),
        ],
        [VMEM, VMEM, VMEM, ANY, ANY, ANY, VMEM], [ANY] + [VMEM] * 5 + [ANY, ANY],
        pair_scratch(rows, 4) + scatter_scratch(nj, wrows, width) * 2
        + [pltpu.VMEM((2, wrows, width), F32), dma(count), dma(count), dma(16 + 2 * nj)],
        5, 60,
    )(part, hid, att, gains, out_grad, live, grads, grads_up)


def attend_back(q, k, v, gm, marks_col, marks_row, cosine, sine, dq, dk, dv, tiles):
    total = q.shape[0]
    heads, group = q.shape[1] // HEAD_WIDTH, q.shape[1] // k.shape[1]
    size = total // 4
    half = HEAD_WIDTH // 2
    scale = HEAD_WIDTH**-0.5

    def body(t, state):
        at = pl.ds(pl.multiple_of(t * size, size), size)
        allowed = allowed_tile(marks_col, marks_row, at)
        c, s = cosine[at], sine[at]
        for head in range(heads):
            kv = head // group
            cols = slice(head * HEAD_WIDTH, (head + 1) * HEAD_WIDTH)
            kv_at = slice(kv * HEAD_WIDTH, (kv + 1) * HEAD_WIDTH)
            bent, probs = tile_probs(q, k, allowed, at, head, group)
            grad = gm[at, cols]
            dv[:, kv_at] += mm_rows(probs.astype(BF), grad)
            gp = mm_cols(grad, v[:, kv_at])
            inner = jnp.sum(probs * gp, axis=-1, keepdims=True)
            ds = (probs * (gp - inner) * (1.0 - bent * bent)).astype(BF)
            dk[:, kv_at] += mm_rows(ds, q[at, cols]) * scale
            turned = mm(ds, k[:, kv_at]) * scale
            a, b = turned[:, :half], turned[:, half:]
            first = head * HEAD_WIDTH
            dq[at, first : first + half] = (a * c + b * s).astype(BF)
            dq[at, first + half : first + HEAD_WIDTH] = (b * c - a * s).astype(BF)
        return state

    lax.fori_loop(tiles[0], tiles[1], body, 0)


def weight_grad(tokens, grads, out):
    wide = D // 3
    for n in range(0, D, wide):
        out[n : n + wide] = mm_rows(tokens[:, n : n + wide], grads[...]).astype(BF)


def close_kernel(
    n_dp, n_mp, seq_grad, seq_normed, q, k, v, mixed, wo, wq, wkv, cosine, sine, marks_col, marks_row,
    inputs, gains, ghid, terms_in, sum_down, squares,
    gin, sum_q, sum_kv, sum_o, gain_sum, norm,
    terms, got_terms, down, mine, got_squares, tokens, normed, wa, gm, dq, dk, dv, dkv, go, gq, gkv, got_q, got_kv, r1, r2,
    ostay, ocame, olast, ss, rs, ls,
):
    net = Net(n_dp, n_mp, ss, rs, ls)
    p = net.place()
    right = (net.ring(p + 1), net.m)
    left = (net.ring(p + n_dp - 1), net.m)
    nj = n_dp // 2
    rows = inputs.shape[0]
    seq_len, wrows = tokens.shape[0], sum_q.shape[0]
    wide0 = terms.shape[2]
    others = everyone(n_dp, n_mp, net.i, net.m)
    flat = net.i * n_mp + net.m
    per_norm = n_dp * n_mp // NORMS
    terms_load = net.move(terms_in, terms.at[pl.ds(per_norm, (NORMS - 1) * per_norm)])
    down_load = net.move(sum_down, down)
    net.meet(others)
    token_load = net.move(seq_grad, tokens)
    wa_load = net.move(wo, wa)
    normed_load = net.move(seq_normed, normed)
    ghid_load = net.move(ghid, gin)
    dk[...] = jnp.zeros_like(dk)
    dv[...] = jnp.zeros_like(dv)
    token_load.wait()
    wa_load.wait()

    def mix(at):
        gm[at] = mm(tokens[at], wa[...]).astype(BF)

    row_tiles(seq_len, seq_len // 2, mix)
    wa_load = net.move(wq, wa)
    weight_grad(tokens, mixed, go.reshape(D, go.shape[-1]))
    out = Scatter(net, go, ostay, ocame, olast)
    out.along_y()
    attend_back(q, k, v, gm, marks_col, marks_row, cosine, sine, dq, dk, dv, (0, 2))
    out.along_z(out.turns[:1])
    attend_back(q, k, v, gm, marks_col, marks_row, cosine, sine, dq, dk, dv, (2, 4))
    out.along_z(out.turns[1:])
    kv_cols = k.shape[1]
    half = HEAD_WIDTH // 2

    def turn_keys(at):
        c, s = cosine[at], sine[at]
        for h in range(0, kv_cols, HEAD_WIDTH):
            a, b = dk[at, h : h + half], dk[at, h + half : h + HEAD_WIDTH]
            dkv[at, h : h + half] = (a * c + b * s).astype(BF)
            dkv[at, h + half : h + HEAD_WIDTH] = (b * c - a * s).astype(BF)
        dkv[at, kv_cols:] = dv[at].astype(BF)

    row_tiles(seq_len, 128, turn_keys)
    normed_load.wait()
    weight_grad(normed, dq, gq)
    weight_grad(normed, dkv, gkv)

    def block(at, part):
        return pl.ds(pl.multiple_of(net.ring(p + 2 * n_dp + at) * wrows + part[0], 8), part[1])

    lanes = ((gq, got_q, sum_q, right, -1), (gkv, got_kv, sum_kv, left, 1))
    parts = two_parts(wrows)
    flight = {}
    for part in parts:
        for lane, (ref, got, _, device, way) in enumerate(lanes):
            flight[lane, part] = net.send(ref.at[block(way, part)], got.at[0, pl.ds(*part)], device)

    def hop(n):
        end = n == n_dp - 1
        for part in parts:
            for lane, (terms, got, result, device, way) in enumerate(lanes):
                flight[lane, part].wait_recv()
                first = net.ring(p + 2 * n_dp + way * (1 + n)) * wrows

                def add(here, state, step, first=first, terms=terms, got=got, result=result):
                    at = pl.ds(pl.multiple_of(first + here.start, 8), step)
                    value = got[n - 1, here].astype(F32) + terms[at].astype(F32)
                    if end:
                        result[here] = value
                    else:
                        terms[at] = value.astype(BF)
                    return state

                in_steps(part[1], add, 0, part[0])
                if not end:
                    flight[lane, part] = net.send(
                        terms.at[block(way * (1 + n), part)], got.at[n, pl.ds(*part)], device
                    )

    wa_load.wait()
    wide = D // 3
    copies = []
    for pair in (1, 0):
        at = pl.ds(pair * 2 * rows, 2 * rows)
        for n in range(0, D, wide):
            tokens[at, n : n + wide] = (
                mm_cols(dq[at], wa[n : n + wide]) + mm_cols(dkv[at], wkv[n : n + wide])
            ).astype(BF)
        if pair:
            c1 = net.send(tokens.at[pl.ds(3 * rows, rows)], r1.at[1], net.core_n)
            c0 = net.send(tokens.at[pl.ds(2 * rows, rows)], r1.at[0], net.core_n)
            hop(1)
    c1.wait_recv()

    def add_far(at, state):
        here = pl.ds(pl.multiple_of(rows + at.start, ROWS), ROWS)
        tokens[here] = (tokens[here].astype(F32) + r1[1, at].astype(F32)).astype(BF)
        return state

    by_rows(rows, add_far)
    x = net.send(tokens.at[pl.ds(rows, rows)], r2, net.x_n)
    c0.wait_recv()
    hop(2)
    hop(3)
    x.wait_recv()
    ghid_load.wait()
    g0 = 1.0 + gains[0:1]

    def rows_in(at, state):
        grad = tokens[at].astype(F32) + r1[0, at].astype(F32) + r2[at].astype(F32)
        part, d0 = rms_back_rows(inputs[at], g0, grad)
        gin[at] = gin[at] + part
        return state + d0

    dg0 = by_rows(rows, rows_in, jnp.zeros((1, D), F32))
    terms_load.wait()
    for n in range(per_norm):
        terms[n] = dg0[:, n * wide0 : (n + 1) * wide0]
    spread = [net.send(terms.at[dp * n_mp + mp], got_terms.at[flat], (dp, mp)) for dp, mp in others]
    own_terms = net.move(terms.at[flat], got_terms.at[flat])
    for n in range(4, n_dp - 1):
        hop(n)
    down_load.wait()

    def square_of(ref, state):
        return lax.fori_loop(
            0, ref.shape[0] // 8,
            lambda t, total: total + square_tile(ref[pl.ds(pl.multiple_of(t * 8, 8), 8)]), state,
        )

    square = square_of(down, squares[...])
    out.whole(sum_o)
    square = square_of(sum_o, square)
    own_terms.wait()
    for copy in spread:
        copy.wait_recv()
    total_gain = lax.fori_loop(
        0, n_dp * n_mp, lambda t, total: total + got_terms[t], jnp.zeros(got_terms.shape[1:], F32)
    )
    gain_sum[...] = total_gain
    square = square + jnp.sum(total_gain * total_gain) * (1.0 / 1024.0)
    hop(n_dp - 1)
    mine[...] = square_of(sum_kv, square_of(sum_q, square))
    spread = [net.send(mine, got_squares.at[flat], device) for device in others]
    net.move(mine, got_squares.at[flat]).wait()
    for copy in spread:
        copy.wait_recv()
    total = lax.fori_loop(0, n_dp * n_mp, lambda t, value: value + got_squares[t], jnp.zeros((8, 128), F32))
    norm[...] = jnp.broadcast_to(jnp.sqrt(jnp.sum(total, axis=(0, 1), keepdims=True)), (8, 128))
    net.close()


def close(n_dp, n_mp, seq_grad, seq_normed, q, k, v, mixed, wo, wq, wkv, cosine, sine, marks_col, marks_row,
          inputs, gains, ghid, terms, sum_down, squares):
    rows = inputs.shape[0]
    nj = n_dp // 2
    wrows = D // n_dp
    cols, kv_cols = q.shape[1], k.shape[1]
    seq_len = q.shape[0]
    devices = n_dp * n_mp
    count = 16 + 6 * nj + 4 * n_dp + 2 * devices
    piece = (1, NORMS * D // devices)
    vm = lambda *shape: pltpu.VMEM(shape, BF)
    small = jax.ShapeDtypeStruct((wrows, cols), F32)
    return call(
        functools.partial(close_kernel, n_dp, n_mp),
        [
            jax.ShapeDtypeStruct((rows, D), F32), small, jax.ShapeDtypeStruct((wrows, 2 * kv_cols), F32), small,
            jax.ShapeDtypeStruct(piece, F32), jax.ShapeDtypeStruct((8, 128), F32),
        ],
        [VMEM] * 6,
        [ANY, ANY] + [VMEM] * 4 + [ANY, ANY] + [VMEM] * 7 + [ANY] * 3 + [VMEM],
        [
            pltpu.VMEM((devices,) + piece, F32), pltpu.VMEM((devices,) + piece, F32),
            pltpu.VMEM(sum_down.shape, F32), pltpu.VMEM((8, 128), F32), pltpu.VMEM((devices, 8, 128), F32),
            vm(seq_len, D), vm(seq_len, D), vm(D, cols), vm(seq_len, cols), vm(seq_len, cols),
            pltpu.VMEM((seq_len, kv_cols), F32), pltpu.VMEM((seq_len, kv_cols), F32), vm(seq_len, 2 * kv_cols),
            vm(nj, 2, wrows, cols), vm(D, cols), vm(D, 2 * kv_cols),
            vm(n_dp - 1, wrows, cols), vm(n_dp - 1, wrows, 2 * kv_cols), vm(2, rows, D), vm(rows, D),
        ]
        + scatter_scratch(nj, wrows, cols) + [dma(count), dma(count), dma(14 + 2 * nj)],
        6, 60,
    )(seq_grad, seq_normed, q, k, v, mixed, wo, wq, wkv, cosine, sine, marks_col, marks_row,
      inputs, gains, ghid, terms, sum_down, squares)


def plain(kernel, grid, outs, out_specs, in_specs, mb, flops):
    return pl.pallas_call(
        kernel,
        out_shape=outs,
        grid=grid,
        in_specs=in_specs,
        out_specs=out_specs,
        compiler_params=pltpu.CompilerParams(
            dimension_semantics=("arbitrary",) * len(grid), vmem_limit_bytes=mb << 20
        ),
        cost_estimate=pl.CostEstimate(flops=flops, bytes_accessed=40 << 20, transcendentals=0),
    )


def whole(shape):
    return pl.BlockSpec(shape, lambda t: (0,) * len(shape), pipeline_mode=pl.Buffered(1))


def tile(rows, cols):
    return pl.BlockSpec((None, rows, cols), lambda t: (t, 0, 0))


GELU = math.sqrt(2.0 / math.pi)


def down_back_kernel(grad, gate, up, wg, wu, wd, dgate, dup, part):
    ga = mm(grad[...], wd[...])
    g = gate[...]
    square = g * g
    bend = jnp.tanh(GELU * (g + 0.044715 * (square * g)))
    halved = 0.5 * (1.0 + bend)
    slope = halved + (0.5 * GELU) * g * (1.0 - bend * bend) * (1.0 + (3.0 * 0.044715) * square)
    dg = (ga * up[...] * slope).astype(BF)
    du = (ga * (g * halved)).astype(BF)
    dgate[...] = dg
    dup[...] = du
    part[...] = (mm_cols(dg, wg[...]) + mm_cols(du, wu[...])).astype(BF)


def mlp_back(grad, gate, up, wg, wu, wd):
    blocks, rows, _ = grad.shape
    width = wg.shape[1]
    shape = (blocks, rows, width)
    return plain(
        down_back_kernel, (blocks,),
        [jax.ShapeDtypeStruct(shape, BF), jax.ShapeDtypeStruct(shape, BF), jax.ShapeDtypeStruct((blocks, rows, D), BF)],
        [tile(rows, width), tile(rows, width), tile(rows, D)],
        [tile(rows, D), tile(rows, width), tile(rows, width)] + [whole(wg.shape)] * 3, 56,
        6 * blocks * rows * D * width,
    )(grad, gate, up, wg, wu, wd)


def adam_kernel(norm, gain_grad, gw, gm, gv, g_gate, g_up, g_down, g_q, g_o, g_kv, *refs):
    ins, gain_outs, outs = refs[:9], refs[9:12], refs[12:]
    factor = jnp.minimum(1.0, CLIP_SCALE * math.sqrt(PARAMS) / norm[0:1, 0:1])
    news = adam_update(gw[...], gm[...], gv[...], gain_grad[0], factor[0])
    for out, new in zip(gain_outs, news):
        out[...] = new
    kv_cols = ins[6].shape[2]
    grads = (
        (lambda: g_gate[...], lambda: g_up[...], lambda: g_down[...]),
        (lambda: g_q[...], lambda: g_o[...]),
        (lambda: g_kv[:, :kv_cols], lambda: g_kv[:, kv_cols:]),
    )
    for n, group in enumerate(grads):
        w, m, v = ins[3 * n : 3 * n + 3]
        for k, grad in enumerate(group):
            news = adam_update(w[k], m[k], v[k], grad(), factor)
            for out, new in zip(outs[3 * n : 3 * n + 3], news):
                out[k] = new


def adam_all(norm, gain_grad, gains, grads, states):
    wrows = grads[0].shape[0]
    step = 48 if wrows % 48 == 0 else 8
    like = lambda a: jax.ShapeDtypeStruct(a.shape, F32)
    fixed = lambda a: pl.BlockSpec(a.shape, lambda t: (0,) * a.ndim)
    flat = lambda a: pl.BlockSpec((step, a.shape[1]), lambda t: (t, 0))
    deep = lambda a: pl.BlockSpec((a.shape[0], step, a.shape[2]), lambda t: (0, t, 0))
    return plain(
        adam_kernel, (wrows // step,), [like(a) for a in gains] + [like(a) for a in states],
        [fixed(a) for a in gains] + [deep(a) for a in states],
        [fixed(a) for a in (norm, gain_grad) + tuple(gains)] + [flat(a) for a in grads] + [deep(a) for a in states],
        56, 100,
    )(norm, gain_grad, *gains, *grads, *states)


def build_local(n_dp, n_mp):
    nj = n_dp // 2

    def y_swap(value):
        return lax.ppermute(value, "dp", [(k, k ^ 1) for k in range(n_dp)])

    def z_shift(value, d):
        pairs = [(a * 2 + b, ((a + d) % nj) * 2 + b) for a in range(nj) for b in range(2)]
        return lax.ppermute(value, "dp", pairs)

    def scatter_first(grad, y):
        away = lax.dynamic_index_in_dim(grad, 1 - y, 1, keepdims=False)
        stay = lax.dynamic_index_in_dim(grad, y, 1, keepdims=False)
        return stay, y_swap(away)

    def scatter_second(stay, came, j):
        both = (stay.astype(F32) + came.astype(F32)).astype(BF)
        both = [lax.dynamic_index_in_dim(both, (j + d) % nj, 0, keepdims=False) for d in range(nj)]
        return both[0], [z_shift(both[d], d) for d in range(1, nj)]

    def local(
        inputs, out_grad, segment_ids, pad_mask, bit_sel, w_qo, w_kv, w_mlp, norm_gains,
        m_qo, m_kv, m_mlp, m_gains, v_qo, v_kv, v_mlp, v_gains,
    ):
        i, m = lax.axis_index("dp"), lax.axis_index("mp")
        y, j = i % 2, i // 2
        zl = j % 2
        rows = inputs.shape[0]
        seq_len = segment_ids.shape[1]
        wrows = w_qo.shape[1]

        low_q = quantize(w_qo[0], D, bit_sel[0])
        low_o = quantize(w_qo[1], QW, bit_sel[0])
        low_kv = jnp.concatenate([quantize(w_kv[0], D, bit_sel[1]), quantize(w_kv[1], D, bit_sel[1])], 1)
        order = jnp.stack([m, m ^ 2, m ^ 1, m ^ 3])

        segments = segment_ids[0]
        every = jnp.arange(seq_len, dtype=jnp.int32)
        same = segments[:, None] == segments[None, :]
        begins = jnp.min(jnp.where(same, every[None, :], seq_len), axis=1)
        facts = jnp.stack([segments, pad_mask[0], every - begins]).reshape(3, n_mp, rows)
        segs, pads, positions = facts[:, order].reshape(3, seq_len)
        slots = (order[:, None] * rows + jnp.arange(rows, dtype=jnp.int32)[None, :]).reshape(-1)
        kv_cols = w_kv.shape[2]
        half_dim = HEAD_WIDTH // 2
        frequency = ROPE_BASE ** (-jnp.arange(half_dim, dtype=F32) * 2.0 / HEAD_WIDTH)
        angles = positions.astype(F32)[:, None] * frequency[None, :]
        cosine = jnp.cos(angles)
        sine = jnp.sin(angles)
        marks = jnp.stack([segs, slots, pads] + [segs] * 5)
        (
            query_bf, key_bf, value_bf, mixed_bf, attended, hidden_in, gain_rows, group_ffn, w_gate, w_up, w_down,
            wq, wkv, wo, seq_normed,
        ) = open_layer(
            n_dp, n_mp, low_q, low_kv, low_o, w_mlp, code_spacing(bit_sel[2]).reshape(1, 1), cosine, sine,
            marks.T, marks, inputs, norm_gains.reshape(1, -1),
        )
        w_gate, w_up, w_down = w_gate.reshape(D, -1), w_up.reshape(D, -1), w_down.reshape(D, -1)
        live = lax.dynamic_slice_in_dim(pad_mask[0], m * rows, rows).astype(F32)[:, None]
        outputs, grad_gain_three, gate, up, activated, group_grad = turn(
            n_dp, n_mp, group_ffn, w_gate, w_up, w_down, hidden_in, gain_rows, out_grad, live
        )
        tokens = 8 * rows
        grad_down = mm_rows(group_grad.reshape(tokens, D), activated.reshape(tokens, -1))
        grad_down = grad_down.astype(BF).reshape(nj, 2, wrows, -1)
        grad_down, group_grad = lax.optimization_barrier((grad_down, group_grad))
        down_stay, down_came = scatter_first(grad_down, y)
        grad_gate, grad_up, part = mlp_back(group_grad, gate, up, w_gate, w_up, w_down)
        flat_ffn = group_ffn.reshape(tokens, D)
        grad_gate, grad_up, down_came = lax.optimization_barrier((grad_gate, grad_up, down_came))
        down_own, down_shifted = scatter_second(down_stay, down_came, j)
        grads_gate = mm_rows(flat_ffn, grad_gate.reshape(tokens, -1)).astype(BF).reshape(nj, 2, wrows, -1)
        grads_gate, grad_up = lax.optimization_barrier((grads_gate, grad_up))
        grads_up = mm_rows(flat_ffn, grad_up.reshape(tokens, -1)).astype(BF).reshape(nj, 2, wrows, -1)
        grad_hidden, grad_gain_one, grad_gain_two, seq_grad, sum_gate, sum_up, squares = back(
            n_dp, n_mp, part, hidden_in, attended, gain_rows, out_grad, live,
            grads_gate, grads_up
        )
        seq_grad, down_shifted = lax.optimization_barrier((seq_grad, down_shifted))
        sums = [down_own.astype(F32), 0.0]
        for d in range(1, nj):
            sums[d % 2] = sums[d % 2] + down_shifted[d - 1].astype(F32)
        sum_down = jnp.concatenate(
            [jnp.where(zl == 0, sums[0], sums[1]), jnp.where(zl == 0, sums[1], sums[0])], 1
        )
        terms = jnp.concatenate([grad_gain_one, grad_gain_two, grad_gain_three])
        terms = terms.reshape((NORMS - 1) * n_dp * n_mp // NORMS, 1, -1)
        grad_in, sum_q, sum_kv, sum_o, sum_gains, norm = close(
            n_dp, n_mp, seq_grad.reshape(seq_len, D), seq_normed, query_bf, key_bf, value_bf, mixed_bf,
            wo, wq, wkv, cosine, sine, marks.T, marks, inputs, gain_rows, grad_hidden,
            terms, sum_down, squares,
        )
        sums = [sum_gate, sum_up, sum_down, sum_q, sum_o, sum_kv]
        news = adam_all(
            norm, sum_gains, [norm_gains, m_gains, v_gains], sums, [w_mlp, m_mlp, v_mlp, w_qo, m_qo, v_qo, w_kv, m_kv, v_kv]
        )
        grad_norm = norm[0, :1]
        new_gains, new_m_gains, new_v_gains = news[:3]
        new_w_mlp, new_m_mlp, new_v_mlp, new_w_qo, new_m_qo, new_v_qo, new_w_kv, new_m_kv, new_v_kv = news[3:]
        return (
            outputs, grad_in, grad_norm, new_w_qo, new_w_kv, new_w_mlp, new_gains,
            new_m_qo, new_m_kv, new_m_mlp, new_m_gains, new_v_qo, new_v_kv, new_v_mlp, new_v_gains,
        )

    return local


def solution(mesh):
    tokens = P(("dp", "mp"), None)
    weight = P(None, "dp", "mp")
    flat = P(("dp", "mp"))
    per_weight = (weight, weight, weight, flat)
    return jax.shard_map(
        build_local(mesh.shape["dp"], mesh.shape["mp"]),
        mesh=mesh,
        in_specs=(tokens, tokens, P("dp", None), P("dp", None), P()) + per_weight * 3,
        out_specs=(tokens, tokens, P()) + per_weight * 3,
        check_vma=False,
    )
```

```python
import functools
import math

import jax
import jax.numpy as jnp
from jax import lax
from jax.experimental import pallas as pl
from jax.experimental.pallas import tpu as pltpu
from jax.sharding import PartitionSpec as P

D = 2304
HEAD_WIDTH = 256
FF = 9216
NORMS = 4
QW = 2048
PARAMS = 77865984

EPSILON = 1e-06
SOFT_CAP = 50.0
ROPE_BASE = 10000.0
MASKED_SCORE = -1e30
FIRST_DECAY = 0.9
SECOND_DECAY = 0.95
LEARN_RATE = 0.04
WEIGHT_DECAY = 0.1
ADAM_EPSILON = 1e-08
CLIP_SCALE = 0.5

BF = jnp.bfloat16
F32 = jnp.float32


def code_spacing(selector):
    return jnp.where(selector == 0, 1.0, jnp.where(selector == 1, 16.0, 64.0)).astype(F32)


def quantize_values(master, step, spacing):
    half = jnp.floor(spacing * 0.5)
    inverse = jnp.where(spacing > 32.0, 1.0 / 64.0, jnp.where(spacing > 8.0, 1.0 / 16.0, 1.0))
    codes = jnp.clip(jnp.floor(master / step + 0.5), -128.0, 127.0)
    top = 128.0 * inverse
    sliced = jnp.clip(jnp.floor((codes + half) * inverse), -top, top - 1.0)
    return (sliced * spacing) * step


def quantize(master, fan_in, selector):
    step = jnp.float32(1.0 / (32.0 * math.sqrt(fan_in)))
    return quantize_values(master, step, code_spacing(selector)).astype(BF)


def inv_root(values):
    return lax.rsqrt(jnp.mean(values * values, axis=-1, keepdims=True) + EPSILON)


def rms_norm(values, norm_gain):
    return values * inv_root(values) * (1.0 + norm_gain)


def rms_back(values, norm_gain, grad):
    root = inv_root(values)
    scaled = grad * (1.0 + norm_gain)
    dot = jnp.mean(values * scaled, axis=-1, keepdims=True)
    grad_values = root * scaled - values * (root * root * root * dot)
    grad_gain = jnp.sum(values * root * grad, axis=0)
    return grad_values, grad_gain


def mm(left, right):
    return lax.dot_general(left, right, (((1,), (0,)), ((), ())), preferred_element_type=F32)


def mm_rows(left, right):
    return lax.dot_general(left, right, (((0,), (0,)), ((), ())), preferred_element_type=F32)


def mm_cols(left, right):
    return lax.dot_general(left, right, (((1,), (1,)), ((), ())), preferred_element_type=F32)


def adam_update(master, first_moment, second_moment, gradient, factor):
    clipped = gradient * factor
    new_first = FIRST_DECAY * first_moment + (1.0 - FIRST_DECAY) * clipped
    new_second = SECOND_DECAY * second_moment + (1.0 - SECOND_DECAY) * clipped * clipped
    new_master = master - LEARN_RATE * (
        new_first / (jnp.sqrt(new_second) + ADAM_EPSILON) + WEIGHT_DECAY * master
    )
    return (new_master, new_first, new_second)


MESH = pl.DeviceIdType.MESH
ANY = pl.BlockSpec(memory_space=pl.ANY)
VMEM = pl.BlockSpec(memory_space=pltpu.VMEM)
ROWS = 32


class Net:
    def __init__(self, n_dp, n_mp, send_sems, recv_sems, local_sems=None):
        self.n_dp, self.n_mp = n_dp, n_mp
        self.send_sems, self.recv_sems, self.local_sems = send_sems, recv_sems, local_sems
        self.used, self.used_local, self.open = 0, 0, []
        self.i, self.m = lax.axis_index("dp"), lax.axis_index("mp")
        self.y, self.j = self.i % 2, self.i // 2
        self.zl = self.j % 2
        self.c, self.x = self.m % 2, self.m // 2
        self.core_n = (self.i, self.m + 1 - 2 * self.c)
        self.x_n = (self.i, (self.m + 2) % 4)
        self.y_n = (self.i + 1 - 2 * self.y, self.m)
        self.z_n = (self.i + 2 - 4 * self.zl, self.m)

    def z_at(self, d):
        nj = self.n_dp // 2
        return (((self.j + d) % nj) * 2 + self.y, self.m)

    def place(self):
        return (1 - self.y) * self.j + self.y * (self.n_dp - 1 - self.j)

    def ring(self, at):
        n, nj = self.n_dp, self.n_dp // 2
        at = at % n
        late = at // nj
        return (1 - late) * 2 * at + late * (2 * (n - 1 - at) + 1)

    def meet(self, devices):
        barrier = pltpu.get_barrier_semaphore()
        for device in devices:
            pl.semaphore_signal(barrier, inc=1, device_id=device, device_id_type=MESH)
        pl.semaphore_wait(barrier, len(devices))

    def send(self, src, dst, device):
        at = self.used
        self.used += 1
        copy = pltpu.make_async_remote_copy(
            src_ref=src, dst_ref=dst, send_sem=self.send_sems.at[at], recv_sem=self.recv_sems.at[at],
            device_id=device, device_id_type=MESH,
        )
        copy.start()
        self.open.append((copy, copy.wait_send))
        return copy

    def family(self, count, make):
        base = self.used
        self.used += count

        def copy_of(k):
            return make(k, self.send_sems.at[base + k], self.recv_sems.at[base + k])

        for k in range(count):
            copy = copy_of(k)
            self.open.append((copy, copy.wait_send))
        return copy_of

    def locals(self, count):
        base = self.used_local
        self.used_local += count
        return base

    def sent(self, copy):
        copy.wait_send()
        self.open = [entry for entry in self.open if entry[0] is not copy]

    def move(self, src, dst):
        at = self.used_local
        self.used_local += 1
        copy = pltpu.make_async_copy(src, dst, self.local_sems.at[at])
        copy.start()
        return copy

    def keep(self, src, dst):
        copy = self.move(src, dst)
        self.open.append((copy, copy.wait))

    def close(self):
        for _, wait in self.open:
            wait()


def upper(count):
    return count // 16 * 8


def dma(n):
    return pltpu.SemaphoreType.DMA((n,))


def call(kernel, outs, out_specs, in_specs, scratch, cid, mb, flops=0):
    return pl.pallas_call(
        kernel,
        out_shape=outs,
        in_specs=in_specs,
        out_specs=out_specs,
        scratch_shapes=scratch,
        compiler_params=pltpu.CompilerParams(
            collective_id=cid, has_side_effects=True, vmem_limit_bytes=mb << 20
        ),
    )


def by_rows(total, body, carry=0):
    return lax.fori_loop(
        0, total // ROWS, lambda t, state: body(pl.ds(pl.multiple_of(t * ROWS, ROWS), ROWS), state), carry
    )


def everyone(n_dp, n_mp, i, m):
    flat = i * n_mp + m
    total = n_dp * n_mp
    return [(((flat + t) % total) // n_mp, (flat + t) % n_mp) for t in range(1, total)]


def gather_seq_steps(net, own, seq):
    far = net.send(own, seq.at[1], net.x_n)
    near = net.send(own, seq.at[2], net.core_n)
    net.keep(own, seq.at[0])

    def finish():
        far.wait_recv()
        both = net.send(seq.at[1], seq.at[3], net.core_n)
        near.wait_recv()
        both.wait_recv()

    return finish


def gather_pair_steps(net, own, group, split=False):
    far = net.send(own, group.at[2], net.x_n)
    zed = net.send(own, group.at[1], net.z_n)
    near = net.send(own, group.at[4], net.core_n)
    net.keep(own, group.at[0])

    def finish(between=lambda: None):
        head = pl.ds(0, D // 2) if split else pl.ds(0, D)
        rest = pl.ds(D // 2, D // 2)
        zed.wait_recv()
        both = net.send(group.at[1, :, head], group.at[3, :, head], net.x_n)
        far.wait_recv()
        if split:
            other = net.send(group.at[2, :, rest], group.at[3, :, rest], net.z_n)
        near_z = net.send(group.at[1], group.at[5], net.core_n)
        near_x = net.send(group.at[2], group.at[6], net.core_n)
        between()
        both.wait_recv()
        if split:
            other.wait_recv()
        near_both = net.send(group.at[3], group.at[7], net.core_n)
        for copy in (near, near_z, near_x, near_both):
            copy.wait_recv()

    return finish


def pair_partners(net, with_y):
    nj = net.n_dp // 2
    zs = [net.z_at(d) for d in range(1, nj)] if with_y else [net.z_n]
    return [net.core_n, net.x_n] + zs + ([net.y_n] if with_y else [])


def row_tiles(total, size, body):
    lax.fori_loop(
        0, total // size, lambda t, state: (body(pl.ds(pl.multiple_of(t * size, size), size)), state)[1], 0
    )


def project(seq, wq, wkv, cosine, sine, q, k, v):
    total = seq.shape[0]
    kv_cols = k.shape[1]
    half = HEAD_WIDTH // 2

    def body(at):
        tokens = seq[at]
        c, s = cosine[at], sine[at]

        def turn(lin, out, cols):
            for h in range(0, cols, HEAD_WIDTH):
                a, b = lin[:, h : h + half], lin[:, h + half : h + HEAD_WIDTH]
                out[at, h : h + half] = (a * c - b * s).astype(BF)
                out[at, h + half : h + HEAD_WIDTH] = (b * c + a * s).astype(BF)

        turn(mm(tokens, wq[...]), q, q.shape[1])
        lin = mm(tokens, wkv[...])
        turn(lin, k, kv_cols)
        v[at] = lin[:, kv_cols:].astype(BF)

    row_tiles(total, total // 2, body)


def allowed_tile(marks_col, marks_row, at):
    segs, slots = marks_col[at, 0:1], marks_col[at, 1:2]
    seg_row, slot_row, pad_row = marks_row[0:1], marks_row[1:2], marks_row[2:3]
    same_slot = slot_row == slots
    return (seg_row == segs) & (slot_row <= slots) & ((pad_row == 1) | same_slot)


def tile_probs(q, k, allowed, at, head, group):
    cols = slice(head * HEAD_WIDTH, (head + 1) * HEAD_WIDTH)
    kv = head // group
    kv_at = slice(kv * HEAD_WIDTH, (kv + 1) * HEAD_WIDTH)
    bent = jnp.tanh(mm_cols(q[at, cols], k[:, kv_at]) * (HEAD_WIDTH**-0.5 / SOFT_CAP))
    raised = jnp.where(allowed, jnp.exp(SOFT_CAP * bent), 0.0)
    return bent, raised * (1.0 / jnp.sum(raised, axis=-1, keepdims=True))


def attend(q, k, v, marks_col, marks_row, mixed):
    total = q.shape[0]
    heads, group = q.shape[1] // HEAD_WIDTH, q.shape[1] // k.shape[1]

    def body(at):
        allowed = allowed_tile(marks_col, marks_row, at)
        for head in range(heads):
            _, probs = tile_probs(q, k, allowed, at, head, group)
            kv = head // group
            kv_at = slice(kv * HEAD_WIDTH, (kv + 1) * HEAD_WIDTH)
            mixed[at, head * HEAD_WIDTH : (head + 1) * HEAD_WIDTH] = mm(
                probs.astype(BF), v[:, kv_at]
            ).astype(BF)

    row_tiles(total, 128, body)


def out_project(mixed, wo, part):
    blocks, rows, _ = part.shape
    wide = D // 3
    for pair in range(blocks // 2 - 1, -1, -1):
        for n in range(0, D, wide):
            got = mm_cols(mixed[pair * 2 * rows : (pair + 1) * 2 * rows], wo[n : n + wide]).astype(BF)
            part[pair * 2, :, n : n + wide] = got[:rows]
            part[pair * 2 + 1, :, n : n + wide] = got[rows:]


def chunks(wrows, parts=3):
    if wrows % (16 * parts) == 0:
        return tuple((n * wrows // parts, wrows // parts) for n in range(parts))
    return ((0, upper(wrows)), (upper(wrows), wrows - upper(wrows)))


def two_parts(wrows):
    return ((0, upper(wrows)), (upper(wrows), wrows - upper(wrows)))


class Gather:
    def __init__(self, net, pieces):
        self.net, self.pieces, self.nj = net, pieces, net.n_dp // 2
        self.flight, self.relays, self.own = {}, {}, {}

    def out(self, n):
        net = self.net
        source, place, parity = self.pieces[n]
        self.own[n] = net.move(source(net.zl), place(net.i))
        self.relays[n] = [net.send(source(net.zl), place(net.i), net.y_n)]
        for d in range(1, self.nj):
            self.flight[n, d] = net.send(source((net.j + d) % self.nj % 2), place(net.i), net.z_at(d))

    def on(self, n):
        net = self.net
        _, place, _ = self.pieces[n]
        for d in range(1, self.nj):
            self.flight[n, d].wait_recv()
            at = ((net.j + self.nj - d) % self.nj) * 2 + net.y
            self.relays[n].append(net.send(place(at), place(at), net.y_n))

    def done(self, n):
        self.own.pop(n).wait()
        for copy in self.relays.pop(n):
            copy.wait_recv()


def all_of_dp(net):
    return [net.x_n, net.core_n] + [((net.i + t) % net.n_dp, net.m) for t in range(1, net.n_dp)]


def open_kernel(
    n_dp, n_mp, low_q, low_kv, low_o, w_mlp, width_mlp, cosine, sine, marks_col, marks_row, inputs, own_gains,
    q, k, v, mixed, att, hid, gains, group, full0, full1, full2, out_q, out_kv, out_o, out_seq,
    wq, wkv, wo, seq, part, r1, r2, own, got_gains, masters, lows, ss, rs, ls,
):
    net = Net(n_dp, n_mp, ss, rs, ls)
    p = net.place()
    right = (net.ring(p + 1), net.m)
    left = (net.ring(p + n_dp - 1), net.m)
    rows = inputs.shape[0]
    wrows, width = full0.shape[1:]
    others = everyone(n_dp, n_mp, net.i, net.m)
    net.meet(others)
    flat = net.i * n_mp + net.m
    loads = [net.move(w_mlp.at[n], masters.at[n]) for n in range(3)]

    def block(ref, at):
        return ref.at[pl.ds(pl.multiple_of(at * wrows, 8), wrows)]

    def lot(n):
        return seq.at[pl.ds(n * rows, rows)]

    def piece(ref, at, part):
        first, count = part
        return ref.at[pl.ds(pl.multiple_of(at * wrows + first, 8), count)]

    parts = two_parts(wrows)
    flight = {}
    for cut in parts:
        for lane, (ref, low, device) in enumerate(((wq, low_q, right), (wkv, low_kv, left))):
            flight[cut, lane] = net.send(low.at[pl.ds(*cut)], piece(ref, net.i, cut), device)
    spread = [net.send(own_gains, got_gains.at[flat], device) for device in others]
    net.move(own_gains, got_gains.at[flat]).wait()
    for copy in spread:
        copy.wait_recv()
    per_norm = n_dp * n_mp // NORMS
    for n in range(NORMS):
        gains[n : n + 1] = jnp.concatenate([got_gains[n * per_norm + t] for t in range(per_norm)], 1)
    g0 = 1.0 + gains[0:1]

    def norm_rows(at, state):
        own[at] = (inputs[at] * inv_root(inputs[at]) * g0).astype(BF)
        return state

    by_rows(rows, norm_rows)
    far = net.send(own, lot(1), net.x_n)
    near = net.send(own, lot(2), net.core_n)

    def quantize_part(n):
        loads[n].wait()
        spacing = width_mlp[...]
        step = jnp.float32(1.0 / (32.0 * math.sqrt(FF if n == 2 else D)))

        def body(at, state, count):
            lows[n, at] = quantize_values(masters[n, at], step, spacing).astype(BF)
            return state

        in_steps(wrows, body)

    own_parts = [net.move(own, lot(0)), net.move(low_q, block(wq, net.i)), net.move(low_kv, block(wkv, net.i))]
    half = lambda which: pl.ds(pl.multiple_of(which * width, width), width)
    pieces = [(lambda which: low_o, lambda at: block(wo, at), 1)]

    def add_piece(ref, full, first, count):
        rows_at = pl.ds(first, count)
        pieces.append((lambda which: ref.at[rows_at, half(which)], lambda at: full.at[at, rows_at], 2))

    for ref, full, cuts in ((lows.at[0], full0, 3), (lows.at[1], full1, 3), (lows.at[2], full2, 6)):
        for first, count in chunks(wrows, cuts):
            add_piece(ref, full, first, count)
    weights = Gather(net, pieces)
    for hop in range(1, n_dp):
        from_right, from_left = net.ring(p + n_dp - hop), net.ring(p + hop)
        for cut in parts:
            for lane, (ref, at, device) in enumerate(((wq, from_right, right), (wkv, from_left, left))):
                flight[cut, lane].wait_recv()
                if hop < n_dp - 1:
                    flight[cut, lane] = net.send(piece(ref, at, cut), piece(ref, at, cut), device)
        if hop == n_dp // 2:
            far.wait_recv()
            both = net.send(lot(1), lot(3), net.core_n)
        if hop in (1, 2, 3):
            quantize_part(hop - 1)
        if hop == n_dp - 2:
            weights.out(0)
    weights.out(1)
    weights.out(2)
    weights.out(3)
    near.wait_recv()
    both.wait_recv()
    for copy in own_parts:
        copy.wait()
    net.sent(far)
    net.sent(near)
    for ref, result in ((wq, out_q), (wkv, out_kv), (seq, out_seq)):
        net.keep(ref, result)
    project(seq, wq, wkv, cosine, sine, q, k, v)
    attend(q, k, v, marks_col, marks_row, mixed)
    def step(n):
        if n < len(pieces):
            weights.on(n)
            if n + 4 < len(pieces):
                weights.out(n + 4)

    step(0)
    weights.done(0)
    net.keep(wo, out_o)
    out_project(mixed, wo, part)
    c1 = net.send(part.at[3], r1.at[1], net.core_n)
    c0 = net.send(part.at[2], r1.at[0], net.core_n)
    c1.wait_recv()

    def first_rows(at, state):
        part[1, at] = (part[1, at].astype(F32) + r1[1, at].astype(F32)).astype(BF)
        return state

    by_rows(rows, first_rows)
    x = net.send(part.at[1], r2, net.x_n)
    c0.wait_recv()
    step(1)
    x.wait_recv()
    g1, g2 = 1.0 + gains[1:2], 1.0 + gains[2:3]

    def second(at, state):
        total = part[0, at].astype(F32) + r1[0, at].astype(F32) + r2[at].astype(F32)
        att[at] = total
        hidden = inputs[at] + total * inv_root(total) * g1
        hid[at] = hidden
        own[at] = (hidden * inv_root(hidden) * g2).astype(BF)
        return state

    by_rows(rows, second)
    finish = gather_pair_steps(net, own, group)
    step(2)
    step(3)
    finish(lambda: (step(4), step(5)))
    for n in range(6, len(pieces)):
        step(n)
    for n in range(1, len(pieces)):
        weights.done(n)
    net.close()


def open_layer(n_dp, n_mp, low_q, low_kv, low_o, w_mlp, width_mlp, cosine, sine, marks_col, marks_row, inputs, gains):
    rows = inputs.shape[0]
    nj = n_dp // 2
    total_devices = n_dp * n_mp
    count = 24 + 4 * n_dp + 28 * nj + total_devices
    block = (rows, D)
    wrows, width = w_mlp.shape[1], w_mlp.shape[2] // 2
    cols, kv_cols = low_q.shape[1], low_kv.shape[1] // 2
    vm = lambda *shape: pltpu.VMEM(shape, BF)
    bf = lambda *shape: jax.ShapeDtypeStruct(shape, BF)
    total = 4 * rows
    f32 = jax.ShapeDtypeStruct(block, F32)
    full = bf(n_dp, wrows, width)
    return call(
        functools.partial(open_kernel, n_dp, n_mp),
        [
            bf(total, cols), bf(total, kv_cols), bf(total, kv_cols), bf(total, cols), f32, f32,
            jax.ShapeDtypeStruct((NORMS, D), F32),
            bf(8, *block), full, full, full, bf(D, cols), bf(D, 2 * kv_cols), bf(D, cols), bf(total, D),
        ],
        [VMEM] * 7 + [ANY] * 8, [ANY] * 4 + [VMEM] * 7,
        [
            vm(D, cols), vm(D, 2 * kv_cols), vm(D, cols), vm(total, D), vm(4, *block), vm(2, *block), vm(*block),
            vm(*block), pltpu.VMEM((total_devices,) + gains.shape, F32), pltpu.VMEM(w_mlp.shape, F32),
            vm(*w_mlp.shape), dma(count), dma(count), dma(32),
        ],
        2, 60,
    )(low_q, low_kv, low_o, w_mlp, width_mlp, cosine, sine, marks_col, marks_row, inputs, gains)


def reduce_pair_steps(net, near, cores, r1, r2, r3, rows, split=False, compute=None, hooks=None):
    plan = [(pl.ds(0, D // 2 if split else D), (3, 2), net.x_n, 1, net.z_n)]
    if split:
        plan.append((pl.ds(D // 2, D // 2), (3, 1), net.z_n, 2, net.x_n))
    firsts = {}
    for k in (3, 2, 1) if split else (3, 2):
        compute(k)
        cores(k).wait_recv()
        for part, (cols, blocks, device, _, _) in enumerate(plan):
            if k not in blocks:
                continue
            at_block = blocks.index(k)

            def add(at, state, k=k, cols=cols):
                near[k, at, cols] = (near[k, at, cols].astype(F32) + r1[k, at, cols].astype(F32)).astype(BF)
                return state

            by_rows(rows, add)
            firsts[part, at_block] = net.send(near.at[k, :, cols], r2.at[at_block, :, cols], device)
    for k in (0,) if split else (1, 0):
        compute(k)
        cores(k).wait_recv()
    last = []
    if hooks:
        hooks[0]()
    for part, (cols, blocks, _, second, device) in enumerate(plan):
        firsts[part, 0].wait_recv()

        def add(at, state, cols=cols, second=second):
            near[second, at, cols] = (
                near[second, at, cols].astype(F32) + r1[second, at, cols].astype(F32) + r2[0, at, cols].astype(F32)
            ).astype(BF)
            return state

        by_rows(rows, add)
        last.append(net.send(near.at[second, :, cols], r3.at[:, cols], device))
    if hooks:
        hooks[1]()
    for part in range(len(plan)):
        firsts[part, 1].wait_recv()
    return last


def pair_sum(near, r1, r2, r3, at):
    return near[0, at].astype(F32) + r1[0, at].astype(F32) + r2[1, at].astype(F32) + r3[at].astype(F32)


def pair_scratch(rows, blocks=8):
    block = (rows, D)
    return [
        pltpu.VMEM((blocks,) + block, BF), pltpu.VMEM((4,) + block, BF), pltpu.VMEM((2,) + block, BF),
        pltpu.VMEM(block, BF), pltpu.VMEM(block, BF),
    ]


def core_family(net, parts, r1):
    return net.family(
        4,
        lambda k, send, recv: pltpu.make_async_remote_copy(
            src_ref=parts.at[4 + k], dst_ref=r1.at[k], send_sem=send, recv_sem=recv,
            device_id=net.core_n, device_id_type=MESH,
        ),
    )


def block_at(t):
    return 7 - t // 2 - 4 * (t % 2)


class Stream:
    def __init__(self, net, pairs, inward):
        self.net, self.pairs, self.inward = net, pairs, inward
        self.base = net.locals(2 * len(pairs))

    def copies(self, t):
        slot = t % 2
        for n, (far, held) in enumerate(self.pairs):
            ends = (far.at[block_at(t)], held.at[slot])
            yield pltpu.make_async_copy(
                *(ends if self.inward else ends[::-1]), self.net.local_sems.at[self.base + 2 * n + slot]
            )

    def start(self, t):
        for copy in self.copies(t):
            copy.start()

    def wait(self, t):
        for copy in self.copies(t):
            copy.wait()


def rms_back_rows(values, gain, grad):
    root = inv_root(values)
    scaled = grad * gain
    dot = jnp.mean(values * scaled, axis=-1, keepdims=True)
    return root * scaled - values * (root * root * root * dot), jnp.sum(values * root * grad, axis=0, keepdims=True)


def turn_kernel(
    n_dp, n_mp, ffn, w_gate, w_up, w_down, hid, gains, out_grad, live,
    outputs, dgain, gate, up, act, group,
    parts, r1, r2, r3, own, wg, wu, wd, tokens, gate_b, up_b, act_b, ss, rs, ls,
):
    net = Net(n_dp, n_mp, ss, rs, ls)
    loads = [net.move(src, dst) for src, dst in ((w_gate, wg), (w_up, wu), (w_down, wd))]
    rows = hid.shape[0]
    incoming = Stream(net, [(ffn, tokens)], True)
    outgoing = Stream(net, [(gate, gate_b), (up, up_b), (act, act_b)], False)
    cores = core_family(net, parts, r1)
    incoming.start(0)
    net.meet(pair_partners(net, False))
    for load in loads:
        load.wait()

    def block(t, state):
        slot, at = t % 2, block_at(t)
        incoming.wait(t)

        @pl.when(t < 7)
        def _():
            incoming.start(t + 1)

        g = mm(tokens[slot], wg[...])
        u = mm(tokens[slot], wu[...])
        bend = jnp.tanh(GELU * (g + 0.044715 * (g * g * g)))
        a = (0.5 * g * (1.0 + bend) * u).astype(BF)

        @pl.when(t >= 2)
        def _():
            outgoing.wait(t - 2)

        gate_b[slot] = g
        up_b[slot] = u
        act_b[slot] = a
        outgoing.start(t)
        parts[at] = mm_cols(a, wd[...]).astype(BF)
        return state

    def compute(k):
        def both(t, state):
            block(t, state)

            @pl.when(t % 2 == 0)
            def _():
                cores(k).start()

            return state

        lax.fori_loop(6 - 2 * k, 8 - 2 * k, both, 0)

    last_sums = reduce_pair_steps(net, parts, cores, r1, r2, r3, rows, True, compute)
    outgoing.wait(6)
    outgoing.wait(7)
    for copy in last_sums:
        copy.wait_recv()
    g3 = 1.0 + gains[3:4]

    def last(at, state):
        total = pair_sum(parts, r1, r2, r3, at)
        outputs[at] = hid[at] + total * inv_root(total) * g3
        grad, dg = rms_back_rows(total, g3, out_grad[at] * live[at])
        own[at] = grad.astype(BF)
        return state + dg

    dgain[...] = by_rows(rows, last, jnp.zeros((1, D), F32))
    gather_pair_steps(net, own, group, True)()
    net.close()


def turn(n_dp, n_mp, ffn, w_gate, w_up, w_down, hid, gains, out_grad, live):
    rows = hid.shape[0]
    block = (rows, D)
    width = w_gate.shape[1]
    vm = lambda *shape: pltpu.VMEM(shape, BF)
    return call(
        functools.partial(turn_kernel, n_dp, n_mp),
        [
            jax.ShapeDtypeStruct(block, F32), jax.ShapeDtypeStruct((1, D), F32),
            jax.ShapeDtypeStruct((8, rows, width), F32), jax.ShapeDtypeStruct((8, rows, width), F32),
            jax.ShapeDtypeStruct((8, rows, width), BF), jax.ShapeDtypeStruct((8,) + block, BF),
        ],
        [VMEM, VMEM] + [ANY] * 4, [ANY] * 4 + [VMEM] * 4,
        pair_scratch(rows)
        + [
            vm(D, width), vm(D, width), vm(D, width), vm(2, *block),
            pltpu.VMEM((2, rows, width), F32), pltpu.VMEM((2, rows, width), F32), vm(2, rows, width),
            dma(32), dma(32), dma(16),
        ],
        4, 60,
    )(ffn, w_gate, w_up, w_down, hid, gains, out_grad, live)


def in_steps(count, body, carry=0, first=0):
    step = 16 if count % 16 == 0 else 8
    return lax.fori_loop(
        0, count // step,
        lambda t, state: body(pl.ds(pl.multiple_of(first + t * step, 8), step), state, step), carry,
    )


def square_tile(value):
    value = value * value
    total = jnp.zeros((8, 128), F32)
    for r in range(0, value.shape[0], 8):
        for c in range(0, value.shape[1], 128):
            total = total + value[r : r + 8, c : c + 128]
    return total


class Scatter:
    def __init__(self, net, grads, stay, came, last):
        self.net, self.grads, self.stay, self.came, self.last = net, grads, stay, came, last
        self.nj, self.wrows, self.width = came.shape
        self.turns = sorted(range(1, self.nj), key=lambda d: abs(d - self.nj // 2)) + [0]
        self.ys, self.moves, self.zs = {}, {}, {}

    def along_y(self, turns=None):
        net = self.net
        for d in self.turns if turns is None else turns:
            at = (net.j + d) % self.nj
            self.ys[d] = net.send(self.grads.at[at, 1 - net.y], self.came.at[d], net.y_n)
            self.moves[d] = net.move(self.grads.at[at, net.y], self.stay.at[d])

    def along_z(self, turns):
        for d in turns:
            self.ys[d].wait_recv()
            self.moves[d].wait()

            def add(at, state, step, d=d):
                self.stay[d, at] = (self.stay[d, at].astype(F32) + self.came[d, at].astype(F32)).astype(BF)
                return state

            in_steps(self.wrows, add)
            if d:
                self.zs[d] = self.net.send(self.stay.at[d], self.last.at[d - 1], self.net.z_at(d))

    def landed(self):
        for d in range(1, self.nj):
            self.zs[d].wait_recv()

    def halves(self, total, sums):
        self.landed()

        def collect(at, state, step):
            both = [self.stay[0, at].astype(F32), jnp.zeros((step, self.width), F32)]
            for d in range(1, self.nj):
                both[d % 2] = both[d % 2] + self.last[d - 1, at].astype(F32)
            for parity in range(2):
                total[parity, at] = both[parity]
                state = state + square_tile(both[parity])
            return state

        square = in_steps(self.wrows, collect, jnp.zeros((8, 128), F32))
        copies = []
        for parity in range(2):
            half = (self.net.zl + parity) % 2
            copies.append(self.net.move(total.at[parity], sums.at[:, pl.ds(pl.multiple_of(half * self.width, self.width), self.width)]))
        return copies, square

    def whole(self, out):
        self.landed()

        def collect(at, state, step):
            value = self.stay[0, at].astype(F32)
            for d in range(1, self.nj):
                value = value + self.last[d - 1, at].astype(F32)
            out[at] = value
            return state

        in_steps(self.wrows, collect)


def scatter_scratch(nj, wrows, width):
    return [
        pltpu.VMEM((nj, wrows, width), BF), pltpu.VMEM((nj, wrows, width), BF),
        pltpu.VMEM((nj - 1, wrows, width), BF),
    ]


def back_kernel(
    n_dp, n_mp, part, hid, att, gains, out_grad, live, grads, grads_up,
    ghid, dg1, dg2, seq, sums, sums_up, squares,
    near, r1, r2, r3, own, stay, came, last, ustay, ucame, ulast, total, ss, rs, ls,
):
    net = Net(n_dp, n_mp, ss, rs, ls)
    loaded = net.move(part.at[pl.ds(0, 4)], near)
    cores = core_family(net, part, r1)
    net.meet(pair_partners(net, True))
    rows = hid.shape[0]
    for k in (3, 2, 1, 0):
        cores(k).start()
    weight = Scatter(net, grads, stay, came, last)
    weight_up = Scatter(net, grads_up, ustay, ucame, ulast)
    weight.along_y()
    loaded.wait()
    last_sums = reduce_pair_steps(
        net, near, cores, r1, r2, r3, rows, False, lambda k: None,
        (lambda: weight.along_z(weight.turns[:1]), lambda: weight.along_z(weight.turns[1:2])),
    )
    weight_up.along_y()
    for copy in last_sums:
        copy.wait_recv()
    g1, g2 = 1.0 + gains[1:2], 1.0 + gains[2:3]

    def rows_back(at, state):
        grad = pair_sum(near, r1, r2, r3, at)
        part_hid, d2 = rms_back_rows(hid[at], g2, grad)
        grad_hidden = out_grad[at] * live[at] + part_hid
        ghid[at] = grad_hidden
        grad_att, d1 = rms_back_rows(att[at], g1, grad_hidden)
        own[at] = grad_att.astype(BF)
        return state[0] + d1, state[1] + d2

    zero = jnp.zeros((1, D), F32)
    done1, done2 = by_rows(rows, rows_back, (zero, zero))
    dg1[...] = done1
    dg2[...] = done2
    finish = gather_seq_steps(net, own, seq)
    weight.along_z(weight.turns[2:])
    weight_up.along_z(weight_up.turns[:1])
    finish()
    weight_up.along_z(weight_up.turns[1:2])
    first_out, square = weight.halves(total, sums)
    weight_up.along_z(weight_up.turns[2:])
    for copy in first_out:
        copy.wait()
    last_out, square_up = weight_up.halves(total, sums_up)
    squares[...] = square + square_up
    for copy in last_out:
        copy.wait()
    net.close()


def back(n_dp, n_mp, part, hid, att, gains, out_grad, live, grads, grads_up):
    rows = hid.shape[0]
    block = (rows, D)
    nj = n_dp // 2
    _, _, wrows, width = grads.shape
    count = 24 + 6 * nj
    return call(
        functools.partial(back_kernel, n_dp, n_mp),
        [
            jax.ShapeDtypeStruct(block, F32), jax.ShapeDtypeStruct((1, D), F32), jax.ShapeDtypeStruct((1, D), F32),
            jax.ShapeDtypeStruct((4,) + block, BF), jax.ShapeDtypeStruct((wrows, 2 * width), F32),
            jax.ShapeDtypeStruct((wrows, 2 * width), F32), jax.ShapeDtypeStruct((8, 128), F32),
        ],
        [VMEM, VMEM, VMEM, ANY, ANY, ANY, VMEM], [ANY] + [VMEM] * 5 + [ANY, ANY],
        pair_scratch(rows, 4) + scatter_scratch(nj, wrows, width) * 2
        + [pltpu.VMEM((2, wrows, width), F32), dma(count), dma(count), dma(16 + 2 * nj)],
        5, 60,
    )(part, hid, att, gains, out_grad, live, grads, grads_up)


def attend_back(q, k, v, gm, marks_col, marks_row, cosine, sine, dq, dk, dv, tiles):
    total = q.shape[0]
    heads, group = q.shape[1] // HEAD_WIDTH, q.shape[1] // k.shape[1]
    size = total // 4
    half = HEAD_WIDTH // 2
    scale = HEAD_WIDTH**-0.5

    def body(t, state):
        at = pl.ds(pl.multiple_of(t * size, size), size)
        allowed = allowed_tile(marks_col, marks_row, at)
        c, s = cosine[at], sine[at]
        for head in range(heads):
            kv = head // group
            cols = slice(head * HEAD_WIDTH, (head + 1) * HEAD_WIDTH)
            kv_at = slice(kv * HEAD_WIDTH, (kv + 1) * HEAD_WIDTH)
            bent, probs = tile_probs(q, k, allowed, at, head, group)
            grad = gm[at, cols]
            dv[:, kv_at] += mm_rows(probs.astype(BF), grad)
            gp = mm_cols(grad, v[:, kv_at])
            inner = jnp.sum(probs * gp, axis=-1, keepdims=True)
            ds = (probs * (gp - inner) * (1.0 - bent * bent)).astype(BF)
            dk[:, kv_at] += mm_rows(ds, q[at, cols]) * scale
            turned = mm(ds, k[:, kv_at]) * scale
            a, b = turned[:, :half], turned[:, half:]
            first = head * HEAD_WIDTH
            dq[at, first : first + half] = (a * c + b * s).astype(BF)
            dq[at, first + half : first + HEAD_WIDTH] = (b * c - a * s).astype(BF)
        return state

    lax.fori_loop(tiles[0], tiles[1], body, 0)


def weight_grad(tokens, grads, out):
    wide = D // 3
    for n in range(0, D, wide):
        out[n : n + wide] = mm_rows(tokens[:, n : n + wide], grads[...]).astype(BF)


def close_kernel(
    n_dp, n_mp, seq_grad, seq_normed, q, k, v, mixed, wo, wq, wkv, cosine, sine, marks_col, marks_row,
    inputs, gains, ghid, terms_in, sum_down, squares,
    gin, sum_q, sum_kv, sum_o, gain_sum, norm,
    terms, got_terms, down, mine, got_squares, tokens, normed, wa, gm, dq, dk, dv, dkv, go, gq, gkv, got_q, got_kv, r1, r2,
    ostay, ocame, olast, ss, rs, ls,
):
    net = Net(n_dp, n_mp, ss, rs, ls)
    p = net.place()
    right = (net.ring(p + 1), net.m)
    left = (net.ring(p + n_dp - 1), net.m)
    nj = n_dp // 2
    rows = inputs.shape[0]
    seq_len, wrows = tokens.shape[0], sum_q.shape[0]
    wide0 = terms.shape[2]
    others = everyone(n_dp, n_mp, net.i, net.m)
    flat = net.i * n_mp + net.m
    per_norm = n_dp * n_mp // NORMS
    terms_load = net.move(terms_in, terms.at[pl.ds(per_norm, (NORMS - 1) * per_norm)])
    down_load = net.move(sum_down, down)
    net.meet(others)
    token_load = net.move(seq_grad, tokens)
    wa_load = net.move(wo, wa)
    normed_load = net.move(seq_normed, normed)
    ghid_load = net.move(ghid, gin)
    dk[...] = jnp.zeros_like(dk)
    dv[...] = jnp.zeros_like(dv)
    token_load.wait()
    wa_load.wait()

    def mix(at):
        gm[at] = mm(tokens[at], wa[...]).astype(BF)

    row_tiles(seq_len, seq_len // 2, mix)
    wa_load = net.move(wq, wa)
    weight_grad(tokens, mixed, go.reshape(D, go.shape[-1]))
    out = Scatter(net, go, ostay, ocame, olast)
    out.along_y()
    attend_back(q, k, v, gm, marks_col, marks_row, cosine, sine, dq, dk, dv, (0, 2))
    out.along_z(out.turns[:1])
    attend_back(q, k, v, gm, marks_col, marks_row, cosine, sine, dq, dk, dv, (2, 4))
    out.along_z(out.turns[1:])
    kv_cols = k.shape[1]
    half = HEAD_WIDTH // 2

    def turn_keys(at):
        c, s = cosine[at], sine[at]
        for h in range(0, kv_cols, HEAD_WIDTH):
            a, b = dk[at, h : h + half], dk[at, h + half : h + HEAD_WIDTH]
            dkv[at, h : h + half] = (a * c + b * s).astype(BF)
            dkv[at, h + half : h + HEAD_WIDTH] = (b * c - a * s).astype(BF)
        dkv[at, kv_cols:] = dv[at].astype(BF)

    row_tiles(seq_len, 128, turn_keys)
    normed_load.wait()
    weight_grad(normed, dq, gq)
    weight_grad(normed, dkv, gkv)

    def block(at, part):
        return pl.ds(pl.multiple_of(net.ring(p + 2 * n_dp + at) * wrows + part[0], 8), part[1])

    lanes = ((gq, got_q, sum_q, right, -1), (gkv, got_kv, sum_kv, left, 1))
    parts = two_parts(wrows)
    flight = {}
    for part in parts:
        for lane, (ref, got, _, device, way) in enumerate(lanes):
            flight[lane, part] = net.send(ref.at[block(way, part)], got.at[0, pl.ds(*part)], device)

    def hop(n):
        end = n == n_dp - 1
        for part in parts:
            for lane, (terms, got, result, device, way) in enumerate(lanes):
                flight[lane, part].wait_recv()
                first = net.ring(p + 2 * n_dp + way * (1 + n)) * wrows

                def add(here, state, step, first=first, terms=terms, got=got, result=result):
                    at = pl.ds(pl.multiple_of(first + here.start, 8), step)
                    value = got[n - 1, here].astype(F32) + terms[at].astype(F32)
                    if end:
                        result[here] = value
                    else:
                        terms[at] = value.astype(BF)
                    return state

                in_steps(part[1], add, 0, part[0])
                if not end:
                    flight[lane, part] = net.send(
                        terms.at[block(way * (1 + n), part)], got.at[n, pl.ds(*part)], device
                    )

    wa_load.wait()
    wide = D // 3
    copies = []
    for pair in (1, 0):
        at = pl.ds(pair * 2 * rows, 2 * rows)
        for n in range(0, D, wide):
            tokens[at, n : n + wide] = (
                mm_cols(dq[at], wa[n : n + wide]) + mm_cols(dkv[at], wkv[n : n + wide])
            ).astype(BF)
        if pair:
            c1 = net.send(tokens.at[pl.ds(3 * rows, rows)], r1.at[1], net.core_n)
            c0 = net.send(tokens.at[pl.ds(2 * rows, rows)], r1.at[0], net.core_n)
            hop(1)
    c1.wait_recv()

    def add_far(at, state):
        here = pl.ds(pl.multiple_of(rows + at.start, ROWS), ROWS)
        tokens[here] = (tokens[here].astype(F32) + r1[1, at].astype(F32)).astype(BF)
        return state

    by_rows(rows, add_far)
    x = net.send(tokens.at[pl.ds(rows, rows)], r2, net.x_n)
    c0.wait_recv()
    hop(2)
    hop(3)
    x.wait_recv()
    ghid_load.wait()
    g0 = 1.0 + gains[0:1]

    def rows_in(at, state):
        grad = tokens[at].astype(F32) + r1[0, at].astype(F32) + r2[at].astype(F32)
        part, d0 = rms_back_rows(inputs[at], g0, grad)
        gin[at] = gin[at] + part
        return state + d0

    dg0 = by_rows(rows, rows_in, jnp.zeros((1, D), F32))
    terms_load.wait()
    for n in range(per_norm):
        terms[n] = dg0[:, n * wide0 : (n + 1) * wide0]
    spread = [net.send(terms.at[dp * n_mp + mp], got_terms.at[flat], (dp, mp)) for dp, mp in others]
    own_terms = net.move(terms.at[flat], got_terms.at[flat])
    for n in range(4, n_dp - 1):
        hop(n)
    down_load.wait()

    def square_of(ref, state):
        return lax.fori_loop(
            0, ref.shape[0] // 8,
            lambda t, total: total + square_tile(ref[pl.ds(pl.multiple_of(t * 8, 8), 8)]), state,
        )

    square = square_of(down, squares[...])
    out.whole(sum_o)
    square = square_of(sum_o, square)
    own_terms.wait()
    for copy in spread:
        copy.wait_recv()
    total_gain = lax.fori_loop(
        0, n_dp * n_mp, lambda t, total: total + got_terms[t], jnp.zeros(got_terms.shape[1:], F32)
    )
    gain_sum[...] = total_gain
    square = square + jnp.sum(total_gain * total_gain) * (1.0 / 1024.0)
    hop(n_dp - 1)
    mine[...] = square_of(sum_kv, square_of(sum_q, square))
    spread = [net.send(mine, got_squares.at[flat], device) for device in others]
    net.move(mine, got_squares.at[flat]).wait()
    for copy in spread:
        copy.wait_recv()
    total = lax.fori_loop(0, n_dp * n_mp, lambda t, value: value + got_squares[t], jnp.zeros((8, 128), F32))
    norm[...] = jnp.broadcast_to(jnp.sqrt(jnp.sum(total, axis=(0, 1), keepdims=True)), (8, 128))
    net.close()


def close(n_dp, n_mp, seq_grad, seq_normed, q, k, v, mixed, wo, wq, wkv, cosine, sine, marks_col, marks_row,
          inputs, gains, ghid, terms, sum_down, squares):
    rows = inputs.shape[0]
    nj = n_dp // 2
    wrows = D // n_dp
    cols, kv_cols = q.shape[1], k.shape[1]
    seq_len = q.shape[0]
    devices = n_dp * n_mp
    count = 16 + 6 * nj + 4 * n_dp + 2 * devices
    piece = (1, NORMS * D // devices)
    vm = lambda *shape: pltpu.VMEM(shape, BF)
    small = jax.ShapeDtypeStruct((wrows, cols), F32)
    return call(
        functools.partial(close_kernel, n_dp, n_mp),
        [
            jax.ShapeDtypeStruct((rows, D), F32), small, jax.ShapeDtypeStruct((wrows, 2 * kv_cols), F32), small,
            jax.ShapeDtypeStruct(piece, F32), jax.ShapeDtypeStruct((8, 128), F32),
        ],
        [VMEM] * 6,
        [ANY, ANY] + [VMEM] * 4 + [ANY, ANY] + [VMEM] * 7 + [ANY] * 3 + [VMEM],
        [
            pltpu.VMEM((devices,) + piece, F32), pltpu.VMEM((devices,) + piece, F32),
            pltpu.VMEM(sum_down.shape, F32), pltpu.VMEM((8, 128), F32), pltpu.VMEM((devices, 8, 128), F32),
            vm(seq_len, D), vm(seq_len, D), vm(D, cols), vm(seq_len, cols), vm(seq_len, cols),
            pltpu.VMEM((seq_len, kv_cols), F32), pltpu.VMEM((seq_len, kv_cols), F32), vm(seq_len, 2 * kv_cols),
            vm(nj, 2, wrows, cols), vm(D, cols), vm(D, 2 * kv_cols),
            vm(n_dp - 1, wrows, cols), vm(n_dp - 1, wrows, 2 * kv_cols), vm(2, rows, D), vm(rows, D),
        ]
        + scatter_scratch(nj, wrows, cols) + [dma(count), dma(count), dma(14 + 2 * nj)],
        6, 60,
    )(seq_grad, seq_normed, q, k, v, mixed, wo, wq, wkv, cosine, sine, marks_col, marks_row,
      inputs, gains, ghid, terms, sum_down, squares)


def plain(kernel, grid, outs, out_specs, in_specs, mb, flops):
    return pl.pallas_call(
        kernel,
        out_shape=outs,
        grid=grid,
        in_specs=in_specs,
        out_specs=out_specs,
        compiler_params=pltpu.CompilerParams(
            dimension_semantics=("arbitrary",) * len(grid), vmem_limit_bytes=mb << 20
        ),
        cost_estimate=pl.CostEstimate(flops=flops, bytes_accessed=40 << 20, transcendentals=0),
    )


def whole(shape):
    return pl.BlockSpec(shape, lambda t: (0,) * len(shape), pipeline_mode=pl.Buffered(1))


def tile(rows, cols):
    return pl.BlockSpec((None, rows, cols), lambda t: (t, 0, 0))


GELU = math.sqrt(2.0 / math.pi)


def down_back_kernel(grad, gate, up, wg, wu, wd, dgate, dup, part):
    ga = mm(grad[...], wd[...])
    g = gate[...]
    square = g * g
    bend = jnp.tanh(GELU * (g + 0.044715 * (square * g)))
    halved = 0.5 * (1.0 + bend)
    slope = halved + (0.5 * GELU) * g * (1.0 - bend * bend) * (1.0 + (3.0 * 0.044715) * square)
    dg = (ga * up[...] * slope).astype(BF)
    du = (ga * (g * halved)).astype(BF)
    dgate[...] = dg
    dup[...] = du
    part[...] = (mm_cols(dg, wg[...]) + mm_cols(du, wu[...])).astype(BF)


def mlp_back(grad, gate, up, wg, wu, wd):
    real_blocks, real_rows, _ = grad.shape
    width = wg.shape[1]
    blocks, rows = real_blocks // 2, real_rows * 2
    grad, gate, up = (a.reshape(blocks, rows, a.shape[2]) for a in (grad, gate, up))
    shape = (blocks, rows, width)
    dgate, dup, part = plain(
        down_back_kernel, (blocks,),
        [jax.ShapeDtypeStruct(shape, BF), jax.ShapeDtypeStruct(shape, BF), jax.ShapeDtypeStruct((blocks, rows, D), BF)],
        [tile(rows, width), tile(rows, width), tile(rows, D)],
        [tile(rows, D), tile(rows, width), tile(rows, width)] + [whole(wg.shape)] * 3, 56,
        6 * blocks * rows * D * width,
    )(grad, gate, up, wg, wu, wd)
    return dgate, dup, part.reshape(real_blocks, real_rows, D)


def adam_kernel(norm, gain_grad, gw, gm, gv, g_gate, g_up, g_down, g_q, g_o, g_kv, *refs):
    ins, gain_outs, outs = refs[:9], refs[9:12], refs[12:]
    factor = jnp.minimum(1.0, CLIP_SCALE * math.sqrt(PARAMS) / norm[0:1, 0:1])
    news = adam_update(gw[...], gm[...], gv[...], gain_grad[0], factor[0])
    for out, new in zip(gain_outs, news):
        out[...] = new
    kv_cols = ins[6].shape[2]
    grads = (
        (lambda: g_gate[...], lambda: g_up[...], lambda: g_down[...]),
        (lambda: g_q[...], lambda: g_o[...]),
        (lambda: g_kv[:, :kv_cols], lambda: g_kv[:, kv_cols:]),
    )
    for n, group in enumerate(grads):
        w, m, v = ins[3 * n : 3 * n + 3]
        for k, grad in enumerate(group):
            news = adam_update(w[k], m[k], v[k], grad(), factor)
            for out, new in zip(outs[3 * n : 3 * n + 3], news):
                out[k] = new


def adam_all(norm, gain_grad, gains, grads, states):
    wrows = grads[0].shape[0]
    step = 48 if wrows % 48 == 0 else 8
    like = lambda a: jax.ShapeDtypeStruct(a.shape, F32)
    fixed = lambda a: pl.BlockSpec(a.shape, lambda t: (0,) * a.ndim)
    flat = lambda a: pl.BlockSpec((step, a.shape[1]), lambda t: (t, 0))
    deep = lambda a: pl.BlockSpec((a.shape[0], step, a.shape[2]), lambda t: (0, t, 0))
    return plain(
        adam_kernel, (wrows // step,), [like(a) for a in gains] + [like(a) for a in states],
        [fixed(a) for a in gains] + [deep(a) for a in states],
        [fixed(a) for a in (norm, gain_grad) + tuple(gains)] + [flat(a) for a in grads] + [deep(a) for a in states],
        56, 100,
    )(norm, gain_grad, *gains, *grads, *states)


def build_local(n_dp, n_mp):
    nj = n_dp // 2

    def y_swap(value):
        return lax.ppermute(value, "dp", [(k, k ^ 1) for k in range(n_dp)])

    def z_shift(value, d):
        pairs = [(a * 2 + b, ((a + d) % nj) * 2 + b) for a in range(nj) for b in range(2)]
        return lax.ppermute(value, "dp", pairs)

    def scatter_first(grad, y):
        away = lax.dynamic_index_in_dim(grad, 1 - y, 1, keepdims=False)
        stay = lax.dynamic_index_in_dim(grad, y, 1, keepdims=False)
        return stay, y_swap(away)

    def scatter_second(stay, came, j):
        both = (stay.astype(F32) + came.astype(F32)).astype(BF)
        both = [lax.dynamic_index_in_dim(both, (j + d) % nj, 0, keepdims=False) for d in range(nj)]
        return both[0], [z_shift(both[d], d) for d in range(1, nj)]

    def local(
        inputs, out_grad, segment_ids, pad_mask, bit_sel, w_qo, w_kv, w_mlp, norm_gains,
        m_qo, m_kv, m_mlp, m_gains, v_qo, v_kv, v_mlp, v_gains,
    ):
        i, m = lax.axis_index("dp"), lax.axis_index("mp")
        y, j = i % 2, i // 2
        zl = j % 2
        rows = inputs.shape[0]
        seq_len = segment_ids.shape[1]
        wrows = w_qo.shape[1]

        low_q = quantize(w_qo[0], D, bit_sel[0])
        low_o = quantize(w_qo[1], QW, bit_sel[0])
        low_kv = jnp.concatenate([quantize(w_kv[0], D, bit_sel[1]), quantize(w_kv[1], D, bit_sel[1])], 1)
        order = jnp.stack([m, m ^ 2, m ^ 1, m ^ 3])

        segments = segment_ids[0]
        every = jnp.arange(seq_len, dtype=jnp.int32)
        same = segments[:, None] == segments[None, :]
        begins = jnp.min(jnp.where(same, every[None, :], seq_len), axis=1)
        facts = jnp.stack([segments, pad_mask[0], every - begins]).reshape(3, n_mp, rows)
        segs, pads, positions = facts[:, order].reshape(3, seq_len)
        slots = (order[:, None] * rows + jnp.arange(rows, dtype=jnp.int32)[None, :]).reshape(-1)
        kv_cols = w_kv.shape[2]
        half_dim = HEAD_WIDTH // 2
        frequency = ROPE_BASE ** (-jnp.arange(half_dim, dtype=F32) * 2.0 / HEAD_WIDTH)
        angles = positions.astype(F32)[:, None] * frequency[None, :]
        cosine = jnp.cos(angles)
        sine = jnp.sin(angles)
        marks = jnp.stack([segs, slots, pads] + [segs] * 5)
        (
            query_bf, key_bf, value_bf, mixed_bf, attended, hidden_in, gain_rows, group_ffn, w_gate, w_up, w_down,
            wq, wkv, wo, seq_normed,
        ) = open_layer(
            n_dp, n_mp, low_q, low_kv, low_o, w_mlp, code_spacing(bit_sel[2]).reshape(1, 1), cosine, sine,
            marks.T, marks, inputs, norm_gains.reshape(1, -1),
        )
        w_gate, w_up, w_down = w_gate.reshape(D, -1), w_up.reshape(D, -1), w_down.reshape(D, -1)
        live = lax.dynamic_slice_in_dim(pad_mask[0], m * rows, rows).astype(F32)[:, None]
        outputs, grad_gain_three, gate, up, activated, group_grad = turn(
            n_dp, n_mp, group_ffn, w_gate, w_up, w_down, hidden_in, gain_rows, out_grad, live
        )
        tokens = 8 * rows
        grad_down = mm_rows(group_grad.reshape(tokens, D), activated.reshape(tokens, -1))
        grad_down = grad_down.astype(BF).reshape(nj, 2, wrows, -1)
        grad_down, group_grad = lax.optimization_barrier((grad_down, group_grad))
        down_stay, down_came = scatter_first(grad_down, y)
        grad_gate, grad_up, part = mlp_back(group_grad, gate, up, w_gate, w_up, w_down)
        flat_ffn = group_ffn.reshape(tokens, D)
        grad_gate, grad_up, down_came = lax.optimization_barrier((grad_gate, grad_up, down_came))
        down_own, down_shifted = scatter_second(down_stay, down_came, j)
        grads_gate = mm_rows(flat_ffn, grad_gate.reshape(tokens, -1)).astype(BF).reshape(nj, 2, wrows, -1)
        grads_gate, grad_up = lax.optimization_barrier((grads_gate, grad_up))
        grads_up = mm_rows(flat_ffn, grad_up.reshape(tokens, -1)).astype(BF).reshape(nj, 2, wrows, -1)
        grad_hidden, grad_gain_one, grad_gain_two, seq_grad, sum_gate, sum_up, squares = back(
            n_dp, n_mp, part, hidden_in, attended, gain_rows, out_grad, live,
            grads_gate, grads_up
        )
        seq_grad, down_shifted = lax.optimization_barrier((seq_grad, down_shifted))
        sums = [down_own.astype(F32), 0.0]
        for d in range(1, nj):
            sums[d % 2] = sums[d % 2] + down_shifted[d - 1].astype(F32)
        sum_down = jnp.concatenate(
            [jnp.where(zl == 0, sums[0], sums[1]), jnp.where(zl == 0, sums[1], sums[0])], 1
        )
        terms = jnp.concatenate([grad_gain_one, grad_gain_two, grad_gain_three])
        terms = terms.reshape((NORMS - 1) * n_dp * n_mp // NORMS, 1, -1)
        grad_in, sum_q, sum_kv, sum_o, sum_gains, norm = close(
            n_dp, n_mp, seq_grad.reshape(seq_len, D), seq_normed, query_bf, key_bf, value_bf, mixed_bf,
            wo, wq, wkv, cosine, sine, marks.T, marks, inputs, gain_rows, grad_hidden,
            terms, sum_down, squares,
        )
        sums = [sum_gate, sum_up, sum_down, sum_q, sum_o, sum_kv]
        news = adam_all(
            norm, sum_gains, [norm_gains, m_gains, v_gains], sums, [w_mlp, m_mlp, v_mlp, w_qo, m_qo, v_qo, w_kv, m_kv, v_kv]
        )
        grad_norm = norm[0, :1]
        new_gains, new_m_gains, new_v_gains = news[:3]
        new_w_mlp, new_m_mlp, new_v_mlp, new_w_qo, new_m_qo, new_v_qo, new_w_kv, new_m_kv, new_v_kv = news[3:]
        return (
            outputs, grad_in, grad_norm, new_w_qo, new_w_kv, new_w_mlp, new_gains,
            new_m_qo, new_m_kv, new_m_mlp, new_m_gains, new_v_qo, new_v_kv, new_v_mlp, new_v_gains,
        )

    return local


def solution(mesh):
    tokens = P(("dp", "mp"), None)
    weight = P(None, "dp", "mp")
    flat = P(("dp", "mp"))
    per_weight = (weight, weight, weight, flat)
    return jax.shard_map(
        build_local(mesh.shape["dp"], mesh.shape["mp"]),
        mesh=mesh,
        in_specs=(tokens, tokens, P("dp", None), P("dp", None), P()) + per_weight * 3,
        out_specs=(tokens, tokens, P()) + per_weight * 3,
        check_vma=False,
    )
```

```python
import functools
import math

import jax
import jax.numpy as jnp
from jax import lax
from jax.experimental import pallas as pl
from jax.experimental.pallas import tpu as pltpu
from jax.sharding import PartitionSpec as P

D = 2304
HEAD_WIDTH = 256
FF = 9216
NORMS = 4
QW = 2048
PARAMS = 77865984

EPSILON = 1e-06
SOFT_CAP = 50.0
ROPE_BASE = 10000.0
MASKED_SCORE = -1e30
FIRST_DECAY = 0.9
SECOND_DECAY = 0.95
LEARN_RATE = 0.04
WEIGHT_DECAY = 0.1
ADAM_EPSILON = 1e-08
CLIP_SCALE = 0.5

BF = jnp.bfloat16
F32 = jnp.float32


def code_spacing(selector):
    return jnp.where(selector == 0, 1.0, jnp.where(selector == 1, 16.0, 64.0)).astype(F32)


def quantize_values(master, step, spacing):
    half = jnp.floor(spacing * 0.5)
    inverse = jnp.where(spacing > 32.0, 1.0 / 64.0, jnp.where(spacing > 8.0, 1.0 / 16.0, 1.0))
    codes = jnp.clip(jnp.floor(master / step + 0.5), -128.0, 127.0)
    top = 128.0 * inverse
    sliced = jnp.clip(jnp.floor((codes + half) * inverse), -top, top - 1.0)
    return (sliced * spacing) * step


def quantize(master, fan_in, selector):
    step = jnp.float32(1.0 / (32.0 * math.sqrt(fan_in)))
    return quantize_values(master, step, code_spacing(selector)).astype(BF)


def inv_root(values):
    return lax.rsqrt(jnp.mean(values * values, axis=-1, keepdims=True) + EPSILON)


def rms_norm(values, norm_gain):
    return values * inv_root(values) * (1.0 + norm_gain)


def rms_back(values, norm_gain, grad):
    root = inv_root(values)
    scaled = grad * (1.0 + norm_gain)
    dot = jnp.mean(values * scaled, axis=-1, keepdims=True)
    grad_values = root * scaled - values * (root * root * root * dot)
    grad_gain = jnp.sum(values * root * grad, axis=0)
    return grad_values, grad_gain


def mm(left, right):
    return lax.dot_general(left, right, (((1,), (0,)), ((), ())), preferred_element_type=F32)


def mm_rows(left, right):
    return lax.dot_general(left, right, (((0,), (0,)), ((), ())), preferred_element_type=F32)


def mm_cols(left, right):
    return lax.dot_general(left, right, (((1,), (1,)), ((), ())), preferred_element_type=F32)


def adam_update(master, first_moment, second_moment, gradient, factor):
    clipped = gradient * factor
    new_first = FIRST_DECAY * first_moment + (1.0 - FIRST_DECAY) * clipped
    new_second = SECOND_DECAY * second_moment + (1.0 - SECOND_DECAY) * clipped * clipped
    new_master = master - LEARN_RATE * (
        new_first / (jnp.sqrt(new_second) + ADAM_EPSILON) + WEIGHT_DECAY * master
    )
    return (new_master, new_first, new_second)


MESH = pl.DeviceIdType.MESH
ANY = pl.BlockSpec(memory_space=pl.ANY)
VMEM = pl.BlockSpec(memory_space=pltpu.VMEM)
ROWS = 32


class Net:
    def __init__(self, n_dp, n_mp, send_sems, recv_sems, local_sems=None):
        self.n_dp, self.n_mp = n_dp, n_mp
        self.send_sems, self.recv_sems, self.local_sems = send_sems, recv_sems, local_sems
        self.used, self.used_local, self.open = 0, 0, []
        self.i, self.m = lax.axis_index("dp"), lax.axis_index("mp")
        self.y, self.j = self.i % 2, self.i // 2
        self.zl = self.j % 2
        self.c, self.x = self.m % 2, self.m // 2
        self.core_n = (self.i, self.m + 1 - 2 * self.c)
        self.x_n = (self.i, (self.m + 2) % 4)
        self.y_n = (self.i + 1 - 2 * self.y, self.m)
        self.z_n = (self.i + 2 - 4 * self.zl, self.m)

    def z_at(self, d):
        nj = self.n_dp // 2
        return (((self.j + d) % nj) * 2 + self.y, self.m)

    def place(self):
        return (1 - self.y) * self.j + self.y * (self.n_dp - 1 - self.j)

    def ring(self, at):
        n, nj = self.n_dp, self.n_dp // 2
        at = at % n
        late = at // nj
        return (1 - late) * 2 * at + late * (2 * (n - 1 - at) + 1)

    def meet(self, devices):
        barrier = pltpu.get_barrier_semaphore()
        for device in devices:
            pl.semaphore_signal(barrier, inc=1, device_id=device, device_id_type=MESH)
        pl.semaphore_wait(barrier, len(devices))

    def send(self, src, dst, device):
        at = self.used
        self.used += 1
        copy = pltpu.make_async_remote_copy(
            src_ref=src, dst_ref=dst, send_sem=self.send_sems.at[at], recv_sem=self.recv_sems.at[at],
            device_id=device, device_id_type=MESH,
        )
        copy.start()
        self.open.append((copy, copy.wait_send))
        return copy

    def family(self, count, make):
        base = self.used
        self.used += count

        def copy_of(k):
            return make(k, self.send_sems.at[base + k], self.recv_sems.at[base + k])

        for k in range(count):
            copy = copy_of(k)
            self.open.append((copy, copy.wait_send))
        return copy_of

    def locals(self, count):
        base = self.used_local
        self.used_local += count
        return base

    def sent(self, copy):
        copy.wait_send()
        self.open = [entry for entry in self.open if entry[0] is not copy]

    def move(self, src, dst):
        at = self.used_local
        self.used_local += 1
        copy = pltpu.make_async_copy(src, dst, self.local_sems.at[at])
        copy.start()
        return copy

    def keep(self, src, dst):
        copy = self.move(src, dst)
        self.open.append((copy, copy.wait))

    def close(self):
        for _, wait in self.open:
            wait()


def upper(count):
    return count // 16 * 8


def dma(n):
    return pltpu.SemaphoreType.DMA((n,))


def call(kernel, outs, out_specs, in_specs, scratch, cid, mb, flops=0):
    return pl.pallas_call(
        kernel,
        out_shape=outs,
        in_specs=in_specs,
        out_specs=out_specs,
        scratch_shapes=scratch,
        compiler_params=pltpu.CompilerParams(
            collective_id=cid, has_side_effects=True, vmem_limit_bytes=mb << 20
        ),
    )


def by_rows(total, body, carry=0):
    return lax.fori_loop(
        0, total // ROWS, lambda t, state: body(pl.ds(pl.multiple_of(t * ROWS, ROWS), ROWS), state), carry
    )


def everyone(n_dp, n_mp, i, m):
    flat = i * n_mp + m
    total = n_dp * n_mp
    return [(((flat + t) % total) // n_mp, (flat + t) % n_mp) for t in range(1, total)]


def gather_seq_steps(net, own, seq):
    far = net.send(own, seq.at[1], net.x_n)
    near = net.send(own, seq.at[2], net.core_n)
    net.keep(own, seq.at[0])

    def finish():
        far.wait_recv()
        both = net.send(seq.at[1], seq.at[3], net.core_n)
        near.wait_recv()
        both.wait_recv()

    return finish


def gather_pair_steps(net, own, group, split=False):
    far = net.send(own, group.at[2], net.x_n)
    zed = net.send(own, group.at[1], net.z_n)
    near = net.send(own, group.at[4], net.core_n)
    net.keep(own, group.at[0])

    def finish(between=lambda: None):
        head = pl.ds(0, D // 2) if split else pl.ds(0, D)
        rest = pl.ds(D // 2, D // 2)
        zed.wait_recv()
        both = net.send(group.at[1, :, head], group.at[3, :, head], net.x_n)
        far.wait_recv()
        if split:
            other = net.send(group.at[2, :, rest], group.at[3, :, rest], net.z_n)
        near_z = net.send(group.at[1], group.at[5], net.core_n)
        near_x = net.send(group.at[2], group.at[6], net.core_n)
        between()
        both.wait_recv()
        if split:
            other.wait_recv()
        near_both = net.send(group.at[3], group.at[7], net.core_n)
        for copy in (near, near_z, near_x, near_both):
            copy.wait_recv()

    return finish


def pair_partners(net, with_y):
    nj = net.n_dp // 2
    zs = [net.z_at(d) for d in range(1, nj)] if with_y else [net.z_n]
    return [net.core_n, net.x_n] + zs + ([net.y_n] if with_y else [])


def row_tiles(total, size, body):
    lax.fori_loop(
        0, total // size, lambda t, state: (body(pl.ds(pl.multiple_of(t * size, size), size)), state)[1], 0
    )


def project(seq, wq, wkv, cosine, sine, q, k, v):
    total = seq.shape[0]
    kv_cols = k.shape[1]
    half = HEAD_WIDTH // 2

    def body(at):
        tokens = seq[at]
        c, s = cosine[at], sine[at]

        def turn(lin, out, cols):
            for h in range(0, cols, HEAD_WIDTH):
                a, b = lin[:, h : h + half], lin[:, h + half : h + HEAD_WIDTH]
                out[at, h : h + half] = (a * c - b * s).astype(BF)
                out[at, h + half : h + HEAD_WIDTH] = (b * c + a * s).astype(BF)

        turn(mm(tokens, wq[...]), q, q.shape[1])
        lin = mm(tokens, wkv[...])
        turn(lin, k, kv_cols)
        v[at] = lin[:, kv_cols:].astype(BF)

    row_tiles(total, total // 2, body)


def allowed_tile(marks_col, marks_row, at):
    segs, slots = marks_col[at, 0:1], marks_col[at, 1:2]
    seg_row, slot_row, pad_row = marks_row[0:1], marks_row[1:2], marks_row[2:3]
    same_slot = slot_row == slots
    return (seg_row == segs) & (slot_row <= slots) & ((pad_row == 1) | same_slot)


def tile_probs(q, k, allowed, at, head, group):
    cols = slice(head * HEAD_WIDTH, (head + 1) * HEAD_WIDTH)
    kv = head // group
    kv_at = slice(kv * HEAD_WIDTH, (kv + 1) * HEAD_WIDTH)
    bent = jnp.tanh(mm_cols(q[at, cols], k[:, kv_at]) * (HEAD_WIDTH**-0.5 / SOFT_CAP))
    raised = jnp.where(allowed, jnp.exp(SOFT_CAP * bent), 0.0)
    return bent, raised * (1.0 / jnp.sum(raised, axis=-1, keepdims=True))


def attend(q, k, v, marks_col, marks_row, mixed):
    total = q.shape[0]
    heads, group = q.shape[1] // HEAD_WIDTH, q.shape[1] // k.shape[1]

    def body(at):
        allowed = allowed_tile(marks_col, marks_row, at)
        for head in range(heads):
            _, probs = tile_probs(q, k, allowed, at, head, group)
            kv = head // group
            kv_at = slice(kv * HEAD_WIDTH, (kv + 1) * HEAD_WIDTH)
            mixed[at, head * HEAD_WIDTH : (head + 1) * HEAD_WIDTH] = mm(
                probs.astype(BF), v[:, kv_at]
            ).astype(BF)

    row_tiles(total, 128, body)


def out_project(mixed, wo, part):
    blocks, rows, _ = part.shape
    for pair in range(blocks // 2 - 1, -1, -1):

        def body(at, pair=pair):
            got = mm_cols(mixed[pair * 2 * rows : (pair + 1) * 2 * rows], wo[at]).astype(BF)
            part[pair * 2, :, at] = got[:rows]
            part[pair * 2 + 1, :, at] = got[rows:]

        row_tiles(D, D // 3, body)


def chunks(wrows, parts=3):
    if wrows % (16 * parts) == 0:
        return tuple((n * wrows // parts, wrows // parts) for n in range(parts))
    return ((0, upper(wrows)), (upper(wrows), wrows - upper(wrows)))


def two_parts(wrows):
    return ((0, upper(wrows)), (upper(wrows), wrows - upper(wrows)))


class Gather:
    def __init__(self, net, pieces):
        self.net, self.pieces, self.nj = net, pieces, net.n_dp // 2
        self.flight, self.relays, self.own = {}, {}, {}

    def out(self, n):
        net = self.net
        source, place, parity = self.pieces[n]
        self.own[n] = net.move(source(net.zl), place(net.i))
        self.relays[n] = [net.send(source(net.zl), place(net.i), net.y_n)]
        for d in range(1, self.nj):
            self.flight[n, d] = net.send(source((net.j + d) % self.nj % 2), place(net.i), net.z_at(d))

    def on(self, n):
        net = self.net
        _, place, _ = self.pieces[n]
        for d in range(1, self.nj):
            self.flight[n, d].wait_recv()
            at = ((net.j + self.nj - d) % self.nj) * 2 + net.y
            self.relays[n].append(net.send(place(at), place(at), net.y_n))

    def done(self, n):
        self.own.pop(n).wait()
        for copy in self.relays.pop(n):
            copy.wait_recv()


def all_of_dp(net):
    return [net.x_n, net.core_n] + [((net.i + t) % net.n_dp, net.m) for t in range(1, net.n_dp)]


def open_kernel(
    n_dp, n_mp, low_q, low_kv, low_o, w_mlp, width_mlp, cosine, sine, marks_col, marks_row, inputs, own_gains,
    q, k, v, mixed, att, hid, gains, group, full0, full1, full2, out_q, out_kv, out_o, out_seq,
    wq, wkv, wo, seq, part, r1, r2, own, got_gains, masters, lows, ss, rs, ls,
):
    net = Net(n_dp, n_mp, ss, rs, ls)
    p = net.place()
    right = (net.ring(p + 1), net.m)
    left = (net.ring(p + n_dp - 1), net.m)
    rows = inputs.shape[0]
    wrows, width = full0.shape[1:]
    others = everyone(n_dp, n_mp, net.i, net.m)
    net.meet(others)
    flat = net.i * n_mp + net.m
    loads = [net.move(w_mlp.at[n], masters.at[n]) for n in range(3)]

    def block(ref, at):
        return ref.at[pl.ds(pl.multiple_of(at * wrows, 8), wrows)]

    def lot(n):
        return seq.at[pl.ds(n * rows, rows)]

    def piece(ref, at, part):
        first, count = part
        return ref.at[pl.ds(pl.multiple_of(at * wrows + first, 8), count)]

    parts = two_parts(wrows)
    flight = {}
    for cut in parts:
        for lane, (ref, low, device) in enumerate(((wq, low_q, right), (wkv, low_kv, left))):
            flight[cut, lane] = net.send(low.at[pl.ds(*cut)], piece(ref, net.i, cut), device)
    spread = [net.send(own_gains, got_gains.at[flat], device) for device in others]
    net.move(own_gains, got_gains.at[flat]).wait()
    for copy in spread:
        copy.wait_recv()
    per_norm = n_dp * n_mp // NORMS
    for n in range(NORMS):
        gains[n : n + 1] = jnp.concatenate([got_gains[n * per_norm + t] for t in range(per_norm)], 1)
    g0 = 1.0 + gains[0:1]

    def norm_rows(at, state):
        own[at] = (inputs[at] * inv_root(inputs[at]) * g0).astype(BF)
        return state

    by_rows(rows, norm_rows)
    far = net.send(own, lot(1), net.x_n)
    near = net.send(own, lot(2), net.core_n)

    def quantize_part(n):
        loads[n].wait()
        spacing = width_mlp[...]
        step = jnp.float32(1.0 / (32.0 * math.sqrt(FF if n == 2 else D)))

        def body(at, state, count):
            lows[n, at] = quantize_values(masters[n, at], step, spacing).astype(BF)
            return state

        in_steps(wrows, body)

    own_parts = [net.move(own, lot(0)), net.move(low_q, block(wq, net.i)), net.move(low_kv, block(wkv, net.i))]
    half = lambda which: pl.ds(pl.multiple_of(which * width, width), width)
    pieces = [(lambda which: low_o, lambda at: block(wo, at), 1)]

    def add_piece(ref, full, first, count):
        rows_at = pl.ds(first, count)
        pieces.append((lambda which: ref.at[rows_at, half(which)], lambda at: full.at[at, rows_at], 2))

    for ref, full, cuts in ((lows.at[0], full0, 3), (lows.at[1], full1, 3), (lows.at[2], full2, 6)):
        for first, count in chunks(wrows, cuts):
            add_piece(ref, full, first, count)
    weights = Gather(net, pieces)
    for hop in range(1, n_dp):
        from_right, from_left = net.ring(p + n_dp - hop), net.ring(p + hop)
        for cut in parts:
            for lane, (ref, at, device) in enumerate(((wq, from_right, right), (wkv, from_left, left))):
                flight[cut, lane].wait_recv()
                if hop < n_dp - 1:
                    flight[cut, lane] = net.send(piece(ref, at, cut), piece(ref, at, cut), device)
        if hop == n_dp // 2:
            far.wait_recv()
            both = net.send(lot(1), lot(3), net.core_n)
        if hop in (1, 2, 3):
            quantize_part(hop - 1)
        if hop == n_dp - 2:
            weights.out(0)
    weights.out(1)
    weights.out(2)
    weights.out(3)
    near.wait_recv()
    both.wait_recv()
    for copy in own_parts:
        copy.wait()
    net.sent(far)
    net.sent(near)
    for ref, result in ((wq, out_q), (wkv, out_kv), (seq, out_seq)):
        net.keep(ref, result)
    project(seq, wq, wkv, cosine, sine, q, k, v)
    attend(q, k, v, marks_col, marks_row, mixed)
    def step(n):
        if n < len(pieces):
            weights.on(n)
            if n + 4 < len(pieces):
                weights.out(n + 4)

    step(0)
    weights.done(0)
    net.keep(wo, out_o)
    out_project(mixed, wo, part)
    c1 = net.send(part.at[3], r1.at[1], net.core_n)
    c0 = net.send(part.at[2], r1.at[0], net.core_n)
    c1.wait_recv()

    def first_rows(at, state):
        part[1, at] = (part[1, at].astype(F32) + r1[1, at].astype(F32)).astype(BF)
        return state

    by_rows(rows, first_rows)
    x = net.send(part.at[1], r2, net.x_n)
    c0.wait_recv()
    step(1)
    x.wait_recv()
    g1, g2 = 1.0 + gains[1:2], 1.0 + gains[2:3]

    def second(at, state):
        total = part[0, at].astype(F32) + r1[0, at].astype(F32) + r2[at].astype(F32)
        att[at] = total
        hidden = inputs[at] + total * inv_root(total) * g1
        hid[at] = hidden
        own[at] = (hidden * inv_root(hidden) * g2).astype(BF)
        return state

    by_rows(rows, second)
    finish = gather_pair_steps(net, own, group)
    step(2)
    step(3)
    finish(lambda: (step(4), step(5)))
    for n in range(6, len(pieces)):
        step(n)
    for n in range(1, len(pieces)):
        weights.done(n)
    net.close()


def open_layer(n_dp, n_mp, low_q, low_kv, low_o, w_mlp, width_mlp, cosine, sine, marks_col, marks_row, inputs, gains):
    rows = inputs.shape[0]
    nj = n_dp // 2
    total_devices = n_dp * n_mp
    count = 24 + 4 * n_dp + 28 * nj + total_devices
    block = (rows, D)
    wrows, width = w_mlp.shape[1], w_mlp.shape[2] // 2
    cols, kv_cols = low_q.shape[1], low_kv.shape[1] // 2
    vm = lambda *shape: pltpu.VMEM(shape, BF)
    bf = lambda *shape: jax.ShapeDtypeStruct(shape, BF)
    total = 4 * rows
    f32 = jax.ShapeDtypeStruct(block, F32)
    full = bf(n_dp, wrows, width)
    return call(
        functools.partial(open_kernel, n_dp, n_mp),
        [
            bf(total, cols), bf(total, kv_cols), bf(total, kv_cols), bf(total, cols), f32, f32,
            jax.ShapeDtypeStruct((NORMS, D), F32),
            bf(8, *block), full, full, full, bf(D, cols), bf(D, 2 * kv_cols), bf(D, cols), bf(total, D),
        ],
        [VMEM] * 7 + [ANY] * 8, [ANY] * 4 + [VMEM] * 7,
        [
            vm(D, cols), vm(D, 2 * kv_cols), vm(D, cols), vm(total, D), vm(4, *block), vm(2, *block), vm(*block),
            vm(*block), pltpu.VMEM((total_devices,) + gains.shape, F32), pltpu.VMEM(w_mlp.shape, F32),
            vm(*w_mlp.shape), dma(count), dma(count), dma(32),
        ],
        2, 60,
    )(low_q, low_kv, low_o, w_mlp, width_mlp, cosine, sine, marks_col, marks_row, inputs, gains)


def reduce_pair_steps(net, near, cores, r1, r2, r3, rows, split=False, compute=None, hooks=None):
    plan = [(pl.ds(0, D // 2 if split else D), (3, 2), net.x_n, 1, net.z_n)]
    if split:
        plan.append((pl.ds(D // 2, D // 2), (3, 1), net.z_n, 2, net.x_n))
    firsts = {}
    for k in (3, 2, 1) if split else (3, 2):
        compute(k)
        cores(k).wait_recv()
        for part, (cols, blocks, device, _, _) in enumerate(plan):
            if k not in blocks:
                continue
            at_block = blocks.index(k)

            def add(at, state, k=k, cols=cols):
                near[k, at, cols] = (near[k, at, cols].astype(F32) + r1[k, at, cols].astype(F32)).astype(BF)
                return state

            by_rows(rows, add)
            firsts[part, at_block] = net.send(near.at[k, :, cols], r2.at[at_block, :, cols], device)
    for k in (0,) if split else (1, 0):
        compute(k)
        cores(k).wait_recv()
    last = []
    if hooks:
        hooks[0]()
    for part, (cols, blocks, _, second, device) in enumerate(plan):
        firsts[part, 0].wait_recv()

        def add(at, state, cols=cols, second=second):
            near[second, at, cols] = (
                near[second, at, cols].astype(F32) + r1[second, at, cols].astype(F32) + r2[0, at, cols].astype(F32)
            ).astype(BF)
            return state

        by_rows(rows, add)
        last.append(net.send(near.at[second, :, cols], r3.at[:, cols], device))
    if hooks:
        hooks[1]()
    for part in range(len(plan)):
        firsts[part, 1].wait_recv()
    return last


def pair_sum(near, r1, r2, r3, at):
    return near[0, at].astype(F32) + r1[0, at].astype(F32) + r2[1, at].astype(F32) + r3[at].astype(F32)


def pair_scratch(rows, blocks=8):
    block = (rows, D)
    return [
        pltpu.VMEM((blocks,) + block, BF), pltpu.VMEM((4,) + block, BF), pltpu.VMEM((2,) + block, BF),
        pltpu.VMEM(block, BF), pltpu.VMEM(block, BF),
    ]


def core_family(net, parts, r1):
    return net.family(
        4,
        lambda k, send, recv: pltpu.make_async_remote_copy(
            src_ref=parts.at[4 + k], dst_ref=r1.at[k], send_sem=send, recv_sem=recv,
            device_id=net.core_n, device_id_type=MESH,
        ),
    )


def block_at(t):
    return 7 - t // 2 - 4 * (t % 2)


class Stream:
    def __init__(self, net, pairs, inward):
        self.net, self.pairs, self.inward = net, pairs, inward
        self.base = net.locals(2 * len(pairs))

    def copies(self, t):
        slot = t % 2
        for n, (far, held) in enumerate(self.pairs):
            ends = (far.at[block_at(t)], held.at[slot])
            yield pltpu.make_async_copy(
                *(ends if self.inward else ends[::-1]), self.net.local_sems.at[self.base + 2 * n + slot]
            )

    def start(self, t):
        for copy in self.copies(t):
            copy.start()

    def wait(self, t):
        for copy in self.copies(t):
            copy.wait()


def rms_back_rows(values, gain, grad):
    root = inv_root(values)
    scaled = grad * gain
    dot = jnp.mean(values * scaled, axis=-1, keepdims=True)
    return root * scaled - values * (root * root * root * dot), jnp.sum(values * root * grad, axis=0, keepdims=True)


def turn_kernel(
    n_dp, n_mp, ffn, w_gate, w_up, w_down, hid, gains, out_grad, live,
    outputs, dgain, gate, up, act, group,
    parts, r1, r2, r3, own, wg, wu, wd, tokens, gate_b, up_b, act_b, ss, rs, ls,
):
    net = Net(n_dp, n_mp, ss, rs, ls)
    loads = [net.move(src, dst) for src, dst in ((w_gate, wg), (w_up, wu), (w_down, wd))]
    rows = hid.shape[0]
    incoming = Stream(net, [(ffn, tokens)], True)
    outgoing = Stream(net, [(gate, gate_b), (up, up_b), (act, act_b)], False)
    cores = core_family(net, parts, r1)
    incoming.start(0)
    net.meet(pair_partners(net, False))
    for load in loads:
        load.wait()

    def block(t, state):
        slot, at = t % 2, block_at(t)
        incoming.wait(t)

        @pl.when(t < 7)
        def _():
            incoming.start(t + 1)

        g = mm(tokens[slot], wg[...])
        u = mm(tokens[slot], wu[...])
        bend = jnp.tanh(GELU * (g + 0.044715 * (g * g * g)))
        a = (0.5 * g * (1.0 + bend) * u).astype(BF)

        @pl.when(t >= 2)
        def _():
            outgoing.wait(t - 2)

        gate_b[slot] = g
        up_b[slot] = u
        act_b[slot] = a
        outgoing.start(t)
        parts[at] = mm_cols(a, wd[...]).astype(BF)
        return state

    def compute(k):
        def both(t, state):
            block(t, state)

            @pl.when(t % 2 == 0)
            def _():
                cores(k).start()

            return state

        lax.fori_loop(6 - 2 * k, 8 - 2 * k, both, 0)

    last_sums = reduce_pair_steps(net, parts, cores, r1, r2, r3, rows, True, compute)
    outgoing.wait(6)
    outgoing.wait(7)
    for copy in last_sums:
        copy.wait_recv()
    g3 = 1.0 + gains[3:4]

    def last(at, state):
        total = pair_sum(parts, r1, r2, r3, at)
        outputs[at] = hid[at] + total * inv_root(total) * g3
        grad, dg = rms_back_rows(total, g3, out_grad[at] * live[at])
        own[at] = grad.astype(BF)
        return state + dg

    dgain[...] = by_rows(rows, last, jnp.zeros((1, D), F32))
    gather_pair_steps(net, own, group, True)()
    net.close()


def turn(n_dp, n_mp, ffn, w_gate, w_up, w_down, hid, gains, out_grad, live):
    rows = hid.shape[0]
    block = (rows, D)
    width = w_gate.shape[1]
    vm = lambda *shape: pltpu.VMEM(shape, BF)
    return call(
        functools.partial(turn_kernel, n_dp, n_mp),
        [
            jax.ShapeDtypeStruct(block, F32), jax.ShapeDtypeStruct((1, D), F32),
            jax.ShapeDtypeStruct((8, rows, width), F32), jax.ShapeDtypeStruct((8, rows, width), F32),
            jax.ShapeDtypeStruct((8, rows, width), BF), jax.ShapeDtypeStruct((8,) + block, BF),
        ],
        [VMEM, VMEM] + [ANY] * 4, [ANY] * 4 + [VMEM] * 4,
        pair_scratch(rows)
        + [
            vm(D, width), vm(D, width), vm(D, width), vm(2, *block),
            pltpu.VMEM((2, rows, width), F32), pltpu.VMEM((2, rows, width), F32), vm(2, rows, width),
            dma(32), dma(32), dma(16),
        ],
        4, 60,
    )(ffn, w_gate, w_up, w_down, hid, gains, out_grad, live)


def in_steps(count, body, carry=0, first=0):
    step = 16 if count % 16 == 0 else 8
    return lax.fori_loop(
        0, count // step,
        lambda t, state: body(pl.ds(pl.multiple_of(first + t * step, 8), step), state, step), carry,
    )


def square_tile(value):
    value = value * value
    total = jnp.zeros((8, 128), F32)
    for r in range(0, value.shape[0], 8):
        for c in range(0, value.shape[1], 128):
            total = total + value[r : r + 8, c : c + 128]
    return total


class Scatter:
    def __init__(self, net, grads, stay, came, last):
        self.net, self.grads, self.stay, self.came, self.last = net, grads, stay, came, last
        self.nj, self.wrows, self.width = came.shape
        self.turns = sorted(range(1, self.nj), key=lambda d: abs(d - self.nj // 2)) + [0]
        self.ys, self.moves, self.zs = {}, {}, {}

    def along_y(self, turns=None):
        net = self.net
        for d in self.turns if turns is None else turns:
            at = (net.j + d) % self.nj
            self.ys[d] = net.send(self.grads.at[at, 1 - net.y], self.came.at[d], net.y_n)
            self.moves[d] = net.move(self.grads.at[at, net.y], self.stay.at[d])

    def along_z(self, turns):
        for d in turns:
            self.ys[d].wait_recv()
            self.moves[d].wait()

            def add(at, state, step, d=d):
                self.stay[d, at] = (self.stay[d, at].astype(F32) + self.came[d, at].astype(F32)).astype(BF)
                return state

            in_steps(self.wrows, add)
            if d:
                self.zs[d] = self.net.send(self.stay.at[d], self.last.at[d - 1], self.net.z_at(d))

    def landed(self):
        for d in range(1, self.nj):
            self.zs[d].wait_recv()

    def halves(self, total, sums):
        self.landed()

        def collect(at, state, step):
            both = [self.stay[0, at].astype(F32), jnp.zeros((step, self.width), F32)]
            for d in range(1, self.nj):
                both[d % 2] = both[d % 2] + self.last[d - 1, at].astype(F32)
            for parity in range(2):
                total[parity, at] = both[parity]
                state = state + square_tile(both[parity])
            return state

        square = in_steps(self.wrows, collect, jnp.zeros((8, 128), F32))
        copies = []
        for parity in range(2):
            half = (self.net.zl + parity) % 2
            copies.append(self.net.move(total.at[parity], sums.at[:, pl.ds(pl.multiple_of(half * self.width, self.width), self.width)]))
        return copies, square

    def whole(self, out):
        self.landed()

        def collect(at, state, step):
            value = self.stay[0, at].astype(F32)
            for d in range(1, self.nj):
                value = value + self.last[d - 1, at].astype(F32)
            out[at] = value
            return state

        in_steps(self.wrows, collect)


def scatter_scratch(nj, wrows, width):
    return [
        pltpu.VMEM((nj, wrows, width), BF), pltpu.VMEM((nj, wrows, width), BF),
        pltpu.VMEM((nj - 1, wrows, width), BF),
    ]


def back_kernel(
    n_dp, n_mp, part, hid, att, gains, out_grad, live, grads, grads_up,
    ghid, dg1, dg2, seq, sums, sums_up, squares,
    near, r1, r2, r3, own, stay, came, last, ustay, ucame, ulast, total, ss, rs, ls,
):
    net = Net(n_dp, n_mp, ss, rs, ls)
    loaded = net.move(part.at[pl.ds(0, 4)], near)
    cores = core_family(net, part, r1)
    net.meet(pair_partners(net, True))
    rows = hid.shape[0]
    for k in (3, 2, 1, 0):
        cores(k).start()
    weight = Scatter(net, grads, stay, came, last)
    weight_up = Scatter(net, grads_up, ustay, ucame, ulast)
    weight.along_y()
    loaded.wait()
    last_sums = reduce_pair_steps(
        net, near, cores, r1, r2, r3, rows, False, lambda k: None,
        (lambda: weight.along_z(weight.turns[:1]), lambda: weight.along_z(weight.turns[1:2])),
    )
    weight_up.along_y()
    for copy in last_sums:
        copy.wait_recv()
    g1, g2 = 1.0 + gains[1:2], 1.0 + gains[2:3]

    def rows_back(at, state):
        grad = pair_sum(near, r1, r2, r3, at)
        part_hid, d2 = rms_back_rows(hid[at], g2, grad)
        grad_hidden = out_grad[at] * live[at] + part_hid
        ghid[at] = grad_hidden
        grad_att, d1 = rms_back_rows(att[at], g1, grad_hidden)
        own[at] = grad_att.astype(BF)
        return state[0] + d1, state[1] + d2

    zero = jnp.zeros((1, D), F32)
    done1, done2 = by_rows(rows, rows_back, (zero, zero))
    dg1[...] = done1
    dg2[...] = done2
    finish = gather_seq_steps(net, own, seq)
    weight.along_z(weight.turns[2:])
    weight_up.along_z(weight_up.turns[:1])
    finish()
    weight_up.along_z(weight_up.turns[1:2])
    first_out, square = weight.halves(total, sums)
    weight_up.along_z(weight_up.turns[2:])
    for copy in first_out:
        copy.wait()
    last_out, square_up = weight_up.halves(total, sums_up)
    squares[...] = square + square_up
    for copy in last_out:
        copy.wait()
    net.close()


def back(n_dp, n_mp, part, hid, att, gains, out_grad, live, grads, grads_up):
    rows = hid.shape[0]
    block = (rows, D)
    nj = n_dp // 2
    _, _, wrows, width = grads.shape
    count = 24 + 6 * nj
    return call(
        functools.partial(back_kernel, n_dp, n_mp),
        [
            jax.ShapeDtypeStruct(block, F32), jax.ShapeDtypeStruct((1, D), F32), jax.ShapeDtypeStruct((1, D), F32),
            jax.ShapeDtypeStruct((4,) + block, BF), jax.ShapeDtypeStruct((wrows, 2 * width), F32),
            jax.ShapeDtypeStruct((wrows, 2 * width), F32), jax.ShapeDtypeStruct((8, 128), F32),
        ],
        [VMEM, VMEM, VMEM, ANY, ANY, ANY, VMEM], [ANY] + [VMEM] * 5 + [ANY, ANY],
        pair_scratch(rows, 4) + scatter_scratch(nj, wrows, width) * 2
        + [pltpu.VMEM((2, wrows, width), F32), dma(count), dma(count), dma(16 + 2 * nj)],
        5, 60,
    )(part, hid, att, gains, out_grad, live, grads, grads_up)


def attend_back(q, k, v, gm, marks_col, marks_row, cosine, sine, dq, dk, dv, tiles):
    total = q.shape[0]
    heads, group = q.shape[1] // HEAD_WIDTH, q.shape[1] // k.shape[1]
    size = total // 4
    half = HEAD_WIDTH // 2
    scale = HEAD_WIDTH**-0.5

    def body(t, state):
        at = pl.ds(pl.multiple_of(t * size, size), size)
        allowed = allowed_tile(marks_col, marks_row, at)
        c, s = cosine[at], sine[at]
        for head in range(heads):
            kv = head // group
            cols = slice(head * HEAD_WIDTH, (head + 1) * HEAD_WIDTH)
            kv_at = slice(kv * HEAD_WIDTH, (kv + 1) * HEAD_WIDTH)
            bent, probs = tile_probs(q, k, allowed, at, head, group)
            grad = gm[at, cols]
            dv[:, kv_at] += mm_rows(probs.astype(BF), grad)
            gp = mm_cols(grad, v[:, kv_at])
            inner = jnp.sum(probs * gp, axis=-1, keepdims=True)
            ds = (probs * (gp - inner) * (1.0 - bent * bent)).astype(BF)
            dk[:, kv_at] += mm_rows(ds, q[at, cols]) * scale
            turned = mm(ds, k[:, kv_at]) * scale
            a, b = turned[:, :half], turned[:, half:]
            first = head * HEAD_WIDTH
            dq[at, first : first + half] = (a * c + b * s).astype(BF)
            dq[at, first + half : first + HEAD_WIDTH] = (b * c - a * s).astype(BF)
        return state

    lax.fori_loop(tiles[0], tiles[1], body, 0)


def weight_grad(tokens, grads, out):
    def body(at):
        out[at] = mm_rows(tokens[:, at], grads[...]).astype(BF)

    row_tiles(D, D // 3, body)


def close_kernel(
    n_dp, n_mp, seq_grad, seq_normed, q, k, v, mixed, wo, wq, wkv, cosine, sine, marks_col, marks_row,
    inputs, gains, ghid, terms_in, sum_down, squares,
    gin, sum_q, sum_kv, sum_o, gain_sum, norm,
    terms, got_terms, down, mine, got_squares, tokens, normed, wa, gm, dq, dk, dv, dkv, go, gq, gkv, got_q, got_kv, r1, r2,
    ostay, ocame, olast, ss, rs, ls,
):
    net = Net(n_dp, n_mp, ss, rs, ls)
    p = net.place()
    right = (net.ring(p + 1), net.m)
    left = (net.ring(p + n_dp - 1), net.m)
    nj = n_dp // 2
    rows = inputs.shape[0]
    seq_len, wrows = tokens.shape[0], sum_q.shape[0]
    wide0 = terms.shape[2]
    others = everyone(n_dp, n_mp, net.i, net.m)
    flat = net.i * n_mp + net.m
    per_norm = n_dp * n_mp // NORMS
    terms_load = net.move(terms_in, terms.at[pl.ds(per_norm, (NORMS - 1) * per_norm)])
    down_load = net.move(sum_down, down)
    net.meet(others)
    token_load = net.move(seq_grad, tokens)
    wa_load = net.move(wo, wa)
    normed_load = net.move(seq_normed, normed)
    ghid_load = net.move(ghid, gin)
    dk[...] = jnp.zeros_like(dk)
    dv[...] = jnp.zeros_like(dv)
    token_load.wait()
    wa_load.wait()

    def mix(at):
        gm[at] = mm(tokens[at], wa[...]).astype(BF)

    row_tiles(seq_len, seq_len // 2, mix)
    wa_load = net.move(wq, wa)
    weight_grad(tokens, mixed, go.reshape(D, go.shape[-1]))
    out = Scatter(net, go, ostay, ocame, olast)
    out.along_y()
    attend_back(q, k, v, gm, marks_col, marks_row, cosine, sine, dq, dk, dv, (0, 2))
    out.along_z(out.turns[:1])
    attend_back(q, k, v, gm, marks_col, marks_row, cosine, sine, dq, dk, dv, (2, 4))
    out.along_z(out.turns[1:])
    kv_cols = k.shape[1]
    half = HEAD_WIDTH // 2

    def turn_keys(at):
        c, s = cosine[at], sine[at]
        for h in range(0, kv_cols, HEAD_WIDTH):
            a, b = dk[at, h : h + half], dk[at, h + half : h + HEAD_WIDTH]
            dkv[at, h : h + half] = (a * c + b * s).astype(BF)
            dkv[at, h + half : h + HEAD_WIDTH] = (b * c - a * s).astype(BF)
        dkv[at, kv_cols:] = dv[at].astype(BF)

    row_tiles(seq_len, 128, turn_keys)
    normed_load.wait()
    weight_grad(normed, dq, gq)
    weight_grad(normed, dkv, gkv)

    def block(at, part):
        return pl.ds(pl.multiple_of(net.ring(p + 2 * n_dp + at) * wrows + part[0], 8), part[1])

    lanes = ((gq, got_q, sum_q, right, -1), (gkv, got_kv, sum_kv, left, 1))
    parts = two_parts(wrows)
    flight = {}
    for part in parts:
        for lane, (ref, got, _, device, way) in enumerate(lanes):
            flight[lane, part] = net.send(ref.at[block(way, part)], got.at[0, pl.ds(*part)], device)

    def hop(n):
        end = n == n_dp - 1
        for part in parts:
            for lane, (terms, got, result, device, way) in enumerate(lanes):
                flight[lane, part].wait_recv()
                first = net.ring(p + 2 * n_dp + way * (1 + n)) * wrows

                def add(here, state, step, first=first, terms=terms, got=got, result=result):
                    at = pl.ds(pl.multiple_of(first + here.start, 8), step)
                    value = got[n - 1, here].astype(F32) + terms[at].astype(F32)
                    if end:
                        result[here] = value
                    else:
                        terms[at] = value.astype(BF)
                    return state

                in_steps(part[1], add, 0, part[0])
                if not end:
                    flight[lane, part] = net.send(
                        terms.at[block(way * (1 + n), part)], got.at[n, pl.ds(*part)], device
                    )

    wa_load.wait()
    for pair in (1, 0):
        at = pl.ds(pair * 2 * rows, 2 * rows)

        def body(n, at=at):
            tokens[at, n] = (mm_cols(dq[at], wa[n]) + mm_cols(dkv[at], wkv[n])).astype(BF)

        row_tiles(D, D // 3, body)
        if pair:
            c1 = net.send(tokens.at[pl.ds(3 * rows, rows)], r1.at[1], net.core_n)
            c0 = net.send(tokens.at[pl.ds(2 * rows, rows)], r1.at[0], net.core_n)
            hop(1)
    c1.wait_recv()

    def add_far(at, state):
        here = pl.ds(pl.multiple_of(rows + at.start, ROWS), ROWS)
        tokens[here] = (tokens[here].astype(F32) + r1[1, at].astype(F32)).astype(BF)
        return state

    by_rows(rows, add_far)
    x = net.send(tokens.at[pl.ds(rows, rows)], r2, net.x_n)
    c0.wait_recv()
    hop(2)
    hop(3)
    x.wait_recv()
    ghid_load.wait()
    g0 = 1.0 + gains[0:1]

    def rows_in(at, state):
        grad = tokens[at].astype(F32) + r1[0, at].astype(F32) + r2[at].astype(F32)
        part, d0 = rms_back_rows(inputs[at], g0, grad)
        gin[at] = gin[at] + part
        return state + d0

    dg0 = by_rows(rows, rows_in, jnp.zeros((1, D), F32))
    terms_load.wait()
    for n in range(per_norm):
        terms[n] = dg0[:, n * wide0 : (n + 1) * wide0]
    spread = [net.send(terms.at[dp * n_mp + mp], got_terms.at[flat], (dp, mp)) for dp, mp in others]
    own_terms = net.move(terms.at[flat], got_terms.at[flat])
    for n in range(4, n_dp - 1):
        hop(n)
    down_load.wait()

    def square_of(ref, state):
        return lax.fori_loop(
            0, ref.shape[0] // 8,
            lambda t, total: total + square_tile(ref[pl.ds(pl.multiple_of(t * 8, 8), 8)]), state,
        )

    square = square_of(down, squares[...])
    out.whole(sum_o)
    square = square_of(sum_o, square)
    own_terms.wait()
    for copy in spread:
        copy.wait_recv()
    total_gain = lax.fori_loop(
        0, n_dp * n_mp, lambda t, total: total + got_terms[t], jnp.zeros(got_terms.shape[1:], F32)
    )
    gain_sum[...] = total_gain
    square = square + jnp.sum(total_gain * total_gain) * (1.0 / 1024.0)
    hop(n_dp - 1)
    mine[...] = square_of(sum_kv, square_of(sum_q, square))
    spread = [net.send(mine, got_squares.at[flat], device) for device in others]
    net.move(mine, got_squares.at[flat]).wait()
    for copy in spread:
        copy.wait_recv()
    total = lax.fori_loop(0, n_dp * n_mp, lambda t, value: value + got_squares[t], jnp.zeros((8, 128), F32))
    norm[...] = jnp.broadcast_to(jnp.sqrt(jnp.sum(total, axis=(0, 1), keepdims=True)), (8, 128))
    net.close()


def close(n_dp, n_mp, seq_grad, seq_normed, q, k, v, mixed, wo, wq, wkv, cosine, sine, marks_col, marks_row,
          inputs, gains, ghid, terms, sum_down, squares):
    rows = inputs.shape[0]
    nj = n_dp // 2
    wrows = D // n_dp
    cols, kv_cols = q.shape[1], k.shape[1]
    seq_len = q.shape[0]
    devices = n_dp * n_mp
    count = 16 + 6 * nj + 4 * n_dp + 2 * devices
    piece = (1, NORMS * D // devices)
    vm = lambda *shape: pltpu.VMEM(shape, BF)
    small = jax.ShapeDtypeStruct((wrows, cols), F32)
    return call(
        functools.partial(close_kernel, n_dp, n_mp),
        [
            jax.ShapeDtypeStruct((rows, D), F32), small, jax.ShapeDtypeStruct((wrows, 2 * kv_cols), F32), small,
            jax.ShapeDtypeStruct(piece, F32), jax.ShapeDtypeStruct((8, 128), F32),
        ],
        [VMEM] * 6,
        [ANY, ANY] + [VMEM] * 4 + [ANY, ANY] + [VMEM] * 7 + [ANY] * 3 + [VMEM],
        [
            pltpu.VMEM((devices,) + piece, F32), pltpu.VMEM((devices,) + piece, F32),
            pltpu.VMEM(sum_down.shape, F32), pltpu.VMEM((8, 128), F32), pltpu.VMEM((devices, 8, 128), F32),
            vm(seq_len, D), vm(seq_len, D), vm(D, cols), vm(seq_len, cols), vm(seq_len, cols),
            pltpu.VMEM((seq_len, kv_cols), F32), pltpu.VMEM((seq_len, kv_cols), F32), vm(seq_len, 2 * kv_cols),
            vm(nj, 2, wrows, cols), vm(D, cols), vm(D, 2 * kv_cols),
            vm(n_dp - 1, wrows, cols), vm(n_dp - 1, wrows, 2 * kv_cols), vm(2, rows, D), vm(rows, D),
        ]
        + scatter_scratch(nj, wrows, cols) + [dma(count), dma(count), dma(14 + 2 * nj)],
        6, 60,
    )(seq_grad, seq_normed, q, k, v, mixed, wo, wq, wkv, cosine, sine, marks_col, marks_row,
      inputs, gains, ghid, terms, sum_down, squares)


def plain(kernel, grid, outs, out_specs, in_specs, mb, flops):
    return pl.pallas_call(
        kernel,
        out_shape=outs,
        grid=grid,
        in_specs=in_specs,
        out_specs=out_specs,
        compiler_params=pltpu.CompilerParams(
            dimension_semantics=("arbitrary",) * len(grid), vmem_limit_bytes=mb << 20
        ),
        cost_estimate=pl.CostEstimate(flops=flops, bytes_accessed=40 << 20, transcendentals=0),
    )


def whole(shape):
    return pl.BlockSpec(shape, lambda t: (0,) * len(shape), pipeline_mode=pl.Buffered(1))


def tile(rows, cols):
    return pl.BlockSpec((None, rows, cols), lambda t: (t, 0, 0))


GELU = math.sqrt(2.0 / math.pi)


def down_back_kernel(grad, gate, up, wg, wu, wd, dgate, dup, part):
    ga = mm(grad[...], wd[...])
    g = gate[...]
    square = g * g
    bend = jnp.tanh(GELU * (g + 0.044715 * (square * g)))
    halved = 0.5 * (1.0 + bend)
    slope = halved + (0.5 * GELU) * g * (1.0 - bend * bend) * (1.0 + (3.0 * 0.044715) * square)
    dg = (ga * up[...] * slope).astype(BF)
    du = (ga * (g * halved)).astype(BF)
    dgate[...] = dg
    dup[...] = du
    part[...] = (mm_cols(dg, wg[...]) + mm_cols(du, wu[...])).astype(BF)


def mlp_back(grad, gate, up, wg, wu, wd):
    real_blocks, real_rows, _ = grad.shape
    width = wg.shape[1]
    blocks, rows = real_blocks // 2, real_rows * 2
    grad, gate, up = (a.reshape(blocks, rows, a.shape[2]) for a in (grad, gate, up))
    shape = (blocks, rows, width)
    dgate, dup, part = plain(
        down_back_kernel, (blocks,),
        [jax.ShapeDtypeStruct(shape, BF), jax.ShapeDtypeStruct(shape, BF), jax.ShapeDtypeStruct((blocks, rows, D), BF)],
        [tile(rows, width), tile(rows, width), tile(rows, D)],
        [tile(rows, D), tile(rows, width), tile(rows, width)] + [whole(wg.shape)] * 3, 56,
        6 * blocks * rows * D * width,
    )(grad, gate, up, wg, wu, wd)
    return dgate, dup, part.reshape(real_blocks, real_rows, D)


def adam_kernel(norm, gain_grad, gw, gm, gv, g_gate, g_up, g_down, g_q, g_o, g_kv, *refs):
    ins, gain_outs, outs = refs[:9], refs[9:12], refs[12:]
    factor = jnp.minimum(1.0, CLIP_SCALE * math.sqrt(PARAMS) / norm[0:1, 0:1])
    news = adam_update(gw[...], gm[...], gv[...], gain_grad[0], factor[0])
    for out, new in zip(gain_outs, news):
        out[...] = new
    kv_cols = ins[6].shape[2]
    grads = (
        (lambda: g_gate[...], lambda: g_up[...], lambda: g_down[...]),
        (lambda: g_q[...], lambda: g_o[...]),
        (lambda: g_kv[:, :kv_cols], lambda: g_kv[:, kv_cols:]),
    )
    for n, group in enumerate(grads):
        w, m, v = ins[3 * n : 3 * n + 3]
        for k, grad in enumerate(group):
            news = adam_update(w[k], m[k], v[k], grad(), factor)
            for out, new in zip(outs[3 * n : 3 * n + 3], news):
                out[k] = new


def adam_all(norm, gain_grad, gains, grads, states):
    wrows = grads[0].shape[0]
    step = 48 if wrows % 48 == 0 else 8
    like = lambda a: jax.ShapeDtypeStruct(a.shape, F32)
    fixed = lambda a: pl.BlockSpec(a.shape, lambda t: (0,) * a.ndim)
    flat = lambda a: pl.BlockSpec((step, a.shape[1]), lambda t: (t, 0))
    deep = lambda a: pl.BlockSpec((a.shape[0], step, a.shape[2]), lambda t: (0, t, 0))
    return plain(
        adam_kernel, (wrows // step,), [like(a) for a in gains] + [like(a) for a in states],
        [fixed(a) for a in gains] + [deep(a) for a in states],
        [fixed(a) for a in (norm, gain_grad) + tuple(gains)] + [flat(a) for a in grads] + [deep(a) for a in states],
        56, 100,
    )(norm, gain_grad, *gains, *grads, *states)


def build_local(n_dp, n_mp):
    nj = n_dp // 2

    def y_swap(value):
        return lax.ppermute(value, "dp", [(k, k ^ 1) for k in range(n_dp)])

    def z_shift(value, d):
        pairs = [(a * 2 + b, ((a + d) % nj) * 2 + b) for a in range(nj) for b in range(2)]
        return lax.ppermute(value, "dp", pairs)

    def scatter_first(grad, y):
        away = lax.dynamic_index_in_dim(grad, 1 - y, 1, keepdims=False)
        stay = lax.dynamic_index_in_dim(grad, y, 1, keepdims=False)
        return stay, y_swap(away)

    def scatter_second(stay, came, j):
        both = (stay.astype(F32) + came.astype(F32)).astype(BF)
        both = [lax.dynamic_index_in_dim(both, (j + d) % nj, 0, keepdims=False) for d in range(nj)]
        return both[0], [z_shift(both[d], d) for d in range(1, nj)]

    def local(
        inputs, out_grad, segment_ids, pad_mask, bit_sel, w_qo, w_kv, w_mlp, norm_gains,
        m_qo, m_kv, m_mlp, m_gains, v_qo, v_kv, v_mlp, v_gains,
    ):
        i, m = lax.axis_index("dp"), lax.axis_index("mp")
        y, j = i % 2, i // 2
        zl = j % 2
        rows = inputs.shape[0]
        seq_len = segment_ids.shape[1]
        wrows = w_qo.shape[1]

        low_q = quantize(w_qo[0], D, bit_sel[0])
        low_o = quantize(w_qo[1], QW, bit_sel[0])
        low_kv = jnp.concatenate([quantize(w_kv[0], D, bit_sel[1]), quantize(w_kv[1], D, bit_sel[1])], 1)
        order = jnp.stack([m, m ^ 2, m ^ 1, m ^ 3])

        segments = segment_ids[0]
        every = jnp.arange(seq_len, dtype=jnp.int32)
        same = segments[:, None] == segments[None, :]
        begins = jnp.min(jnp.where(same, every[None, :], seq_len), axis=1)
        facts = jnp.stack([segments, pad_mask[0], every - begins]).reshape(3, n_mp, rows)
        segs, pads, positions = facts[:, order].reshape(3, seq_len)
        slots = (order[:, None] * rows + jnp.arange(rows, dtype=jnp.int32)[None, :]).reshape(-1)
        kv_cols = w_kv.shape[2]
        half_dim = HEAD_WIDTH // 2
        frequency = ROPE_BASE ** (-jnp.arange(half_dim, dtype=F32) * 2.0 / HEAD_WIDTH)
        angles = positions.astype(F32)[:, None] * frequency[None, :]
        cosine = jnp.cos(angles)
        sine = jnp.sin(angles)
        marks = jnp.stack([segs, slots, pads] + [segs] * 5)
        (
            query_bf, key_bf, value_bf, mixed_bf, attended, hidden_in, gain_rows, group_ffn, w_gate, w_up, w_down,
            wq, wkv, wo, seq_normed,
        ) = open_layer(
            n_dp, n_mp, low_q, low_kv, low_o, w_mlp, code_spacing(bit_sel[2]).reshape(1, 1), cosine, sine,
            marks.T, marks, inputs, norm_gains.reshape(1, -1),
        )
        w_gate, w_up, w_down = w_gate.reshape(D, -1), w_up.reshape(D, -1), w_down.reshape(D, -1)
        live = lax.dynamic_slice_in_dim(pad_mask[0], m * rows, rows).astype(F32)[:, None]
        outputs, grad_gain_three, gate, up, activated, group_grad = turn(
            n_dp, n_mp, group_ffn, w_gate, w_up, w_down, hidden_in, gain_rows, out_grad, live
        )
        tokens = 8 * rows
        grad_down = mm_rows(group_grad.reshape(tokens, D), activated.reshape(tokens, -1))
        grad_down = grad_down.astype(BF).reshape(nj, 2, wrows, -1)
        grad_down, group_grad = lax.optimization_barrier((grad_down, group_grad))
        down_stay, down_came = scatter_first(grad_down, y)
        grad_gate, grad_up, part = mlp_back(group_grad, gate, up, w_gate, w_up, w_down)
        flat_ffn = group_ffn.reshape(tokens, D)
        grad_gate, grad_up, down_came = lax.optimization_barrier((grad_gate, grad_up, down_came))
        down_own, down_shifted = scatter_second(down_stay, down_came, j)
        grads_gate = mm_rows(flat_ffn, grad_gate.reshape(tokens, -1)).astype(BF).reshape(nj, 2, wrows, -1)
        grads_gate, grad_up = lax.optimization_barrier((grads_gate, grad_up))
        grads_up = mm_rows(flat_ffn, grad_up.reshape(tokens, -1)).astype(BF).reshape(nj, 2, wrows, -1)
        grad_hidden, grad_gain_one, grad_gain_two, seq_grad, sum_gate, sum_up, squares = back(
            n_dp, n_mp, part, hidden_in, attended, gain_rows, out_grad, live,
            grads_gate, grads_up
        )
        seq_grad, down_shifted = lax.optimization_barrier((seq_grad, down_shifted))
        sums = [down_own.astype(F32), 0.0]
        for d in range(1, nj):
            sums[d % 2] = sums[d % 2] + down_shifted[d - 1].astype(F32)
        sum_down = jnp.concatenate(
            [jnp.where(zl == 0, sums[0], sums[1]), jnp.where(zl == 0, sums[1], sums[0])], 1
        )
        terms = jnp.concatenate([grad_gain_one, grad_gain_two, grad_gain_three])
        terms = terms.reshape((NORMS - 1) * n_dp * n_mp // NORMS, 1, -1)
        grad_in, sum_q, sum_kv, sum_o, sum_gains, norm = close(
            n_dp, n_mp, seq_grad.reshape(seq_len, D), seq_normed, query_bf, key_bf, value_bf, mixed_bf,
            wo, wq, wkv, cosine, sine, marks.T, marks, inputs, gain_rows, grad_hidden,
            terms, sum_down, squares,
        )
        sums = [sum_gate, sum_up, sum_down, sum_q, sum_o, sum_kv]
        news = adam_all(
            norm, sum_gains, [norm_gains, m_gains, v_gains], sums, [w_mlp, m_mlp, v_mlp, w_qo, m_qo, v_qo, w_kv, m_kv, v_kv]
        )
        grad_norm = norm[0, :1]
        new_gains, new_m_gains, new_v_gains = news[:3]
        new_w_mlp, new_m_mlp, new_v_mlp, new_w_qo, new_m_qo, new_v_qo, new_w_kv, new_m_kv, new_v_kv = news[3:]
        return (
            outputs, grad_in, grad_norm, new_w_qo, new_w_kv, new_w_mlp, new_gains,
            new_m_qo, new_m_kv, new_m_mlp, new_m_gains, new_v_qo, new_v_kv, new_v_mlp, new_v_gains,
        )

    return local


def solution(mesh):
    tokens = P(("dp", "mp"), None)
    weight = P(None, "dp", "mp")
    flat = P(("dp", "mp"))
    per_weight = (weight, weight, weight, flat)
    return jax.shard_map(
        build_local(mesh.shape["dp"], mesh.shape["mp"]),
        mesh=mesh,
        in_specs=(tokens, tokens, P("dp", None), P("dp", None), P()) + per_weight * 3,
        out_specs=(tokens, tokens, P()) + per_weight * 3,
        check_vma=False,
    )
```
